512 devices in a mesh: dp: 32 (over z, x_hi), txt: 16 (over y, x_lo, core).
Axes of the slice: x: 4 (x_hi: 2, x_lo: 2; x = x_hi * 2 + x_lo), y: 4, z: 16, core: 2. Of those that a mesh axis runs over, the one named last changes fastest.
Arguments:
- resid: bfloat16 [8192, 1024], P('dp', 'txt'), may hold values from -40 to 40
- prenorm_gain: float32 [1024], replicated, may hold values from 0.25 to 1.75
- prenorm_bias: float32 [1024], replicated, may hold values from -3 to 3
- up_weight: bfloat16 [1024, 4096], P('dp', 'txt'), may hold values from -0.1875 to 0.1875
- up_bias: float32 [4096], P('txt'), may hold values from -3 to 3
- down_weight: bfloat16 [4096, 1024], P('txt', 'dp'), may hold values from -0.09375 to 0.09375
- down_bias: float32 [1024], replicated, may hold values from -3 to 3
- post_gain: float32 [1024], P('txt'), may hold values from 0.25 to 1.75
- post_bias: float32 [1024], P('txt'), may hold values from -3 to 3
- projection: bfloat16 [1024, 768], P('txt'), may hold values from -1 to 1
- texts: bfloat16 [20480, 768], P('txt'), may hold values from -48 to 48
- labels: int32 [8192], P('dp'), may hold values from 0 to 20479
- step_size: float32 [1], replicated, may hold values from 0.5 to 2
Outputs:
- adversarial: float32 [8192, 1024], P('dp', 'txt')
The draws below stay inside these ranges and needn't reach their ends.
All inputs are finite; a program needn't handle non-finite values.
Results may differ from the reference program's by a relative error of at most 0.0036.
Values may be sent and summed in bfloat16 or wider, within the bound.
No kernel may reach another device: no remote copies, remote signals or barrier semaphores. Data moves between devices by JAX's collectives and lax.ppermute only.
A program may use at most 64 MiB of HBM per device.

```python
import math
import jax
import jax.numpy as jnp
from jax import lax

MODEL_WIDTH = 1024
FF = 4096
E = 768
IMG_DEV = 256
IMAGES = 8192
TEXTS = 20480
N_DP = 32


def shared_directions(key):
    feature_dir = jax.random.normal(jax.random.fold_in(key, 101), (MODEL_WIDTH,), jnp.float32)
    feature_dir = feature_dir / jnp.sqrt(jnp.sum(feature_dir * feature_dir))
    embed_dir = jax.random.normal(jax.random.fold_in(key, 102), (E,), jnp.float32)
    embed_dir = embed_dir / jnp.sqrt(jnp.sum(embed_dir * embed_dir))
    return (feature_dir, embed_dir)


def noise_draw(key, shape):
    return jax.random.normal(key, shape, jnp.float32)


def draw_resid(key, part):
    feature_dir, embed_dir = shared_directions(key)
    noise = noise_draw(jax.random.fold_in(key, 201), (IMAGES, MODEL_WIDTH))
    heavy = jax.random.uniform(jax.random.fold_in(key, 202), (IMAGES,), jnp.float32) < 0.125
    strength = jax.random.uniform(jax.random.fold_in(key, 203), (IMAGES,), jnp.float32, 3.0, 6.0)
    lift = jnp.where(heavy, strength * math.sqrt(MODEL_WIDTH), 0.0)
    rows = noise + lift[:, None] * feature_dir[None, :]
    return jnp.clip(rows, -40.0, 40.0).astype(jnp.bfloat16)


def draw_projection(key, part):
    feature_dir, embed_dir = shared_directions(key)
    base = jax.random.normal(jax.random.fold_in(key, 301), (MODEL_WIDTH, E), jnp.float32) / math.sqrt(MODEL_WIDTH)
    matrix = base + 3.0 * feature_dir[:, None] * embed_dir[None, :]
    return jnp.clip(matrix, -1.0, 1.0).astype(jnp.bfloat16)


def draw_texts(key, part):
    feature_dir, embed_dir = shared_directions(key)
    noise = noise_draw(jax.random.fold_in(key, 401), (TEXTS, E))
    order = jax.random.permutation(jax.random.fold_in(key, 402), TEXTS)
    count = max(2, TEXTS // 64)
    chosen = order[:count]
    strength = jax.random.uniform(jax.random.fold_in(key, 403), (count,), jnp.float32, 3.0, 6.0)
    rows = noise.at[chosen].add(strength[:, None] * math.sqrt(E) * embed_dir[None, :])
    return jnp.clip(rows, -48.0, 48.0).astype(jnp.bfloat16)


def with_ends(values, stream_key, least, high):
    index_at = [jax.random.randint(jax.random.fold_in(stream_key, axis), (), 0, length) for axis, length in enumerate(values.shape)]
    widest = values.shape.index(max(values.shape))
    next_to = index_at[:widest] + [(index_at[widest] + 1) % values.shape[widest]] + index_at[widest + 1:]
    return values.at[tuple(index_at)].set(least).at[tuple(next_to)].set(high)


def block_levels(key, dims, pieces, low, high):
    level, own = 1.0, jax.random.fold_in(key, 6)
    for dim, parts in pieces:
        steps = jnp.exp(jax.random.uniform(jax.random.fold_in(own, dim), (parts,), jnp.float32, low / len(pieces), high / len(pieces)))
        level = level * jnp.repeat(steps, dims[dim] // parts).reshape([-1 if axis == dim else 1 for axis in range(len(dims))])
    return level


def gaussian(rng, dims, deviation, most, pieces=(), held_as=jnp.bfloat16):
    level = block_levels(rng, dims, pieces, -0.22, 0.18) if pieces else 1.0
    values = jax.random.normal(rng, dims, jnp.float32) * deviation * level
    return jnp.minimum(jnp.maximum(values, -most), most).astype(held_as)


def setup_inputs(seed: int = 0) -> dict:
    splits = jax.random.split(jax.random.key(seed), 14)
    return {
        "resid": draw_resid(jax.random.fold_in(splits[13], 71), 0),
        "prenorm_gain": jnp.clip(1.0 + 0.15 * jax.random.normal(splits[1], (MODEL_WIDTH,), jnp.float32), 0.25, 1.75),
        "prenorm_bias": gaussian(splits[2], (MODEL_WIDTH,), 0.5, 3.0, (), jnp.float32),
        "up_weight": gaussian(splits[3], (MODEL_WIDTH, FF), MODEL_WIDTH ** -0.5, 0.1875, ((0, 32), (1, 16))),
        "up_bias": gaussian(splits[4], (FF,), 0.5, 3.0, ((0, 16),), jnp.float32),
        "down_weight": gaussian(splits[5], (FF, MODEL_WIDTH), FF ** -0.5, 0.09375, ((0, 16), (1, 32))),
        "down_bias": gaussian(splits[6], (MODEL_WIDTH,), 0.5, 3.0, (), jnp.float32),
        "post_gain": jnp.clip(1.0 + 0.15 * jax.random.normal(splits[7], (MODEL_WIDTH,), jnp.float32), 0.25, 1.75),
        "post_bias": gaussian(splits[8], (MODEL_WIDTH,), 0.5, 3.0, ((0, 16),), jnp.float32),
        "projection": draw_projection(jax.random.fold_in(splits[13], 71), 0),
        "texts": draw_texts(jax.random.fold_in(splits[13], 71), 0),
        "labels": with_ends(jax.random.randint(splits[11], (IMAGES,), 0, TEXTS), jax.random.fold_in(splits[11], 1), 0, TEXTS - 1).astype(jnp.int32),
        "step_size": jnp.clip(jnp.exp(jax.random.uniform(splits[12], (1,), jnp.float32, math.log(0.5), math.log(2.0))), 0.5, 2.0),
    }


def row_statistics(values):
    mean_val = lax.optimization_barrier(jnp.mean(values, axis=1, keepdims=True))
    var_val = lax.optimization_barrier(jnp.mean(values * values, axis=1, keepdims=True)) - mean_val * mean_val
    rstd_val = lax.rsqrt(var_val + 1e-05)
    return ((values - mean_val) * rstd_val, rstd_val)

def norm_backward_pass(grad_in, gain, normed_val, rstd_val):
    scaled = grad_in * gain
    first = lax.optimization_barrier(jnp.mean(scaled, axis=1, keepdims=True))
    second = lax.optimization_barrier(jnp.mean(scaled * normed_val, axis=1, keepdims=True))
    return (scaled - first - normed_val * second) * rstd_val

def reference(resid, prenorm_gain, prenorm_bias, up_weight, up_bias, down_weight, down_bias, post_gain, post_bias, projection, texts, labels, step_size):
    input_rows = resid.astype(jnp.float32)
    centered_input, input_inverse_deviation = row_statistics(input_rows)
    normed_input = (centered_input * prenorm_gain + prenorm_bias).astype(jnp.bfloat16)
    pre_act = jnp.dot(normed_input, up_weight, preferred_element_type=jnp.float32) + up_bias
    gate_sig = jax.nn.sigmoid(1.702 * pre_act)
    hidden = (pre_act * gate_sig).astype(jnp.bfloat16)
    block_out = input_rows + jnp.dot(hidden, down_weight, preferred_element_type=jnp.float32) + down_bias
    yhat, rstd_out = row_statistics(block_out)
    post_normed = (yhat * post_gain + post_bias).astype(jnp.bfloat16)
    embedding = jnp.dot(post_normed, projection, preferred_element_type=jnp.float32)
    emb_norm = jnp.sqrt(lax.optimization_barrier(jnp.sum(embedding * embedding, axis=1, keepdims=True)) + 1e-06)
    unit_vec = embedding / emb_norm
    unit_low = unit_vec.astype(jnp.bfloat16)
    text_f = texts.astype(jnp.float32)
    text_unit = (text_f / jnp.sqrt(lax.optimization_barrier(jnp.sum(text_f * text_f, axis=1, keepdims=True)) + 1e-06)).astype(jnp.bfloat16)

    def block_grad(pair):
        unit_blk, label_blk = pair
        logits = 100.0 * jnp.dot(unit_blk, text_unit.T, preferred_element_type=jnp.float32)
        top_val = lax.optimization_barrier(jnp.max(logits, axis=1, keepdims=True))
        exponent = jnp.exp(logits - top_val)
        prob = exponent / lax.optimization_barrier(jnp.sum(exponent, axis=1, keepdims=True))
        columns = lax.broadcasted_iota(jnp.int32, logits.shape, 1)
        target = (columns == label_blk[:, None]).astype(jnp.float32)
        score_grad = (100.0 * (prob - target)).astype(jnp.bfloat16)
        return jnp.dot(score_grad, text_unit, preferred_element_type=jnp.float32)
    unit_grad = lax.map(block_grad, (unit_low.reshape(N_DP, IMG_DEV, E), labels.astype(jnp.int32).reshape(N_DP, IMG_DEV)))
    unit_grad = unit_grad.reshape(IMAGES, E)
    along = lax.optimization_barrier(jnp.sum(unit_vec * unit_grad, axis=1, keepdims=True))
    emb_grad = ((unit_grad - unit_vec * along) / emb_norm).astype(jnp.bfloat16)
    post_grad = jnp.dot(emb_grad, projection.T, preferred_element_type=jnp.float32)
    output_gradient = norm_backward_pass(post_grad, post_gain, yhat, rstd_out)
    out_low = output_gradient.astype(jnp.bfloat16)
    hid_grad = jnp.dot(out_low, down_weight.T, preferred_element_type=jnp.float32)
    act_grad = (hid_grad * (gate_sig + 1.702 * pre_act * gate_sig * (1.0 - gate_sig))).astype(jnp.bfloat16)
    normed_gradient = jnp.dot(act_grad, up_weight.T, preferred_element_type=jnp.float32)
    input_gradient = output_gradient + norm_backward_pass(normed_gradient, prenorm_gain, centered_input, input_inverse_deviation)
    grad_rms = jnp.sqrt(lax.optimization_barrier(jnp.mean(input_gradient * input_gradient, axis=1, keepdims=True)) + 1e-06)
    return input_rows + step_size[0] * input_gradient / grad_rms
```

```python
import jax
import jax.numpy as jnp
from jax import lax
from jax.sharding import PartitionSpec as P

WIDTH = 1024
BF = jnp.bfloat16
F32 = jnp.float32


def swapped(x, axis, groups=None):
    return lax.all_to_all(x, axis, 0, 0, tiled=True, axis_index_groups=groups)


def copies(x, n):
    return jnp.broadcast_to(x, (n, *x.shape))


def pieces(x, count):
    out = []
    for _ in range(count):
        part = lax.reduce_precision(x, 8, 7)
        out.append(part.astype(BF))
        x = x - part
    return out


def row_norm(rows):
    mean = jnp.mean(rows, axis=1, keepdims=True)
    var = jnp.mean(rows * rows, axis=1, keepdims=True) - mean * mean
    rstd = lax.rsqrt(var + 1e-05)
    return (rows - mean) * rstd, rstd


def norm_back(scaled, normed, rstd):
    first = jnp.mean(scaled, axis=1, keepdims=True)
    second = jnp.mean(scaled * normed, axis=1, keepdims=True)
    return (scaled - first - normed * second) * rstd


def local(
    resid,
    prenorm_gain,
    prenorm_bias,
    up_weight,
    up_bias,
    down_weight,
    down_bias,
    post_gain,
    post_bias,
    projection,
    texts,
    labels,
    step_size,
):
    n_txt, n_dp = lax.axis_size("txt"), lax.axis_size("dp")
    n_z = n_dp // 2
    me = lax.axis_index("txt")
    images, share = resid.shape
    rows = images // n_txt
    hid = up_weight.shape[1]
    n_text, emb = texts.shape

    proj = lax.all_gather(projection, "txt", axis=0, tiled=True)

    along_z = [[2 * z + x for z in range(n_z)] for x in range(2)]
    mine = jnp.stack([up_weight, down_weight.T])
    mine = swapped(copies(mine, n_z), "dp", along_z)

    text_f = texts.astype(F32)
    text_unit = (text_f / jnp.sqrt(jnp.sum(text_f * text_f, axis=1, keepdims=True) + 1e-06)).astype(BF)
    local_label = labels - me * n_text
    columns = lax.broadcasted_iota(jnp.int32, (images, n_text), 1)
    target = columns == local_label[:, None]
    label_text = jnp.dot(target.astype(BF), text_unit, preferred_element_type=F32).astype(BF)

    label_text = label_text.reshape(n_txt, rows, emb // images, images).transpose(0, 2, 1, 3)
    label_text = label_text.reshape(n_txt, rows * emb // images, images)
    vectors = jnp.stack(pieces(post_gain, 3) + pieces(post_bias, 3))
    vectors = jnp.pad(vectors, ((0, 2), (0, images - share)))
    message = jnp.concatenate(
        [copies(resid.T, n_txt), label_text, copies(vectors, n_txt)], axis=1
    )
    mine, message = lax.optimization_barrier((mine, message))
    pairs = [(i, i ^ 1) for i in range(n_dp)]
    other_up = lax.ppermute(mine[:, 0], "dp", pairs)
    other_down = lax.ppermute(mine[:, 1], "dp", pairs)
    message = swapped(message, "txt")

    state = message[:, :share].reshape(n_txt * share, images)
    label_rows = jnp.sum(message[:, share : share + rows * emb // images].astype(F32), axis=0)
    label_rows = label_rows.reshape(emb // images, rows, images).transpose(1, 0, 2).reshape(rows, emb)
    vectors = message[:, -8:, :share].astype(F32)
    gain_out = (vectors[:, 0] + vectors[:, 1] + vectors[:, 2]).reshape(-1)
    bias_out = (vectors[:, 3] + vectors[:, 4] + vectors[:, 5]).reshape(-1)

    first = lax.rem(lax.axis_index("dp"), 2) == 0

    def whole(own, other):
        both = jnp.stack([jnp.where(first, own, other), jnp.where(first, other, own)], axis=1)
        return both.reshape(WIDTH, hid)

    w_up = whole(mine[:, 0], other_up)
    w_down = whole(mine[:, 1], other_down)

    inputs = state.astype(F32)
    mean_in = jnp.mean(inputs, axis=0)
    var_in = jnp.mean(inputs * inputs, axis=0) - mean_in * mean_in
    rstd_in = lax.rsqrt(var_in + 1e-05)
    normed = ((inputs - mean_in) * rstd_in * prenorm_gain[:, None] + prenorm_bias[:, None]).astype(BF)
    pre_act = jnp.einsum("di,df->if", normed, w_up, preferred_element_type=F32) + up_bias
    gate = jax.nn.sigmoid(1.702 * pre_act)
    hidden = (pre_act * gate).astype(BF)
    mixed = jnp.einsum("if,df->id", hidden, w_down, preferred_element_type=F32).astype(BF)
    mixed = swapped(mixed.reshape(n_txt, rows, WIDTH), "txt")

    pick = lax.broadcasted_iota(jnp.int32, (rows, images), 1) == (
        lax.broadcasted_iota(jnp.int32, (rows, images), 0) + me * rows
    )
    own = jnp.einsum("ri,di->rd", pick.astype(BF), state, preferred_element_type=F32)
    block_out = own + jnp.sum(mixed.astype(F32), axis=0) + down_bias
    yhat, rstd_out = row_norm(block_out)
    post_normed = (yhat * gain_out + bias_out).astype(BF)
    embedding = jnp.dot(post_normed, proj, preferred_element_type=F32)
    emb_norm = jnp.sqrt(jnp.sum(embedding * embedding, axis=1, keepdims=True) + 1e-06)
    unit_vec = embedding / emb_norm
    unit_low = swapped(copies(unit_vec.astype(BF), n_txt), "txt").reshape(images, emb)

    logits = 100.0 * jnp.einsum("ie,je->ij", unit_low, text_unit, preferred_element_type=F32)
    top = lax.reduce_precision(jnp.max(logits, axis=1), 8, 7)
    exponent = jnp.exp(logits - top[:, None])
    others = jnp.where(target, 0.0, exponent)
    rest = jnp.sum(others, axis=1)
    hit = jnp.sum(jnp.where(target, exponent, 0.0), axis=1)
    back = jnp.dot(others.astype(BF), text_unit, preferred_element_type=F32).astype(BF)
    stats = jnp.stack(pieces(top, 1) + pieces(rest, 2) + pieces(hit, 2), axis=1)
    stats = jnp.pad(stats, ((0, 0), (0, 128 - stats.shape[1])))
    back = jnp.concatenate([back, stats], axis=1).reshape(n_txt, rows, emb + 128)
    back = swapped(back, "txt").astype(F32)

    stats = back[:, :, emb:]
    top = stats[:, :, 0]
    weight = jnp.exp(top - jnp.max(top, axis=0))
    rest = jnp.sum(weight * (stats[:, :, 1] + stats[:, :, 2]), axis=0)[:, None]
    hit = jnp.sum(weight * (stats[:, :, 3] + stats[:, :, 4]), axis=0)[:, None]
    unit_grad = jnp.sum(weight[:, :, None] * back[:, :, :emb], axis=0)
    unit_grad = (unit_grad - rest * label_rows) * (100.0 / (rest + hit))
    along = jnp.sum(unit_vec * unit_grad, axis=1, keepdims=True)
    emb_grad = ((unit_grad - unit_vec * along) / emb_norm).astype(BF)
    post_grad = jnp.einsum("ie,de->id", emb_grad, proj, preferred_element_type=F32)
    out_grad = norm_back(post_grad * gain_out, yhat, rstd_out)
    out_low = swapped(copies(out_grad.astype(BF), n_txt), "txt").reshape(images, WIDTH)

    hid_grad = jnp.einsum("id,df->if", out_low, w_down, preferred_element_type=F32)
    act_grad = (hid_grad * (gate + 1.702 * pre_act * gate * (1.0 - gate))).astype(BF)
    normed_grad = jnp.einsum("if,df->id", act_grad, w_up, preferred_element_type=F32).astype(BF)
    normed_grad = swapped(normed_grad.reshape(n_txt, rows, WIDTH), "txt")
    normed_grad = jnp.sum(normed_grad.astype(F32), axis=0)
    xhat, rstd_own = row_norm(own)
    input_grad = out_grad + norm_back(normed_grad * prenorm_gain, xhat, rstd_own)
    rms = jnp.sqrt(jnp.mean(input_grad * input_grad, axis=1, keepdims=True) + 1e-06)
    change = step_size[0] * input_grad / rms
    change = change.reshape(rows, n_txt, share).transpose(1, 0, 2)
    change = swapped(change, "txt").reshape(images, share)
    return resid.astype(F32) + change


def solution(mesh):
    placed = (
        P("dp", "txt"),
        P(),
        P(),
        P("dp", "txt"),
        P("txt"),
        P("txt", "dp"),
        P(),
        P("txt"),
        P("txt"),
        P("txt", None),
        P("txt", None),
        P("dp"),
        P(),
    )
    return jax.shard_map(
        local, mesh=mesh, in_specs=placed, out_specs=P("dp", "txt"), check_vma=False
    )
```

```python
import jax
import jax.numpy as jnp
from jax import lax
from jax.experimental import pallas as pl
from jax.experimental.pallas import tpu as pltpu
from jax.sharding import PartitionSpec as P

WIDTH = 1024
BF = jnp.bfloat16
F32 = jnp.float32


def swapped(x, axis, groups=None):
    return lax.all_to_all(x, axis, 0, 0, tiled=True, axis_index_groups=groups)


def copies(x, n):
    return jnp.broadcast_to(x, (n, *x.shape))


def pieces(x, count):
    out = []
    for _ in range(count):
        part = lax.reduce_precision(x, 8, 7)
        out.append(part.astype(BF))
        x = x - part
    return out


def row_norm(rows):
    mean = jnp.mean(rows, axis=1, keepdims=True)
    var = jnp.mean(rows * rows, axis=1, keepdims=True) - mean * mean
    rstd = lax.rsqrt(var + 1e-05)
    return (rows - mean) * rstd, rstd


def norm_back(scaled, normed, rstd):
    first = jnp.mean(scaled, axis=1, keepdims=True)
    second = jnp.mean(scaled * normed, axis=1, keepdims=True)
    return (scaled - first - normed * second) * rstd


def vmem_call(body, outs, *args):
    return pl.pallas_call(
        body,
        out_shape=[jax.ShapeDtypeStruct(s, d) for s, d in outs],
        in_specs=[pl.BlockSpec(memory_space=pltpu.VMEM)] * len(args),
        out_specs=[pl.BlockSpec(memory_space=pltpu.VMEM)] * len(outs),
        compiler_params=pltpu.CompilerParams(vmem_limit_bytes=32 << 20),
    )(*args)


def embed_kernel(mixed, own, bias, gain_out, bias_out, proj, sent, unit, norm, yhat, rstd):
    n = mixed.shape[0]
    total = own[...] + bias[...]
    for j in range(n):
        total += mixed[j].astype(F32)
    normed, scale = row_norm(total)
    yhat[...] = normed
    rstd[...] = jnp.broadcast_to(scale, rstd.shape)
    post_normed = (normed * gain_out[...] + bias_out[...]).astype(BF)
    embedding = jnp.dot(post_normed, proj[...], preferred_element_type=F32)
    length = jnp.sqrt(jnp.sum(embedding * embedding, axis=1, keepdims=True) + 1e-06)
    norm[...] = jnp.broadcast_to(length, norm.shape)
    vec = embedding / length
    unit[...] = vec
    low = vec.astype(BF)
    for j in range(n):
        sent[j] = low


def embed_back_kernel(back, label_rows, unit, norm, yhat, rstd, gain_out, proj, sent, grad):
    n = back.shape[0]
    emb = unit.shape[1]
    stats = [back[j, :, emb:].astype(F32) for j in range(n)]
    top = stats[0][:, 0:1]
    for j in range(1, n):
        top = jnp.maximum(top, stats[j][:, 0:1])
    rest = jnp.zeros_like(top)
    hit = jnp.zeros_like(top)
    unit_grad = jnp.zeros(unit.shape, F32)
    for j in range(n):
        weight = jnp.exp(stats[j][:, 0:1] - top)
        rest += weight * (stats[j][:, 1:2] + stats[j][:, 2:3])
        hit += weight * (stats[j][:, 3:4] + stats[j][:, 4:5])
        unit_grad += weight * back[j, :, :emb].astype(F32)
    unit_grad = (unit_grad - rest * label_rows[...]) * (100.0 / (rest + hit))
    vec = unit[...]
    along = jnp.sum(vec * unit_grad, axis=1, keepdims=True)
    emb_grad = ((unit_grad - vec * along) / norm[:, 0:1]).astype(BF)
    post_grad = lax.dot_general(
        emb_grad, proj[...], (((1,), (1,)), ((), ())), preferred_element_type=F32
    )
    out_grad = norm_back(post_grad * gain_out[...], yhat[...], rstd[:, 0:1])
    grad[...] = out_grad
    low = out_grad.astype(BF)
    for j in range(n):
        sent[j] = low


def result_kernel(parts, gain, own, out_grad, step, sent):
    n, _, share = sent.shape
    total = parts[0].astype(F32)
    for j in range(1, n):
        total += parts[j].astype(F32)
    xhat, scale = row_norm(own[...])
    grad = out_grad[...] + norm_back(total * gain[...], xhat, scale)
    rms = jnp.sqrt(jnp.mean(grad * grad, axis=1, keepdims=True) + 1e-06)
    change = step[0:1, 0:1] * grad / rms
    for j in range(n):
        sent[j] = change[:, j * share : (j + 1) * share]


def local(
    resid,
    prenorm_gain,
    prenorm_bias,
    up_weight,
    up_bias,
    down_weight,
    down_bias,
    post_gain,
    post_bias,
    projection,
    texts,
    labels,
    step_size,
):
    n_txt, n_dp = lax.axis_size("txt"), lax.axis_size("dp")
    n_z = n_dp // 2
    me = lax.axis_index("txt")
    images, share = resid.shape
    rows = images // n_txt
    hid = up_weight.shape[1]
    n_text, emb = texts.shape

    proj = lax.all_gather(projection, "txt", axis=0, tiled=True)

    along_z = [[2 * z + x for z in range(n_z)] for x in range(2)]
    mine = jnp.stack([up_weight, down_weight.T])
    mine = swapped(copies(mine, n_z), "dp", along_z)

    text_f = texts.astype(F32)
    text_unit = (text_f / jnp.sqrt(jnp.sum(text_f * text_f, axis=1, keepdims=True) + 1e-06)).astype(BF)
    local_label = labels - me * n_text
    columns = lax.broadcasted_iota(jnp.int32, (images, n_text), 1)
    target = columns == local_label[:, None]
    label_text = jnp.dot(target.astype(BF), text_unit, preferred_element_type=F32).astype(BF)

    label_text = label_text.reshape(n_txt, rows, emb // images, images).transpose(0, 2, 1, 3)
    label_text = label_text.reshape(n_txt, rows * emb // images, images)
    vectors = jnp.stack(pieces(post_gain, 3) + pieces(post_bias, 3))
    vectors = jnp.pad(vectors, ((0, 2), (0, images - share)))
    message = jnp.concatenate([label_text, copies(vectors, n_txt)], axis=1)

    def from_partner(x, bits):
        return lax.ppermute(x, "txt", [(i, i ^ bits) for i in range(n_txt)])

    state = resid.T
    state = jnp.stack([state] + [from_partner(state, 4 * k) for k in (1, 2, 3)])
    state = jnp.stack([state, from_partner(state, 2)], axis=1)
    state = jnp.stack([state, from_partner(state, 1)], axis=2)
    state = state.reshape(2, 2, 2, 2, share, images)
    for axis in range(4):
        bit = lax.rem(lax.shift_right_logical(me, 3 - axis), 2) == 1
        state = jnp.where(bit, jnp.flip(state, axis), state)
    state = state.reshape(n_txt * share, images)

    mine, message = lax.optimization_barrier((mine, message))
    pairs = [(i, i ^ 1) for i in range(n_dp)]
    other_up = lax.ppermute(mine[:, 0], "dp", pairs)
    other_down = lax.ppermute(mine[:, 1], "dp", pairs)
    message = swapped(message, "txt")

    label_rows = jnp.sum(message[:, : rows * emb // images].astype(F32), axis=0)
    label_rows = label_rows.reshape(emb // images, rows, images).transpose(1, 0, 2).reshape(rows, emb)
    vectors = message[:, -8:, :share].astype(F32)
    gain_out = (vectors[:, 0] + vectors[:, 1] + vectors[:, 2]).reshape(1, WIDTH)
    bias_out = (vectors[:, 3] + vectors[:, 4] + vectors[:, 5]).reshape(1, WIDTH)

    first = lax.rem(lax.axis_index("dp"), 2) == 0

    def whole(own, other):
        both = jnp.stack([jnp.where(first, own, other), jnp.where(first, other, own)], axis=1)
        return both.reshape(WIDTH, hid)

    w_up = whole(mine[:, 0], other_up)
    w_down = whole(mine[:, 1], other_down)

    inputs = state.astype(F32)
    mean_in = jnp.mean(inputs, axis=0)
    var_in = jnp.mean(inputs * inputs, axis=0) - mean_in * mean_in
    rstd_in = lax.rsqrt(var_in + 1e-05)
    normed = ((inputs - mean_in) * rstd_in * prenorm_gain[:, None] + prenorm_bias[:, None]).astype(BF)
    pre_act = jnp.einsum("di,df->if", normed, w_up, preferred_element_type=F32) + up_bias
    gate = jax.nn.sigmoid(1.702 * pre_act)
    hidden = (pre_act * gate).astype(BF)
    mixed = jnp.einsum("if,df->id", hidden, w_down, preferred_element_type=F32).astype(BF)
    mixed = swapped(mixed.reshape(n_txt, rows, WIDTH), "txt")

    pick = lax.broadcasted_iota(jnp.int32, (rows, images), 1) == (
        lax.broadcasted_iota(jnp.int32, (rows, images), 0) + me * rows
    )
    own = jnp.einsum("ri,di->rd", pick.astype(BF), state, preferred_element_type=F32)
    sent, unit_vec, emb_norm, yhat, rstd_out = vmem_call(
        embed_kernel,
        (
            ((n_txt, rows, emb), BF),
            ((rows, emb), F32),
            ((rows, 128), F32),
            ((rows, WIDTH), F32),
            ((rows, 128), F32),
        ),
        mixed,
        own,
        down_bias[None],
        gain_out,
        bias_out,
        proj,
    )
    unit_low = swapped(sent, "txt").reshape(images, emb)

    logits = 100.0 * jnp.einsum("ie,je->ij", unit_low, text_unit, preferred_element_type=F32)
    top = lax.reduce_precision(jnp.max(logits, axis=1), 8, 7)
    exponent = jnp.exp(logits - top[:, None])
    others = jnp.where(target, 0.0, exponent)
    rest = jnp.sum(others, axis=1)
    hit = jnp.sum(jnp.where(target, exponent, 0.0), axis=1)
    back = jnp.dot(others.astype(BF), text_unit, preferred_element_type=F32).astype(BF)
    stats = jnp.stack(pieces(top, 1) + pieces(rest, 2) + pieces(hit, 2), axis=1)
    stats = jnp.pad(stats, ((0, 0), (0, 128 - stats.shape[1])))
    back = jnp.concatenate([back, stats], axis=1).reshape(n_txt, rows, emb + 128)
    back = swapped(back, "txt")

    sent, out_grad = vmem_call(
        embed_back_kernel,
        (((n_txt, rows, WIDTH), BF), ((rows, WIDTH), F32)),
        back,
        label_rows,
        unit_vec,
        emb_norm,
        yhat,
        rstd_out,
        gain_out,
        proj,
    )
    out_low = swapped(sent, "txt").reshape(images, WIDTH)

    hid_grad = jnp.einsum("id,df->if", out_low, w_down, preferred_element_type=F32)
    act_grad = (hid_grad * (gate + 1.702 * pre_act * gate * (1.0 - gate))).astype(BF)
    normed_grad = jnp.einsum("if,df->id", act_grad, w_up, preferred_element_type=F32).astype(BF)
    normed_grad = swapped(normed_grad.reshape(n_txt, rows, WIDTH), "txt")
    (change,) = vmem_call(
        result_kernel,
        (((n_txt, rows, share), F32),),
        normed_grad,
        prenorm_gain[None],
        own,
        out_grad,
        step_size[None],
    )
    change = swapped(change, "txt").reshape(images, share)
    return resid.astype(F32) + change


def solution(mesh):
    placed = (
        P("dp", "txt"),
        P(),
        P(),
        P("dp", "txt"),
        P("txt"),
        P("txt", "dp"),
        P(),
        P("txt"),
        P("txt"),
        P("txt", None),
        P("txt", None),
        P("dp"),
        P(),
    )
    return jax.shard_map(
        local, mesh=mesh, in_specs=placed, out_specs=P("dp", "txt"), check_vma=False
    )
```

```python
import jax
import jax.numpy as jnp
from jax import lax
from jax.experimental import pallas as pl
from jax.experimental.pallas import tpu as pltpu
from jax.sharding import PartitionSpec as P

WIDTH = 1024
BF = jnp.bfloat16
F32 = jnp.float32
NT = (((1,), (1,)), ((), ()))
SMALL = pl.CostEstimate(flops=1024, bytes_accessed=1024, transcendentals=0)


def swapped(x, axis, groups=None):
    return lax.all_to_all(x, axis, 0, 0, tiled=True, axis_index_groups=groups)


def copies(x, n):
    return jnp.broadcast_to(x, (n, *x.shape))


def from_partner(x, axis, bits):
    pairs = [(i, i ^ bits) for i in range(lax.axis_size(axis))]
    return lax.ppermute(x, axis, pairs)


def pieces(x, count):
    out = []
    for _ in range(count):
        part = lax.reduce_precision(x, 8, 7)
        out.append(part.astype(BF))
        x = x - part
    return out


def row_norm(rows):
    mean = jnp.mean(rows, axis=1, keepdims=True)
    var = jnp.mean(rows * rows, axis=1, keepdims=True) - mean * mean
    rstd = lax.rsqrt(var + 1e-05)
    return (rows - mean) * rstd, rstd


def norm_back(scaled, normed, rstd):
    first = jnp.mean(scaled, axis=1, keepdims=True)
    second = jnp.mean(scaled * normed, axis=1, keepdims=True)
    return (scaled - first - normed * second) * rstd


def vmem_call(body, outs, *args, scalars=0, cost=None):
    smem = pl.BlockSpec(memory_space=pltpu.SMEM)
    vmem = pl.BlockSpec(memory_space=pltpu.VMEM)
    return pl.pallas_call(
        body,
        out_shape=[jax.ShapeDtypeStruct(s, d) for s, d in outs],
        in_specs=[smem] * scalars + [vmem] * (len(args) - scalars),
        out_specs=[vmem] * len(outs),
        compiler_params=pltpu.CompilerParams(vmem_limit_bytes=32 << 20),
        cost_estimate=cost,
    )(*args)


def text_kernel(near, far, label, unit, label_text):
    n_text = near.shape[0]
    half = label_text.shape[0]
    step = n_text // 5
    total = jnp.zeros(label_text.shape, F32)
    for side, texts in enumerate((near, far)):
        for k in range(5):
            block = texts[k * step : (k + 1) * step, :].astype(F32)
            squares = jnp.sum(block * block, axis=1, keepdims=True)
            low = (block / jnp.sqrt(squares + 1e-06)).astype(BF)
            start = side * n_text + k * step
            unit[start : start + step, :] = low
            columns = lax.broadcasted_iota(jnp.int32, (half, step), 1) + start
            pick = jnp.where(columns == label[...], 1.0, 0.0).astype(BF)
            total += jnp.dot(pick, low, preferred_element_type=F32)
    label_text[...] = total.astype(BF)


def order_kernel(me, near, far, proj, state, vectors):
    emb = proj.shape[1]
    share = near.shape[1]
    half = state.shape[1]
    at = me[0]
    first = lax.rem(at, 2) == 0
    for c, side in enumerate((near, far)):
        for k in range(side.shape[0]):
            x, y = k // 4, k % 4
            there = pl.multiple_of((at ^ (4 * y + 2 * x + c)) * share, share)
            block = side[k]
            proj[pl.ds(there, share), :] = block[:, :emb]
            left = block[:, emb : emb + half]
            right = block[:, emb + half : emb + 2 * half]
            state[pl.ds(there, share), :] = jnp.where(first, left, right)
            vectors[pl.ds(there, share), :] = block[:, emb + 2 * half :]


def rows_kernel(me, state, vectors, own, lines):
    rows, half = own.shape[0], state.shape[1]
    start = (me[0] // 2) * rows
    at = lax.broadcasted_iota(jnp.int32, (rows, half), 1)
    line = lax.broadcasted_iota(jnp.int32, (rows, half), 0)
    own[...] = lax.dot_general(
        (at == line + start).astype(F32).astype(BF), state[...], NT, preferred_element_type=F32
    )
    at = lax.broadcasted_iota(jnp.int32, (16, half), 1)
    line = lax.broadcasted_iota(jnp.int32, (16, half), 0)
    pick = (at >= 3 * line) & (at < 3 * line + 3) & (line < 2)
    lines[...] = lax.dot_general(
        pick.astype(F32).astype(BF), vectors[...], NT, preferred_element_type=F32
    )


def embed_kernel(mixed, own, bias, lines, proj, sent, unit, norm, yhat, rstd):
    n = mixed.shape[0]
    total = own[...] + bias[...]
    for j in range(n):
        total += mixed[j].astype(F32)
    normed, scale = row_norm(total)
    yhat[...] = normed
    rstd[...] = jnp.broadcast_to(scale, rstd.shape)
    post_normed = (normed * lines[0:1, :] + lines[1:2, :]).astype(BF)
    embedding = jnp.dot(post_normed, proj[...], preferred_element_type=F32)
    length = jnp.sqrt(jnp.sum(embedding * embedding, axis=1, keepdims=True) + 1e-06)
    norm[...] = jnp.broadcast_to(length, norm.shape)
    vec = embedding / length
    unit[...] = vec
    low = vec.astype(BF)
    for j in range(n):
        sent[j] = low


def embed_back_kernel(back, label_parts, unit, norm, yhat, rstd, lines, proj, sent, grad):
    n = back.shape[0]
    emb = unit.shape[1]
    stats = [back[j, :, emb:].astype(F32) for j in range(n)]
    top = stats[0][:, 0:1]
    label_rows = label_parts[0].astype(F32)
    for j in range(1, n):
        top = jnp.maximum(top, stats[j][:, 0:1])
        label_rows += label_parts[j].astype(F32)
    rest = jnp.zeros_like(top)
    hit = jnp.zeros_like(top)
    unit_grad = jnp.zeros(unit.shape, F32)
    for j in range(n):
        weight = jnp.exp(stats[j][:, 0:1] - top)
        rest += weight * (stats[j][:, 1:2] + stats[j][:, 2:3])
        hit += weight * (stats[j][:, 3:4] + stats[j][:, 4:5])
        unit_grad += weight * back[j, :, :emb].astype(F32)
    unit_grad = (unit_grad - rest * label_rows) * (100.0 / (rest + hit))
    vec = unit[...]
    along = jnp.sum(vec * unit_grad, axis=1, keepdims=True)
    emb_grad = ((unit_grad - vec * along) / norm[:, 0:1]).astype(BF)
    post_grad = lax.dot_general(emb_grad, proj[...], NT, preferred_element_type=F32)
    out_grad = norm_back(post_grad * lines[0:1, :], yhat[...], rstd[:, 0:1])
    grad[...] = out_grad
    low = out_grad.astype(BF)
    for j in range(n):
        sent[j] = low


def change_kernel(parts, gain, own, out_grad, step, sent):
    n, half, _ = sent.shape
    share = own.shape[1] // n
    total = parts[0].astype(F32)
    for j in range(1, parts.shape[0]):
        total += parts[j].astype(F32)
    xhat, scale = row_norm(own[...])
    grad = out_grad[...] + norm_back(total * gain[...], xhat, scale)
    rms = jnp.sqrt(jnp.mean(grad * grad, axis=1, keepdims=True) + 1e-06)
    change = step[0:1, 0:1] * grad / rms
    for j in range(n):
        block = change[:, j * share : (j + 1) * share]
        sent[j, :, :share] = block[:half]
        sent[j, :, share:] = block[half:]


def result_kernel(parts, resid, out):
    n, _, width = parts.shape
    share = width // 2
    blocks = []
    for c in range(2):
        for g in range(n // 2):
            block = parts[2 * g + c]
            blocks += [block[:, :share], block[:, share:]]
    change = jnp.concatenate(blocks, axis=0)
    out[...] = resid[...].astype(F32) + change.T


def local(
    resid,
    prenorm_gain,
    prenorm_bias,
    up_weight,
    up_bias,
    down_weight,
    down_bias,
    post_gain,
    post_bias,
    projection,
    texts,
    labels,
    step_size,
):
    n_txt, n_dp = lax.axis_size("txt"), lax.axis_size("dp")
    n_z, n_pair = n_dp // 2, n_txt // 2
    me = lax.axis_index("txt")
    core = lax.rem(me, 2)
    images, share = resid.shape
    half = images // 2
    rows = images // n_txt
    hid = up_weight.shape[1]
    n_text, emb = texts.shape
    cores = [[2 * i + c for i in range(n_pair)] for c in range(2)]
    along_z = [[2 * z + x for z in range(n_z)] for x in range(2)]

    mine = jnp.stack([up_weight, down_weight.T])
    mine = swapped(copies(mine, n_z), "dp", along_z)

    vectors = jnp.stack(pieces(post_gain, 3) + pieces(post_bias, 3), axis=1)
    vectors = jnp.pad(vectors, ((0, 0), (0, 128 - vectors.shape[1])))
    chain = jnp.concatenate([projection, resid.T, vectors], axis=1)
    far_texts = from_partner(texts, "txt", 1)
    far_bias = from_partner(up_bias, "txt", 1)
    chain = jnp.stack([chain] + [from_partner(chain, "txt", 4 * k) for k in (1, 2, 3)])
    chain = jnp.concatenate([chain, from_partner(chain, "txt", 2)])
    far_chain = from_partner(chain, "txt", 1)
    here = me.astype(jnp.int32).reshape(1)
    proj, state, vectors = vmem_call(
        order_kernel,
        (((WIDTH, emb), BF), ((WIDTH, half), BF), ((WIDTH, 128), BF)),
        here,
        chain,
        far_chain,
        scalars=1,
        cost=SMALL,
    )
    own, lines = vmem_call(
        rows_kernel,
        (((rows, WIDTH), F32), ((16, WIDTH), F32)),
        here,
        state,
        vectors,
        scalars=1,
    )

    label = lax.dynamic_slice_in_dim(labels, core * half, half) - (me - core) * n_text
    inside = (label >= 0) & (label < 2 * n_text)
    label = jnp.where(core == 0, label, jnp.where(label < n_text, label + n_text, label - n_text))
    label = jnp.where(inside, label, -1)
    text_unit, label_text = vmem_call(
        text_kernel,
        (((2 * n_text, emb), BF), ((half, emb), BF)),
        texts,
        far_texts,
        label[:, None],
        cost=SMALL,
    )
    target = lax.broadcasted_iota(jnp.int32, (half, 2 * n_text), 1) == label[:, None]
    mine, label_text = lax.optimization_barrier((mine, label_text))
    other_up = from_partner(mine[:, 0], "dp", 1)
    other_down = from_partner(mine[:, 1], "dp", 1)
    label_text = swapped(label_text.reshape(n_pair, rows, emb), "txt", cores)
    first = lax.rem(lax.axis_index("dp"), 2) == 0

    def whole(own, other):
        both = jnp.stack([jnp.where(first, own, other), jnp.where(first, other, own)], axis=1)
        return both.reshape(WIDTH, hid)

    w_up = whole(mine[:, 0], other_up)
    w_down = whole(mine[:, 1], other_down)
    w_up = (w_up, from_partner(w_up, "txt", 1))
    w_down = (w_down, from_partner(w_down, "txt", 1))

    inputs = state.astype(F32)
    mean_in = jnp.mean(inputs, axis=0)
    var_in = jnp.mean(inputs * inputs, axis=0) - mean_in * mean_in
    rstd_in = lax.rsqrt(var_in + 1e-05)
    normed = ((inputs - mean_in) * rstd_in * prenorm_gain[:, None] + prenorm_bias[:, None]).astype(BF)
    pre_act = [
        jnp.einsum("di,df->if", normed, w, preferred_element_type=F32) + b
        for w, b in zip(w_up, (up_bias, far_bias))
    ]
    gate = [jax.nn.sigmoid(1.702 * p) for p in pre_act]
    hidden = [(p * g).astype(BF) for p, g in zip(pre_act, gate)]
    mixed = sum(
        jnp.einsum("if,df->id", h, w, preferred_element_type=F32) for h, w in zip(hidden, w_down)
    )
    mixed = mixed.astype(BF).reshape(n_pair, rows, WIDTH)
    mixed, label_text = lax.optimization_barrier((mixed, label_text))
    mixed = swapped(mixed, "txt", cores)

    sent, unit_vec, emb_norm, yhat, rstd_out = vmem_call(
        embed_kernel,
        (
            ((n_pair, rows, emb), BF),
            ((rows, emb), F32),
            ((rows, 128), F32),
            ((rows, WIDTH), F32),
            ((rows, 128), F32),
        ),
        mixed,
        own,
        down_bias[None],
        lines,
        proj,
    )
    unit_low = swapped(sent, "txt", cores).reshape(half, emb)

    logits = 100.0 * jnp.einsum("ie,je->ij", unit_low, text_unit, preferred_element_type=F32)
    top = lax.reduce_precision(jnp.max(logits, axis=1), 8, 7)
    exponent = jnp.exp(logits - top[:, None])
    others = jnp.where(target, 0.0, exponent)
    rest = jnp.sum(others, axis=1)
    hit = jnp.sum(jnp.where(target, exponent, 0.0), axis=1)
    back = jnp.dot(others.astype(BF), text_unit, preferred_element_type=F32).astype(BF)
    stats = jnp.stack(pieces(top, 1) + pieces(rest, 2) + pieces(hit, 2), axis=1)
    stats = jnp.pad(stats, ((0, 0), (0, 128 - stats.shape[1])))
    back = jnp.concatenate([back, stats], axis=1).reshape(n_pair, rows, emb + 128)
    back = swapped(back, "txt", cores)

    sent, out_grad = vmem_call(
        embed_back_kernel,
        (((n_pair, rows, WIDTH), BF), ((rows, WIDTH), F32)),
        back,
        label_text,
        unit_vec,
        emb_norm,
        yhat,
        rstd_out,
        lines,
        proj,
    )
    out_low = swapped(sent, "txt", cores).reshape(half, WIDTH)

    normed_grad = 0.0
    for p, g, up, down in zip(pre_act, gate, w_up, w_down):
        hid_grad = jnp.einsum("id,df->if", out_low, down, preferred_element_type=F32)
        act_grad = (hid_grad * (g + 1.702 * p * g * (1.0 - g))).astype(BF)
        normed_grad += jnp.einsum("if,df->id", act_grad, up, preferred_element_type=F32)
    normed_grad = swapped(normed_grad.astype(BF).reshape(n_pair, rows, WIDTH), "txt", cores)
    (change,) = vmem_call(
        change_kernel,
        (((n_txt, rows // 2, 2 * share), F32),),
        normed_grad,
        prenorm_gain[None],
        own,
        out_grad,
        step_size[None],
    )
    change = swapped(change, "txt")
    (out,) = vmem_call(result_kernel, (((share, images), F32),), change, resid.T)
    return out.T


def solution(mesh):
    placed = (
        P("dp", "txt"),
        P(),
        P(),
        P("dp", "txt"),
        P("txt"),
        P("txt", "dp"),
        P(),
        P("txt"),
        P("txt"),
        P("txt", None),
        P("txt", None),
        P("dp"),
        P(),
    )
    return jax.shard_map(
        local, mesh=mesh, in_specs=placed, out_specs=P("dp", "txt"), check_vma=False
    )
```

```python
import jax
import jax.numpy as jnp
from jax import lax
from jax.experimental import pallas as pl
from jax.experimental.pallas import tpu as pltpu
from jax.sharding import PartitionSpec as P

WIDTH = 1024
BF = jnp.bfloat16
F32 = jnp.float32
NT = (((1,), (1,)), ((), ()))
SMALL = pl.CostEstimate(flops=1024, bytes_accessed=1024, transcendentals=0)


def swapped(x, axis, groups=None):
    return lax.all_to_all(x, axis, 0, 0, tiled=True, axis_index_groups=groups)


def copies(x, n):
    return jnp.broadcast_to(x, (n, *x.shape))


def from_partner(x, axis, bits):
    pairs = [(i, i ^ bits) for i in range(lax.axis_size(axis))]
    return lax.ppermute(x, axis, pairs)


def pieces(x, count):
    out = []
    for _ in range(count):
        part = lax.reduce_precision(x, 8, 7)
        out.append(part.astype(BF))
        x = x - part
    return out


def row_norm(rows):
    mean = jnp.mean(rows, axis=1, keepdims=True)
    var = jnp.mean(rows * rows, axis=1, keepdims=True) - mean * mean
    rstd = lax.rsqrt(var + 1e-05)
    return (rows - mean) * rstd, rstd


def norm_back(scaled, normed, rstd):
    first = jnp.mean(scaled, axis=1, keepdims=True)
    second = jnp.mean(scaled * normed, axis=1, keepdims=True)
    return (scaled - first - normed * second) * rstd


def vmem_call(body, outs, *args, scalars=0, cost=None, scratch=()):
    smem = pl.BlockSpec(memory_space=pltpu.SMEM)
    vmem = pl.BlockSpec(memory_space=pltpu.VMEM)
    return pl.pallas_call(
        body,
        out_shape=[jax.ShapeDtypeStruct(s, d) for s, d in outs],
        in_specs=[smem] * scalars + [vmem] * (len(args) - scalars),
        out_specs=[vmem] * len(outs),
        compiler_params=pltpu.CompilerParams(vmem_limit_bytes=32 << 20),
        cost_estimate=cost,
        scratch_shapes=[pltpu.VMEM(*spec) for spec in scratch],
    )(*args)


def text_kernel(near, far, label, unit, label_text):
    n_text = near.shape[0]
    half = label_text.shape[0]
    step = n_text // 5
    total = jnp.zeros(label_text.shape, F32)
    for side, texts in enumerate((near, far)):
        for k in range(5):
            block = texts[k * step : (k + 1) * step, :].astype(F32)
            squares = jnp.sum(block * block, axis=1, keepdims=True)
            low = (block / jnp.sqrt(squares + 1e-06)).astype(BF)
            start = side * n_text + k * step
            unit[start : start + step, :] = low
            columns = lax.broadcasted_iota(jnp.int32, (half, step), 1) + start
            pick = jnp.where(columns == label[...], 1.0, 0.0).astype(BF)
            total += jnp.dot(pick, low, preferred_element_type=F32)
    label_text[...] = total.astype(BF)


def stack_kernel(*refs):
    out = refs[-1]
    for k, part in enumerate(refs[:-1]):
        out[k] = part[...]


def order_kernel(me, *refs):
    sides, (proj, state, vectors, far_bias) = refs[:4], refs[4:]
    emb = proj.shape[1]
    share = sides[0].shape[1]
    half = state.shape[1]
    at = me[0]
    first = lax.rem(at, 2) == 0
    for side, bits in zip(sides, (0, 2, 1, 3)):
        for y in range(side.shape[0]):
            owner = at ^ (4 * y + bits)
            there = pl.multiple_of(owner * share, share)
            proj[pl.ds(there, share), :] = side[y, :, :emb]
            left = side[y, :, emb : emb + half]
            right = side[y, :, emb + half : emb + 2 * half]
            state[pl.ds(there, share), :] = jnp.where(first, left, right)
            vectors[owner] = side[y, :8, emb + 2 * half :].astype(F32)
    parts = sides[2][0, 8:16, emb + 2 * half :].astype(F32)
    for k in range(2):
        far_bias[:, 128 * k : 128 * k + 128] = (
            parts[k : k + 1] + parts[k + 2 : k + 3] + parts[k + 4 : k + 5]
        )


def rows_kernel(me, state, vectors, gain, bias, own, lines, normed):
    rows, half = own.shape[0], state.shape[1]
    share = state.shape[0] // vectors.shape[0]
    start = (me[0] // 2) * rows
    at = lax.broadcasted_iota(jnp.int32, (rows, half), 1)
    line = lax.broadcasted_iota(jnp.int32, (rows, half), 0)
    pick = jnp.where(at == line + start, 1.0, 0.0).astype(BF)
    own[...] = lax.dot_general(pick, state[...], NT, preferred_element_type=F32)
    for first in range(2):
        line = [
            vectors[t, 3 * first : 3 * first + 1, :share]
            + vectors[t, 3 * first + 1 : 3 * first + 2, :share]
            + vectors[t, 3 * first + 2 : 3 * first + 3, :share]
            for t in range(vectors.shape[0])
        ]
        lines[first : first + 1, :] = jnp.concatenate(line, axis=1)
    xhat, _ = row_norm(state[...].astype(F32).T)
    normed[...] = (xhat * gain[...] + bias[...]).astype(BF)


def mlp_kernel(side, own, other, far_own, far_other, normed, bias, far_bias, *outs):
    w_up, w_down, pre_act, mixed = outs
    depth = own.shape[2]
    for k, (mine, theirs) in enumerate(((own, other), (far_own, far_other))):
        for z in range(own.shape[0]):
            here = pl.multiple_of(2 * depth * z + depth * side[0], depth)
            there = pl.multiple_of(2 * depth * z + depth * (1 - side[0]), depth)
            w_up[k, pl.ds(here, depth), :] = mine[z, 0]
            w_down[k, pl.ds(here, depth), :] = mine[z, 1]
            w_up[k, pl.ds(there, depth), :] = theirs[z, 0]
            w_down[k, pl.ds(there, depth), :] = theirs[z, 1]
    total = jnp.zeros(mixed.shape, F32)
    for k, add in enumerate((bias, far_bias)):
        pre = jnp.dot(normed[...], w_up[k], preferred_element_type=F32) + add[...]
        pre_act[k] = pre
        hidden = (pre * jax.nn.sigmoid(1.702 * pre)).astype(BF)
        total += lax.dot_general(hidden, w_down[k], NT, preferred_element_type=F32)
    mixed[...] = total.astype(BF)


def mlp_back_kernel(out_low, pre_act, w_up, w_down, normed_grad):
    total = jnp.zeros(normed_grad.shape, F32)
    for k in range(2):
        hid_grad = jnp.dot(out_low[...], w_down[k], preferred_element_type=F32)
        pre = pre_act[k]
        gate = jax.nn.sigmoid(1.702 * pre)
        act_grad = (hid_grad * (gate + 1.702 * pre * gate * (1.0 - gate))).astype(BF)
        total += lax.dot_general(act_grad, w_up[k], NT, preferred_element_type=F32)
    normed_grad[...] = total.astype(BF)


def softmax_kernel(unit_low, text_unit, label, back, logits):
    half, emb = unit_low.shape
    n_block = 5
    step = text_unit.shape[0] // n_block
    top = None
    for k in range(n_block):
        texts = text_unit[k * step : (k + 1) * step, :]
        block = 100.0 * lax.dot_general(unit_low[...], texts, NT, preferred_element_type=F32)
        logits[:, k * step : (k + 1) * step] = block
        block = jnp.max(block, axis=1, keepdims=True)
        top = block if top is None else jnp.maximum(top, block)
    top = top.astype(BF).astype(F32)
    rest = jnp.zeros_like(top)
    hit = jnp.zeros_like(top)
    total = jnp.zeros((half, emb), F32)
    for k in range(n_block):
        block = jnp.exp(logits[:, k * step : (k + 1) * step] - top)
        columns = lax.broadcasted_iota(jnp.int32, (half, step), 1) + k * step
        target = columns == label[...]
        others = jnp.where(target, 0.0, block)
        rest += jnp.sum(others, axis=1, keepdims=True)
        hit += jnp.sum(jnp.where(target, block, 0.0), axis=1, keepdims=True)
        total += jnp.dot(
            others.astype(BF), text_unit[k * step : (k + 1) * step, :], preferred_element_type=F32
        )
    back[:, :emb] = total.astype(BF)
    lane = lax.broadcasted_iota(jnp.int32, (half, 128), 1)
    rest_high = rest.astype(BF).astype(F32)
    hit_high = hit.astype(BF).astype(F32)
    stats = jnp.zeros((half, 128), F32)
    for k, value in enumerate((top, rest_high, rest - rest_high, hit_high, hit - hit_high)):
        stats = jnp.where(lane == k, value, stats)
    back[:, emb:] = stats.astype(BF)


def embed_kernel(mixed, own, bias, lines, proj, sent, unit, norm, yhat, rstd):
    n = mixed.shape[0]
    total = own[...] + bias[...]
    for j in range(n):
        total += mixed[j].astype(F32)
    normed, scale = row_norm(total)
    yhat[...] = normed
    rstd[...] = jnp.broadcast_to(scale, rstd.shape)
    post_normed = (normed * lines[0:1, :] + lines[1:2, :]).astype(BF)
    embedding = jnp.dot(post_normed, proj[...], preferred_element_type=F32)
    length = jnp.sqrt(jnp.sum(embedding * embedding, axis=1, keepdims=True) + 1e-06)
    norm[...] = jnp.broadcast_to(length, norm.shape)
    vec = embedding / length
    unit[...] = vec
    low = vec.astype(BF)
    for j in range(n):
        sent[j] = low


def embed_back_kernel(back, label_parts, unit, norm, yhat, rstd, lines, proj, sent, grad):
    n = back.shape[0]
    emb = unit.shape[1]
    stats = [back[j, :, emb:].astype(F32) for j in range(n)]
    top = stats[0][:, 0:1]
    label_rows = label_parts[0].astype(F32)
    for j in range(1, n):
        top = jnp.maximum(top, stats[j][:, 0:1])
        label_rows += label_parts[j].astype(F32)
    rest = jnp.zeros_like(top)
    hit = jnp.zeros_like(top)
    unit_grad = jnp.zeros(unit.shape, F32)
    for j in range(n):
        weight = jnp.exp(stats[j][:, 0:1] - top)
        rest += weight * (stats[j][:, 1:2] + stats[j][:, 2:3])
        hit += weight * (stats[j][:, 3:4] + stats[j][:, 4:5])
        unit_grad += weight * back[j, :, :emb].astype(F32)
    unit_grad = (unit_grad - rest * label_rows) * (100.0 / (rest + hit))
    vec = unit[...]
    along = jnp.sum(vec * unit_grad, axis=1, keepdims=True)
    emb_grad = ((unit_grad - vec * along) / norm[:, 0:1]).astype(BF)
    post_grad = lax.dot_general(emb_grad, proj[...], NT, preferred_element_type=F32)
    out_grad = norm_back(post_grad * lines[0:1, :], yhat[...], rstd[:, 0:1])
    grad[...] = out_grad
    low = out_grad.astype(BF)
    for j in range(n):
        sent[j] = low


def change_kernel(parts, gain, own, out_grad, step, sent):
    n, half, _ = sent.shape
    share = own.shape[1] // n
    total = parts[0].astype(F32)
    for j in range(1, parts.shape[0]):
        total += parts[j].astype(F32)
    xhat, scale = row_norm(own[...])
    grad = out_grad[...] + norm_back(total * gain[...], xhat, scale)
    rms = jnp.sqrt(jnp.mean(grad * grad, axis=1, keepdims=True) + 1e-06)
    change = step[0:1, 0:1] * grad / rms
    for j in range(n):
        block = change[:, j * share : (j + 1) * share]
        sent[j, :, :share] = block[:half]
        sent[j, :, share:] = block[half:]


def result_kernel(parts, resid, out):
    n, _, width = parts.shape
    share = width // 2
    blocks = []
    for c in range(2):
        for g in range(n // 2):
            block = parts[2 * g + c]
            blocks += [block[:, :share], block[:, share:]]
    change = jnp.concatenate(blocks, axis=0)
    out[...] = resid[...].astype(F32) + change.T


def local(
    resid,
    prenorm_gain,
    prenorm_bias,
    up_weight,
    up_bias,
    down_weight,
    down_bias,
    post_gain,
    post_bias,
    projection,
    texts,
    labels,
    step_size,
):
    n_txt, n_dp = lax.axis_size("txt"), lax.axis_size("dp")
    n_z, n_pair = n_dp // 2, n_txt // 2
    me = lax.axis_index("txt")
    core = lax.rem(me, 2)
    images, share = resid.shape
    half = images // 2
    rows = images // n_txt
    hid = up_weight.shape[1]
    n_text, emb = texts.shape
    cores = [[2 * i + c for i in range(n_pair)] for c in range(2)]
    along_z = [[2 * z + x for z in range(n_z)] for x in range(2)]

    mine = jnp.stack([up_weight, down_weight.T])
    mine = swapped(copies(mine, n_z), "dp", along_z)

    vectors = jnp.stack(pieces(post_gain, 3) + pieces(post_bias, 3))
    vectors = jnp.pad(vectors, ((0, 2), (0, 128 - share)))
    bias_parts = jnp.stack(pieces(up_bias, 3)).reshape(3 * hid // 128, 128)
    vectors = jnp.concatenate([vectors, bias_parts])
    vectors = jnp.pad(vectors, ((0, share - vectors.shape[0]), (0, 0)))
    chain = jnp.concatenate([projection, resid.T, vectors], axis=1)
    far_texts = from_partner(texts, "txt", 1)
    chain = [chain] + [from_partner(chain, "txt", 4 * k) for k in (1, 2, 3)]
    (chain,) = vmem_call(
        stack_kernel, (((len(chain), *chain[0].shape), BF),), *chain, cost=SMALL
    )
    chain_x = from_partner(chain, "txt", 2)
    far_chain = from_partner(chain, "txt", 1)
    far_chain_x = from_partner(chain_x, "txt", 1)
    here = me.astype(jnp.int32).reshape(1)
    proj, state, vectors, far_bias = vmem_call(
        order_kernel,
        (
            ((WIDTH, emb), BF),
            ((WIDTH, half), BF),
            ((n_txt, 8, 128), F32),
            ((1, hid), F32),
        ),
        here,
        chain,
        chain_x,
        far_chain,
        far_chain_x,
        scalars=1,
        cost=SMALL,
    )
    own, lines, normed = vmem_call(
        rows_kernel,
        (((rows, WIDTH), F32), ((8, WIDTH), F32), ((half, WIDTH), BF)),
        here,
        state,
        vectors,
        prenorm_gain[None],
        prenorm_bias[None],
        scalars=1,
        cost=SMALL,
    )

    label = lax.dynamic_slice_in_dim(labels, core * half, half) - (me - core) * n_text
    inside = (label >= 0) & (label < 2 * n_text)
    label = jnp.where(core == 0, label, jnp.where(label < n_text, label + n_text, label - n_text))
    label = jnp.where(inside, label, -1)
    text_unit, label_text = vmem_call(
        text_kernel,
        (((2 * n_text, emb), BF), ((half, emb), BF)),
        texts,
        far_texts,
        label[:, None],
        cost=SMALL,
    )
    mine, label_text, normed = lax.optimization_barrier((mine, label_text, normed))
    other = from_partner(mine, "dp", 1)
    far_mine = from_partner(mine, "txt", 1)
    label_text = swapped(label_text.reshape(n_pair, rows, emb), "txt", cores)
    other, label_text = lax.optimization_barrier((other, label_text))
    far_other = from_partner(other, "txt", 1)
    side = lax.rem(lax.axis_index("dp"), 2).astype(jnp.int32).reshape(1)
    w_up, w_down, pre_act, mixed = vmem_call(
        mlp_kernel,
        (
            ((2, WIDTH, hid), BF),
            ((2, WIDTH, hid), BF),
            ((2, half, hid), F32),
            ((half, WIDTH), BF),
        ),
        side,
        mine,
        other,
        far_mine,
        far_other,
        normed,
        up_bias[None],
        far_bias,
        scalars=1,
    )
    mixed = swapped(mixed.reshape(n_pair, rows, WIDTH), "txt", cores)

    sent, unit_vec, emb_norm, yhat, rstd_out = vmem_call(
        embed_kernel,
        (
            ((n_pair, rows, emb), BF),
            ((rows, emb), F32),
            ((rows, 128), F32),
            ((rows, WIDTH), F32),
            ((rows, 128), F32),
        ),
        mixed,
        own,
        down_bias[None],
        lines,
        proj,
    )
    unit_low = swapped(sent, "txt", cores).reshape(half, emb)

    (back,) = vmem_call(
        softmax_kernel,
        (((half, emb + 128), BF),),
        unit_low,
        text_unit,
        label[:, None],
        scratch=(((half, 2 * n_text), F32),),
    )
    back = back.reshape(n_pair, rows, emb + 128)
    back = swapped(back, "txt", cores)

    sent, out_grad = vmem_call(
        embed_back_kernel,
        (((n_pair, rows, WIDTH), BF), ((rows, WIDTH), F32)),
        back,
        label_text,
        unit_vec,
        emb_norm,
        yhat,
        rstd_out,
        lines,
        proj,
    )
    out_low = swapped(sent, "txt", cores).reshape(half, WIDTH)

    (normed_grad,) = vmem_call(
        mlp_back_kernel, (((half, WIDTH), BF),), out_low, pre_act, w_up, w_down
    )
    normed_grad = swapped(normed_grad.reshape(n_pair, rows, WIDTH), "txt", cores)
    (change,) = vmem_call(
        change_kernel,
        (((n_txt, rows // 2, 2 * share), F32),),
        normed_grad,
        prenorm_gain[None],
        own,
        out_grad,
        step_size[None],
    )
    change = swapped(change, "txt")
    (out,) = vmem_call(result_kernel, (((share, images), F32),), change, resid.T)
    return out.T


def solution(mesh):
    placed = (
        P("dp", "txt"),
        P(),
        P(),
        P("dp", "txt"),
        P("txt"),
        P("txt", "dp"),
        P(),
        P("txt"),
        P("txt"),
        P("txt", None),
        P("txt", None),
        P("dp"),
        P(),
    )
    return jax.shard_map(
        local, mesh=mesh, in_specs=placed, out_specs=P("dp", "txt"), check_vma=False
    )
```

```python
import jax
import jax.numpy as jnp
from jax import lax
from jax.experimental import pallas as pl
from jax.experimental.pallas import tpu as pltpu
from jax.sharding import PartitionSpec as P

WIDTH = 1024
BF = jnp.bfloat16
F32 = jnp.float32
NT = (((1,), (1,)), ((), ()))
SMALL = pl.CostEstimate(flops=1024, bytes_accessed=1024, transcendentals=0)


def swapped(x, axis, groups=None):
    return lax.all_to_all(x, axis, 0, 0, tiled=True, axis_index_groups=groups)


def copies(x, n):
    return jnp.broadcast_to(x, (n, *x.shape))


def from_partner(x, axis, bits):
    pairs = [(i, i ^ bits) for i in range(lax.axis_size(axis))]
    return lax.ppermute(x, axis, pairs)


def pieces(x, count):
    out = []
    for _ in range(count):
        part = lax.reduce_precision(x, 8, 7)
        out.append(part.astype(BF))
        x = x - part
    return out


def row_norm(rows):
    mean = jnp.mean(rows, axis=1, keepdims=True)
    var = jnp.mean(rows * rows, axis=1, keepdims=True) - mean * mean
    rstd = lax.rsqrt(var + 1e-05)
    return (rows - mean) * rstd, rstd


def norm_back(scaled, normed, rstd):
    first = jnp.mean(scaled, axis=1, keepdims=True)
    second = jnp.mean(scaled * normed, axis=1, keepdims=True)
    return (scaled - first - normed * second) * rstd


def vmem_call(body, outs, *args, scalars=0, cost=None, scratch=(), grant=12):
    smem = pl.BlockSpec(memory_space=pltpu.SMEM)
    vmem = pl.BlockSpec(memory_space=pltpu.VMEM)
    return pl.pallas_call(
        body,
        out_shape=[jax.ShapeDtypeStruct(s, d) for s, d in outs],
        in_specs=[smem] * scalars + [vmem] * (len(args) - scalars),
        out_specs=[vmem] * len(outs),
        compiler_params=pltpu.CompilerParams(vmem_limit_bytes=grant << 20),
        cost_estimate=cost,
        scratch_shapes=[pltpu.VMEM(*spec) for spec in scratch],
    )(*args)


def text_kernel(near, far, label, unit, label_text):
    n_text = near.shape[0]
    half = label_text.shape[0]
    step = n_text // 5
    total = jnp.zeros(label_text.shape, F32)
    for side, texts in enumerate((near, far)):
        for k in range(5):
            block = texts[k * step : (k + 1) * step, :].astype(F32)
            squares = jnp.sum(block * block, axis=1, keepdims=True)
            low = (block / jnp.sqrt(squares + 1e-06)).astype(BF)
            start = side * n_text + k * step
            unit[start : start + step, :] = low
            columns = lax.broadcasted_iota(jnp.int32, (half, step), 1) + start
            pick = jnp.where(columns == label[...], 1.0, 0.0).astype(BF)
            total += jnp.dot(pick, low, preferred_element_type=F32)
    label_text[...] = total.astype(BF)


def split_kernel(near, other, proj, rest):
    emb = proj.shape[3]
    for k, part in enumerate((near, other)):
        block = part[:, :emb]
        for y in range(proj.shape[0]):
            proj[y, k] = block
        rest[k] = part[:, emb:]


def stack_kernel(*refs):
    out = refs[-1]
    for k, part in enumerate(refs[:-1]):
        out[k] = part[...]


def rows_kernel(me, near, far, gain, bias, own, lines, normed, far_bias, state, vectors):
    n_txt = vectors.shape[0]
    share = near.shape[2]
    rows, half = own.shape[0], state.shape[1]
    at = me[0]
    first = lax.rem(at, 2) == 0
    for core, side in enumerate((near, far)):
        for y in range(side.shape[0]):
            for x in range(side.shape[1]):
                owner = at ^ (4 * y + 2 * x + core)
                there = pl.multiple_of(owner * share, share)
                left = side[y, x, :, :half]
                right = side[y, x, :, half : 2 * half]
                state[pl.ds(there, share), :] = jnp.where(first, left, right)
                vectors[owner] = side[y, x, :8, 2 * half :].astype(F32)
    parts = far[0, 0, 8:16, 2 * half :].astype(F32)
    for k in range(2):
        far_bias[:, 128 * k : 128 * k + 128] = (
            parts[k : k + 1] + parts[k + 2 : k + 3] + parts[k + 4 : k + 5]
        )
    start = (at // 2) * rows
    column = lax.broadcasted_iota(jnp.int32, (rows, half), 1)
    line = lax.broadcasted_iota(jnp.int32, (rows, half), 0)
    pick = jnp.where(column == line + start, 1.0, 0.0).astype(BF)
    own[...] = lax.dot_general(pick, state[...], NT, preferred_element_type=F32)
    for k in range(2):
        line = [
            vectors[t, 3 * k : 3 * k + 1, :share]
            + vectors[t, 3 * k + 1 : 3 * k + 2, :share]
            + vectors[t, 3 * k + 2 : 3 * k + 3, :share]
            for t in range(n_txt)
        ]
        lines[k : k + 1, :] = jnp.concatenate(line, axis=1)
    xhat, _ = row_norm(state[...].astype(F32).T)
    normed[...] = (xhat * gain[...] + bias[...]).astype(BF)


def proj_kernel(me, near, far, proj):
    share = near.shape[2]
    for core, side in enumerate((near, far)):
        for y in range(side.shape[0]):
            for x in range(side.shape[1]):
                owner = 4 * y + (lax.rem(me[0], 4) ^ (2 * x + core))
                there = pl.multiple_of(owner * share, share)
                proj[pl.ds(there, share), :] = side[y, x]


def mlp_kernel(side, own, other, far_own, far_other, normed, bias, far_bias, *outs):
    w_up, w_down, pre_act, mixed = outs
    depth = own.shape[2]
    for k, (mine, theirs) in enumerate(((own, other), (far_own, far_other))):
        for z in range(own.shape[0]):
            here = pl.multiple_of(2 * depth * z + depth * side[0], depth)
            there = pl.multiple_of(2 * depth * z + depth * (1 - side[0]), depth)
            w_up[k, pl.ds(here, depth), :] = mine[z, 0]
            w_down[k, pl.ds(here, depth), :] = mine[z, 1]
            w_up[k, pl.ds(there, depth), :] = theirs[z, 0]
            w_down[k, pl.ds(there, depth), :] = theirs[z, 1]
    total = jnp.zeros(normed.shape, F32)
    for k, add in enumerate((bias, far_bias)):
        pre = jnp.dot(normed[...], w_up[k], preferred_element_type=F32) + add[...]
        pre_act[k] = pre
        hidden = (pre * jax.nn.sigmoid(1.702 * pre)).astype(BF)
        total += lax.dot_general(hidden, w_down[k], NT, preferred_element_type=F32)
    mixed[...] = total.astype(BF)


def mlp_back_kernel(out_low, pre_act, w_up, w_down, normed_grad):
    total = jnp.zeros(normed_grad.shape, F32)
    for k in range(2):
        hid_grad = jnp.dot(out_low[...], w_down[k], preferred_element_type=F32)
        pre = pre_act[k]
        gate = jax.nn.sigmoid(1.702 * pre)
        act_grad = (hid_grad * (gate + 1.702 * pre * gate * (1.0 - gate))).astype(BF)
        total += lax.dot_general(act_grad, w_up[k], NT, preferred_element_type=F32)
    normed_grad[...] = total.astype(BF)


def softmax_kernel(arrived, text_unit, label, back, label_rows, logits, unit_low):
    half, emb = unit_low.shape
    n = arrived.shape[0]
    texts = jnp.zeros(label_rows.shape, F32)
    for j in range(n):
        unit_low[j * half // n : (j + 1) * half // n, :] = arrived[j, :, :emb]
        texts += arrived[j, :, emb:].astype(F32)
    label_rows[...] = texts
    n_block = 5
    step = text_unit.shape[0] // n_block
    top = None
    for k in range(n_block):
        texts = text_unit[k * step : (k + 1) * step, :]
        block = 100.0 * lax.dot_general(unit_low[...], texts, NT, preferred_element_type=F32)
        logits[:, k * step : (k + 1) * step] = block
        block = jnp.max(block, axis=1, keepdims=True)
        top = block if top is None else jnp.maximum(top, block)
    top = top.astype(BF).astype(F32)
    rest = jnp.zeros_like(top)
    hit = jnp.zeros_like(top)
    total = jnp.zeros((half, emb), F32)
    for k in range(n_block):
        block = jnp.exp(logits[:, k * step : (k + 1) * step] - top)
        columns = lax.broadcasted_iota(jnp.int32, (half, step), 1) + k * step
        target = columns == label[...]
        others = jnp.where(target, 0.0, block)
        rest += jnp.sum(others, axis=1, keepdims=True)
        hit += jnp.sum(jnp.where(target, block, 0.0), axis=1, keepdims=True)
        total += jnp.dot(
            others.astype(BF), text_unit[k * step : (k + 1) * step, :], preferred_element_type=F32
        )
    back[:, :emb] = total.astype(BF)
    lane = lax.broadcasted_iota(jnp.int32, (half, 128), 1)
    rest_high = rest.astype(BF).astype(F32)
    hit_high = hit.astype(BF).astype(F32)
    stats = jnp.zeros((half, 128), F32)
    for k, value in enumerate((top, rest_high, rest - rest_high, hit_high, hit - hit_high)):
        stats = jnp.where(lane == k, value, stats)
    back[:, emb:] = stats.astype(BF)


def embed_kernel(mixed, own, bias, lines, proj, label_text, sent, unit, norm, yhat, rstd):
    n = mixed.shape[0]
    emb = unit.shape[1]
    rows = own.shape[0]
    total = own[...] + bias[...]
    for j in range(n):
        total += mixed[j].astype(F32)
    normed, scale = row_norm(total)
    yhat[...] = normed
    rstd[...] = jnp.broadcast_to(scale, rstd.shape)
    post_normed = (normed * lines[0:1, :] + lines[1:2, :]).astype(BF)
    embedding = jnp.dot(post_normed, proj[...], preferred_element_type=F32)
    length = jnp.sqrt(jnp.sum(embedding * embedding, axis=1, keepdims=True) + 1e-06)
    norm[...] = jnp.broadcast_to(length, norm.shape)
    vec = embedding / length
    unit[...] = vec
    low = vec.astype(BF)
    for j in range(n):
        sent[j, :, :emb] = low
        sent[j, :, emb:] = label_text[j * rows : (j + 1) * rows, :]


def embed_back_kernel(back, label_rows, unit, norm, yhat, rstd, lines, proj, sent, grad):
    n = back.shape[0]
    emb = unit.shape[1]
    stats = [back[j, :, emb:].astype(F32) for j in range(n)]
    top = stats[0][:, 0:1]
    for j in range(1, n):
        top = jnp.maximum(top, stats[j][:, 0:1])
    rest = jnp.zeros_like(top)
    hit = jnp.zeros_like(top)
    unit_grad = jnp.zeros(unit.shape, F32)
    for j in range(n):
        weight = jnp.exp(stats[j][:, 0:1] - top)
        rest += weight * (stats[j][:, 1:2] + stats[j][:, 2:3])
        hit += weight * (stats[j][:, 3:4] + stats[j][:, 4:5])
        unit_grad += weight * back[j, :, :emb].astype(F32)
    unit_grad = (unit_grad - rest * label_rows[...]) * (100.0 / (rest + hit))
    vec = unit[...]
    along = jnp.sum(vec * unit_grad, axis=1, keepdims=True)
    emb_grad = ((unit_grad - vec * along) / norm[:, 0:1]).astype(BF)
    post_grad = lax.dot_general(emb_grad, proj[...], NT, preferred_element_type=F32)
    out_grad = norm_back(post_grad * lines[0:1, :], yhat[...], rstd[:, 0:1])
    grad[...] = out_grad
    low = out_grad.astype(BF)
    for j in range(n):
        sent[j] = low


def change_kernel(parts, gain, own, out_grad, step, sent):
    n, half, _ = sent.shape
    share = own.shape[1] // n
    total = parts[0].astype(F32)
    for j in range(1, parts.shape[0]):
        total += parts[j].astype(F32)
    xhat, scale = row_norm(own[...])
    grad = out_grad[...] + norm_back(total * gain[...], xhat, scale)
    rms = jnp.sqrt(jnp.mean(grad * grad, axis=1, keepdims=True) + 1e-06)
    change = step[0:1, 0:1] * grad / rms
    for j in range(n):
        block = change[:, j * share : (j + 1) * share]
        sent[j, :, :share] = block[:half]
        sent[j, :, share:] = block[half:]


def result_kernel(parts, resid, out):
    n, _, width = parts.shape
    share = width // 2
    blocks = []
    for c in range(2):
        for g in range(n // 2):
            block = parts[2 * g + c]
            blocks += [block[:, :share], block[:, share:]]
    change = jnp.concatenate(blocks, axis=0)
    out[...] = resid[...].astype(F32) + change.T


def local(
    resid,
    prenorm_gain,
    prenorm_bias,
    up_weight,
    up_bias,
    down_weight,
    down_bias,
    post_gain,
    post_bias,
    projection,
    texts,
    labels,
    step_size,
):
    n_txt, n_dp = lax.axis_size("txt"), lax.axis_size("dp")
    n_z, n_pair = n_dp // 2, n_txt // 2
    me = lax.axis_index("txt")
    core = lax.rem(me, 2)
    images, share = resid.shape
    half = images // 2
    rows = images // n_txt
    hid = up_weight.shape[1]
    n_text, emb = texts.shape
    cores = [[2 * i + c for i in range(n_pair)] for c in range(2)]
    along_z = [[2 * z + x for z in range(n_z)] for x in range(2)]

    mine = jnp.stack([up_weight, down_weight.T])
    mine = swapped(copies(mine, n_z), "dp", along_z)

    vectors = jnp.stack(pieces(post_gain, 3) + pieces(post_bias, 3))
    vectors = jnp.pad(vectors, ((0, 2), (0, 128 - share)))
    bias_parts = jnp.stack(pieces(up_bias, 3)).reshape(3 * hid // 128, 128)
    vectors = jnp.concatenate([vectors, bias_parts])
    vectors = jnp.pad(vectors, ((0, share - vectors.shape[0]), (0, 0)))
    chain = jnp.concatenate([projection, resid.T, vectors], axis=1)
    far_texts = from_partner(texts, "txt", 1)
    proj, rest = vmem_call(
        split_kernel,
        (((4, 2, share, emb), BF), ((2, share, images + 128), BF)),
        chain,
        from_partner(chain, "txt", 2),
        cost=SMALL,
    )
    rest = [rest] + [from_partner(rest, "txt", 4 * k) for k in (1, 2, 3)]
    (rest,) = vmem_call(stack_kernel, (((4, *rest[0].shape), BF),), *rest, cost=SMALL)
    far_rest = from_partner(rest, "txt", 1)
    here = me.astype(jnp.int32).reshape(1)
    own, lines, normed, far_bias = vmem_call(
        rows_kernel,
        (((rows, WIDTH), F32), ((8, WIDTH), F32), ((half, WIDTH), BF), ((1, hid), F32)),
        here,
        rest,
        far_rest,
        prenorm_gain[None],
        prenorm_bias[None],
        scalars=1,
        cost=SMALL,
        scratch=(((WIDTH, half), BF), ((n_txt, 8, 128), F32)),
    )

    label = lax.dynamic_slice_in_dim(labels, core * half, half) - (me - core) * n_text
    inside = (label >= 0) & (label < 2 * n_text)
    label = jnp.where(core == 0, label, jnp.where(label < n_text, label + n_text, label - n_text))
    label = jnp.where(inside, label, -1)
    mine, proj, normed = lax.optimization_barrier((mine, proj, normed))
    other = from_partner(mine, "dp", 1)
    far_mine = from_partner(mine, "txt", 1)
    along_y = [[b + 4 * y for y in range(4)] for b in range(4)]
    proj = swapped(proj, "txt", along_y)
    far_other = from_partner(other, "txt", 1)
    far_proj = from_partner(proj, "txt", 1)
    (proj,) = vmem_call(
        proj_kernel, (((WIDTH, emb), BF),), here, proj, far_proj, scalars=1, cost=SMALL
    )
    side = lax.rem(lax.axis_index("dp"), 2).astype(jnp.int32).reshape(1)
    w_up, w_down, pre_act, mixed = vmem_call(
        mlp_kernel,
        (
            ((2, WIDTH, hid), BF),
            ((2, WIDTH, hid), BF),
            ((2, half, hid), F32),
            ((half, WIDTH), BF),
        ),
        side,
        mine,
        other,
        far_mine,
        far_other,
        normed,
        up_bias[None],
        far_bias,
        scalars=1,
    )
    mixed, far_texts = lax.optimization_barrier((mixed, far_texts))
    text_unit, label_text = vmem_call(
        text_kernel,
        (((2 * n_text, emb), BF), ((half, emb), BF)),
        texts,
        far_texts,
        label[:, None],
        cost=pl.CostEstimate(flops=2 * 2**30, bytes_accessed=12 << 20, transcendentals=0),
    )
    mixed = swapped(mixed.reshape(n_pair, rows, WIDTH), "txt", cores)

    sent, unit_vec, emb_norm, yhat, rstd_out = vmem_call(
        embed_kernel,
        (
            ((n_pair, rows, 2 * emb), BF),
            ((rows, emb), F32),
            ((rows, 128), F32),
            ((rows, WIDTH), F32),
            ((rows, 128), F32),
        ),
        mixed,
        own,
        down_bias[None],
        lines,
        proj,
        label_text,
    )
    arrived = swapped(sent, "txt", cores)

    back, label_rows = vmem_call(
        softmax_kernel,
        (((half, emb + 128), BF), ((rows, emb), F32)),
        arrived,
        text_unit,
        label[:, None],
        scratch=(((half, 2 * n_text), F32), ((half, emb), BF)),
    )
    back = back.reshape(n_pair, rows, emb + 128)
    back = swapped(back, "txt", cores)

    sent, out_grad = vmem_call(
        embed_back_kernel,
        (((n_pair, rows, WIDTH), BF), ((rows, WIDTH), F32)),
        back,
        label_rows,
        unit_vec,
        emb_norm,
        yhat,
        rstd_out,
        lines,
        proj,
    )
    out_low = swapped(sent, "txt", cores).reshape(half, WIDTH)

    (normed_grad,) = vmem_call(
        mlp_back_kernel, (((half, WIDTH), BF),), out_low, pre_act, w_up, w_down
    )
    normed_grad = swapped(normed_grad.reshape(n_pair, rows, WIDTH), "txt", cores)
    (change,) = vmem_call(
        change_kernel,
        (((n_txt, rows // 2, 2 * share), F32),),
        normed_grad,
        prenorm_gain[None],
        own,
        out_grad,
        step_size[None],
    )
    change = swapped(change, "txt")
    (out,) = vmem_call(result_kernel, (((share, images), F32),), change, resid.T)
    return out.T


def solution(mesh):
    placed = (
        P("dp", "txt"),
        P(),
        P(),
        P("dp", "txt"),
        P("txt"),
        P("txt", "dp"),
        P(),
        P("txt"),
        P("txt"),
        P("txt", None),
        P("txt", None),
        P("dp"),
        P(),
    )
    return jax.shard_map(
        local, mesh=mesh, in_specs=placed, out_specs=P("dp", "txt"), check_vma=False
    )
```

```python
import jax
import jax.numpy as jnp
from jax import lax
from jax.experimental import pallas as pl
from jax.experimental.pallas import tpu as pltpu
from jax.sharding import PartitionSpec as P

WIDTH = 1024
BF = jnp.bfloat16
F32 = jnp.float32
NT = (((1,), (1,)), ((), ()))
SMALL = pl.CostEstimate(flops=1024, bytes_accessed=1024, transcendentals=0)


def swapped(x, axis, groups=None):
    return lax.all_to_all(x, axis, 0, 0, tiled=True, axis_index_groups=groups)


def copies(x, n):
    return jnp.broadcast_to(x, (n, *x.shape))


def from_partner(x, axis, bits):
    pairs = [(i, i ^ bits) for i in range(lax.axis_size(axis))]
    return lax.ppermute(x, axis, pairs)


def pieces(x, count):
    out = []
    for _ in range(count):
        part = lax.reduce_precision(x, 8, 7)
        out.append(part.astype(BF))
        x = x - part
    return out


def row_norm(rows):
    mean = jnp.mean(rows, axis=1, keepdims=True)
    var = jnp.mean(rows * rows, axis=1, keepdims=True) - mean * mean
    rstd = lax.rsqrt(var + 1e-05)
    return (rows - mean) * rstd, rstd


def norm_back(scaled, normed, rstd):
    first = jnp.mean(scaled, axis=1, keepdims=True)
    second = jnp.mean(scaled * normed, axis=1, keepdims=True)
    return (scaled - first - normed * second) * rstd


def call(body, outs, spaces, *args, cost=None, scratch=(), sems=0):
    kinds = {"v": pltpu.VMEM, "h": pltpu.HBM, "a": pl.ANY}
    specs = [pl.BlockSpec(memory_space=kinds[c]) for c in spaces]
    shapes = [pltpu.VMEM(*spec) for spec in scratch]
    if sems:
        shapes.append(pltpu.SemaphoreType.DMA((sems,)))
    return pl.pallas_call(
        body,
        out_shape=[
            pltpu.HBM(*out) if c == "h" else jax.ShapeDtypeStruct(*out)
            for c, out in zip(spaces[len(args) :], outs)
        ],
        in_specs=specs[: len(args)],
        out_specs=specs[len(args) :],
        scratch_shapes=shapes,
        compiler_params=pltpu.CompilerParams(vmem_limit_bytes=24 << 20),
        cost_estimate=cost,
    )(*(
        pltpu.with_memory_space_constraint(arg, pltpu.HBM) if c == "h" else arg
        for c, arg in zip(spaces, args)
    ))


def local_labels(labels, n_text):
    half = labels.shape[0] // 2
    me = lax.axis_index("txt")
    core = lax.rem(me, 2)
    label = labels[pl.ds(pl.multiple_of(core * half, half), half), :] - (me - core) * n_text
    inside = (label >= 0) & (label < 2 * n_text)
    turned = jnp.where(label < n_text, label + n_text, label - n_text)
    return jnp.where(inside, jnp.where(core == 0, label, turned), -1)


def text_kernel(near, far, labels, unit, label_text, held, sem):
    n_text = near.shape[0]
    half = label_text.shape[0]
    step = 256
    count = n_text // step
    loads = []
    for k in range(2 * count):
        side = near if k < count else far
        loads.append(
            pltpu.make_async_copy(
                side.at[pl.ds((k % count) * step, step)], held.at[pl.ds(k * step, step)], sem.at[k]
            )
        )
        loads[k].start()
    label = local_labels(labels, n_text)
    total = jnp.zeros(label_text.shape, F32)
    stores = []
    for k in range(2 * count):
        loads[k].wait()
        block = held[k * step : (k + 1) * step, :].astype(F32)
        squares = jnp.sum(block * block, axis=1, keepdims=True)
        low = (block / jnp.sqrt(squares + 1e-06)).astype(BF)
        held[k * step : (k + 1) * step, :] = low
        place = pl.ds(k * step, step)
        stores.append(
            pltpu.make_async_copy(held.at[place], unit.at[place], sem.at[2 * count + k])
        )
        stores[k].start()
        columns = lax.broadcasted_iota(jnp.int32, (half, step), 1) + k * step
        pick = jnp.where(columns == label, 1.0, 0.0).astype(BF)
        total += jnp.dot(pick, low, preferred_element_type=F32)
    label_text[...] = total.astype(BF)
    for store in stores:
        store.wait()


def split_kernel(near, other, proj, rest):
    emb = proj.shape[3]
    for k, part in enumerate((near, other)):
        block = part[:, :emb]
        for y in range(proj.shape[0]):
            proj[y, k] = block
        rest[k] = part[:, emb:]


def stack_kernel(*refs):
    out = refs[-1]
    for k, part in enumerate(refs[:-1]):
        out[k] = part[...]


def rows_kernel(near, far, gain, bias, own, lines, normed, far_bias, state, vectors):
    n_txt = vectors.shape[0]
    share = near.shape[2]
    rows, half = own.shape[0], state.shape[1]
    at = lax.axis_index("txt")
    first = lax.rem(at, 2) == 0
    for core, side in enumerate((near, far)):
        for y in range(side.shape[0]):
            for x in range(side.shape[1]):
                owner = at ^ (4 * y + 2 * x + core)
                there = pl.multiple_of(owner * share, share)
                left = side[y, x, :, :half]
                right = side[y, x, :, half : 2 * half]
                state[pl.ds(there, share), :] = jnp.where(first, left, right)
                vectors[owner] = side[y, x, :8, 2 * half :].astype(F32)
    parts = far[0, 0, 8:16, 2 * half :].astype(F32)
    for k in range(2):
        far_bias[:, 128 * k : 128 * k + 128] = (
            parts[k : k + 1] + parts[k + 2 : k + 3] + parts[k + 4 : k + 5]
        )
    start = (at // 2) * rows
    column = lax.broadcasted_iota(jnp.int32, (rows, half), 1)
    line = lax.broadcasted_iota(jnp.int32, (rows, half), 0)
    pick = jnp.where(column == line + start, 1.0, 0.0).astype(BF)
    own[...] = lax.dot_general(pick, state[...], NT, preferred_element_type=F32)
    for k in range(2):
        line = [
            vectors[t, 3 * k : 3 * k + 1, :share]
            + vectors[t, 3 * k + 1 : 3 * k + 2, :share]
            + vectors[t, 3 * k + 2 : 3 * k + 3, :share]
            for t in range(n_txt)
        ]
        lines[k : k + 1, :] = jnp.concatenate(line, axis=1)
    xhat, _ = row_norm(state[...].astype(F32).T)
    normed[...] = (xhat * gain[...] + bias[...]).astype(BF)


def ordered_proj(near, far, proj, sem):
    low = lax.rem(lax.axis_index("txt"), 4)
    loads = []
    for core, side in enumerate((near, far)):
        for x in range(2):
            k = 2 * x + core
            place = proj.at[:, low ^ k]
            loads.append(pltpu.make_async_copy(side.at[:, x], place, sem.at[k]))
            loads[-1].start()
    return loads


def ordered_weights(own, other, far_own, far_other, weights, sem):
    side = lax.rem(lax.axis_index("dp"), 2)
    loads = {}
    for matrix in weights:
        for k, pair in enumerate(((own, other), (far_own, far_other))):
            for x, part in enumerate(pair):
                place = weights[matrix].at[k, :, side if x == 0 else 1 - side]
                number = 4 * matrix + 2 * k + x
                load = pltpu.make_async_copy(part.at[:, matrix], place, sem.at[number])
                load.start()
                loads[matrix, k, x] = load
    return loads


def mlp_kernel(own, other, far_own, far_other, normed, bias, far_bias, *refs):
    pre_act, mixed, up, down, sem = refs
    width, hid = normed.shape[1], bias.shape[1]
    loads = ordered_weights(own, other, far_own, far_other, {0: up, 1: down}, sem)
    total = jnp.zeros(normed.shape, F32)
    for k, add in enumerate((bias, far_bias)):
        for matrix in range(2):
            for x in range(2):
                loads[matrix, k, x].wait()
        w_up = up[k].reshape(width, hid)
        pre = jnp.dot(normed[...], w_up, preferred_element_type=F32) + add[...]
        pre_act[k] = pre
        hidden = (pre * jax.nn.sigmoid(1.702 * pre)).astype(BF)
        w_down = down[k].reshape(width, hid)
        total += lax.dot_general(hidden, w_down, NT, preferred_element_type=F32)
    mixed[...] = total.astype(BF)


def mlp_back_kernel(own, other, far_own, far_other, arrived, pre_act, *refs):
    normed_grad, up, down, sem = refs
    width, hid = arrived.shape[1], pre_act.shape[2]
    loads = ordered_weights(own, other, far_own, far_other, {1: down, 0: up}, sem)
    total = jnp.zeros(normed_grad.shape, F32)
    for k in range(2):
        for x in range(2):
            loads[1, k, x].wait()
        w_down = down[k].reshape(width, hid)
        hid_grad = jnp.dot(arrived[...], w_down, preferred_element_type=F32)
        pre = pre_act[k]
        gate = jax.nn.sigmoid(1.702 * pre)
        act_grad = (hid_grad * (gate + 1.702 * pre * gate * (1.0 - gate))).astype(BF)
        for x in range(2):
            loads[0, k, x].wait()
        w_up = up[k].reshape(width, hid)
        total += lax.dot_general(act_grad, w_up, NT, preferred_element_type=F32)
    normed_grad[...] = total.astype(BF)


def softmax_kernel(arrived, text_unit, labels, back, label_rows, logits, unit_low, held, sem):
    half, emb = unit_low.shape
    n = arrived.shape[0]
    n_block = 5
    step = text_unit.shape[0] // n_block
    loads = []
    for k in range(n_block):
        place = pl.ds(k * step, step)
        loads.append(pltpu.make_async_copy(text_unit.at[place], held.at[place], sem.at[k]))
        loads[k].start()
    texts = jnp.zeros(label_rows.shape, F32)
    for j in range(n):
        unit_low[j * half // n : (j + 1) * half // n, :] = arrived[j, :, :emb]
        texts += arrived[j, :, emb:].astype(F32)
    label_rows[...] = texts
    label = local_labels(labels, text_unit.shape[0] // 2)
    top = None
    for k in range(n_block):
        loads[k].wait()
        texts = held[k * step : (k + 1) * step, :]
        block = 100.0 * lax.dot_general(unit_low[...], texts, NT, preferred_element_type=F32)
        logits[:, k * step : (k + 1) * step] = block
        block = jnp.max(block, axis=1, keepdims=True)
        top = block if top is None else jnp.maximum(top, block)
    top = top.astype(BF).astype(F32)
    rest = jnp.zeros_like(top)
    hit = jnp.zeros_like(top)
    total = jnp.zeros((half, emb), F32)
    for k in range(n_block):
        block = jnp.exp(logits[:, k * step : (k + 1) * step] - top)
        columns = lax.broadcasted_iota(jnp.int32, (half, step), 1) + k * step
        target = columns == label
        others = jnp.where(target, 0.0, block)
        rest += jnp.sum(others, axis=1, keepdims=True)
        hit += jnp.sum(jnp.where(target, block, 0.0), axis=1, keepdims=True)
        total += jnp.dot(
            others.astype(BF), held[k * step : (k + 1) * step, :], preferred_element_type=F32
        )
    back[:, :emb] = total.astype(BF)
    lane = lax.broadcasted_iota(jnp.int32, (half, 128), 1)
    rest_high = rest.astype(BF).astype(F32)
    hit_high = hit.astype(BF).astype(F32)
    stats = jnp.zeros((half, 128), F32)
    for k, value in enumerate((top, rest_high, rest - rest_high, hit_high, hit - hit_high)):
        stats = jnp.where(lane == k, value, stats)
    back[:, emb:] = stats.astype(BF)


def embed_kernel(mixed, own, bias, lines, near, far, label_text, *refs):
    sent, unit, norm, yhat, rstd, proj, sem = refs
    loads = ordered_proj(near, far, proj, sem)
    n = mixed.shape[0]
    emb = unit.shape[1]
    rows = own.shape[0]
    total = own[...] + bias[...]
    for j in range(n):
        total += mixed[j].astype(F32)
    normed, scale = row_norm(total)
    yhat[...] = normed
    rstd[...] = jnp.broadcast_to(scale, rstd.shape)
    post_normed = (normed * lines[0:1, :] + lines[1:2, :]).astype(BF)
    for load in loads:
        load.wait()
    w_proj = proj[...].reshape(-1, emb)
    embedding = jnp.dot(post_normed, w_proj, preferred_element_type=F32)
    length = jnp.sqrt(jnp.sum(embedding * embedding, axis=1, keepdims=True) + 1e-06)
    norm[...] = jnp.broadcast_to(length, norm.shape)
    vec = embedding / length
    unit[...] = vec
    low = vec.astype(BF)
    for j in range(n):
        sent[j, :, :emb] = low
        sent[j, :, emb:] = label_text[j * rows : (j + 1) * rows, :]


def embed_back_kernel(back, label_rows, unit, norm, yhat, rstd, lines, near, far, *refs):
    sent, grad, proj, sem = refs
    loads = ordered_proj(near, far, proj, sem)
    n = back.shape[0]
    emb = unit.shape[1]
    stats = [back[j, :, emb:].astype(F32) for j in range(n)]
    top = stats[0][:, 0:1]
    for j in range(1, n):
        top = jnp.maximum(top, stats[j][:, 0:1])
    rest = jnp.zeros_like(top)
    hit = jnp.zeros_like(top)
    unit_grad = jnp.zeros(unit.shape, F32)
    for j in range(n):
        weight = jnp.exp(stats[j][:, 0:1] - top)
        rest += weight * (stats[j][:, 1:2] + stats[j][:, 2:3])
        hit += weight * (stats[j][:, 3:4] + stats[j][:, 4:5])
        unit_grad += weight * back[j, :, :emb].astype(F32)
    unit_grad = (unit_grad - rest * label_rows[...]) * (100.0 / (rest + hit))
    vec = unit[...]
    along = jnp.sum(vec * unit_grad, axis=1, keepdims=True)
    emb_grad = ((unit_grad - vec * along) / norm[:, 0:1]).astype(BF)
    for load in loads:
        load.wait()
    w_proj = proj[...].reshape(-1, emb)
    post_grad = lax.dot_general(emb_grad, w_proj, NT, preferred_element_type=F32)
    out_grad = norm_back(post_grad * lines[0:1, :], yhat[...], rstd[:, 0:1])
    grad[...] = out_grad
    low = out_grad.astype(BF)
    for j in range(n):
        sent[j] = low


def change_kernel(parts, gain, own, out_grad, step, sent):
    n, half, _ = sent.shape
    share = own.shape[1] // n
    total = parts[0].astype(F32)
    for j in range(1, parts.shape[0]):
        total += parts[j].astype(F32)
    xhat, scale = row_norm(own[...])
    grad = out_grad[...] + norm_back(total * gain[...], xhat, scale)
    rms = jnp.sqrt(jnp.mean(grad * grad, axis=1, keepdims=True) + 1e-06)
    change = step[0:1, 0:1] * grad / rms
    for j in range(n):
        block = change[:, j * share : (j + 1) * share]
        sent[j, :, :share] = block[:half]
        sent[j, :, share:] = block[half:]


def result_kernel(parts, resid, out):
    n, _, width = parts.shape
    share = width // 2
    blocks = []
    for c in range(2):
        for g in range(n // 2):
            block = parts[2 * g + c]
            blocks += [block[:, :share], block[:, share:]]
    change = jnp.concatenate(blocks, axis=0)
    out[...] = resid[...].astype(F32) + change.T


def local(
    resid,
    prenorm_gain,
    prenorm_bias,
    up_weight,
    up_bias,
    down_weight,
    down_bias,
    post_gain,
    post_bias,
    projection,
    texts,
    labels,
    step_size,
):
    n_txt, n_dp = lax.axis_size("txt"), lax.axis_size("dp")
    n_z, n_pair = n_dp // 2, n_txt // 2
    images, share = resid.shape
    half = images // 2
    rows = images // n_txt
    hid = up_weight.shape[1]
    n_text, emb = texts.shape
    cores = [[2 * i + c for i in range(n_pair)] for c in range(2)]
    along_y = [[b + 4 * y for y in range(4)] for b in range(4)]
    along_z = [[2 * z + x for z in range(n_z)] for x in range(2)]

    mine = jnp.stack([up_weight, down_weight.T], axis=0)
    mine = swapped(copies(mine, n_z), "dp", along_z)

    vectors = jnp.stack(pieces(post_gain, 3) + pieces(post_bias, 3))
    vectors = jnp.pad(vectors, ((0, 2), (0, 128 - share)))
    bias_parts = jnp.stack(pieces(up_bias, 3)).reshape(3 * hid // 128, 128)
    vectors = jnp.concatenate([vectors, bias_parts])
    vectors = jnp.pad(vectors, ((0, share - vectors.shape[0]), (0, 0)))
    chain = jnp.concatenate([projection, resid.T, vectors], axis=1)
    chain, labels = lax.optimization_barrier((chain, labels[:, None]))
    far_texts = from_partner(texts, "txt", 1)
    proj, rest = call(
        split_kernel,
        (((4, 2, share, emb), BF), ((2, share, images + 128), BF)),
        "vvvv",
        chain,
        from_partner(chain, "txt", 2),
        cost=SMALL,
    )
    rest = [rest] + [from_partner(rest, "txt", 4 * k) for k in (1, 2, 3)]
    (rest,) = call(stack_kernel, (((4, *rest[0].shape), BF),), "vvvvv", *rest, cost=SMALL)
    far_rest = from_partner(rest, "txt", 1)
    own, lines, normed, far_bias = call(
        rows_kernel,
        (((rows, WIDTH), F32), ((8, WIDTH), F32), ((half, WIDTH), BF), ((1, hid), F32)),
        "vvvvvvvv",
        rest,
        far_rest,
        prenorm_gain[None],
        prenorm_bias[None],
        cost=SMALL,
        scratch=(((WIDTH, half), BF), ((n_txt, 8, 128), F32)),
    )

    mine, proj, normed = lax.optimization_barrier((mine, proj, normed))
    other = from_partner(mine, "dp", 1)
    far_mine = from_partner(mine, "txt", 1)
    proj = swapped(proj, "txt", along_y)
    far_other = from_partner(other, "txt", 1)
    far_proj = from_partner(proj, "txt", 1)
    weights = (mine, other, far_mine, far_other)
    held = ((2, n_z, 2, WIDTH // n_dp, hid), BF)
    pre_act, mixed = call(
        mlp_kernel,
        (((2, half, hid), F32), ((half, WIDTH), BF)),
        "aaaavvvvv",
        *weights,
        normed,
        up_bias[None],
        far_bias,
        scratch=(held, held),
        sems=8,
    )
    mixed, far_texts = lax.optimization_barrier((mixed, far_texts))
    text_unit, label_text = call(
        text_kernel,
        (((2 * n_text, emb), BF), ((half, emb), BF)),
        "hhvhv",
        texts,
        far_texts,
        labels,
        cost=pl.CostEstimate(flops=2**31, bytes_accessed=12 << 20, transcendentals=0),
        scratch=(((2 * n_text, emb), BF),),
        sems=4 * n_text // 256,
    )
    mixed = swapped(mixed.reshape(n_pair, rows, WIDTH), "txt", cores)

    held_proj = ((4, 4, share, emb), BF)
    sent, unit_vec, emb_norm, yhat, rstd_out = call(
        embed_kernel,
        (
            ((n_pair, rows, 2 * emb), BF),
            ((rows, emb), F32),
            ((rows, 128), F32),
            ((rows, WIDTH), F32),
            ((rows, 128), F32),
        ),
        "vvvvhhvvvvvv",
        mixed,
        own,
        down_bias[None],
        lines,
        proj,
        far_proj,
        label_text,
        scratch=(held_proj,),
        sems=4,
    )
    arrived = swapped(sent, "txt", cores)

    back, label_rows = call(
        softmax_kernel,
        (((half, emb + 128), BF), ((rows, emb), F32)),
        "vhvvv",
        arrived,
        text_unit,
        labels,
        scratch=(((half, 2 * n_text), F32), ((half, emb), BF), ((2 * n_text, emb), BF)),
        sems=5,
    )
    back = swapped(back.reshape(n_pair, rows, emb + 128), "txt", cores)

    sent, out_grad = call(
        embed_back_kernel,
        (((n_pair, rows, WIDTH), BF), ((rows, WIDTH), F32)),
        "vvvvvvvhhvv",
        back,
        label_rows,
        unit_vec,
        emb_norm,
        yhat,
        rstd_out,
        lines,
        proj,
        far_proj,
        scratch=(held_proj,),
        sems=4,
    )
    out_low = swapped(sent, "txt", cores).reshape(half, WIDTH)

    (normed_grad,) = call(
        mlp_back_kernel,
        (((half, WIDTH), BF),),
        "aaaavvv",
        *weights,
        out_low,
        pre_act,
        scratch=(held, held),
        sems=8,
    )
    normed_grad = swapped(normed_grad.reshape(n_pair, rows, WIDTH), "txt", cores)
    (change,) = call(
        change_kernel,
        (((n_txt, rows // 2, 2 * share), F32),),
        "vvvvvv",
        normed_grad,
        prenorm_gain[None],
        own,
        out_grad,
        step_size[None],
    )
    change = swapped(change, "txt")
    (out,) = call(result_kernel, (((share, images), F32),), "vvv", change, resid.T)
    return out.T


def solution(mesh):
    placed = (
        P("dp", "txt"),
        P(),
        P(),
        P("dp", "txt"),
        P("txt"),
        P("txt", "dp"),
        P(),
        P("txt"),
        P("txt"),
        P("txt", None),
        P("txt", None),
        P("dp"),
        P(),
    )
    return jax.shard_map(
        local, mesh=mesh, in_specs=placed, out_specs=P("dp", "txt"), check_vma=False
    )
```

```python
import jax
import jax.numpy as jnp
from jax import lax
from jax.experimental import pallas as pl
from jax.experimental.pallas import tpu as pltpu
from jax.sharding import PartitionSpec as P

WIDTH = 1024
BF = jnp.bfloat16
F32 = jnp.float32
NT = (((1,), (1,)), ((), ()))
SMALL = pl.CostEstimate(flops=1024, bytes_accessed=1024, transcendentals=0)


def swapped(x, axis, groups=None):
    return lax.all_to_all(x, axis, 0, 0, tiled=True, axis_index_groups=groups)


def copies(x, n):
    return jnp.broadcast_to(x, (n, *x.shape))


def from_partner(x, axis, bits):
    pairs = [(i, i ^ bits) for i in range(lax.axis_size(axis))]
    return lax.ppermute(x, axis, pairs)


def row_norm(rows):
    mean = jnp.mean(rows, axis=1, keepdims=True)
    var = jnp.mean(rows * rows, axis=1, keepdims=True) - mean * mean
    rstd = lax.rsqrt(var + 1e-05)
    return (rows - mean) * rstd, rstd


def norm_back(scaled, normed, rstd):
    first = jnp.mean(scaled, axis=1, keepdims=True)
    second = jnp.mean(scaled * normed, axis=1, keepdims=True)
    return (scaled - first - normed * second) * rstd


def call(body, outs, spaces, *args, cost=None, scratch=(), sems=0):
    kinds = {"v": pltpu.VMEM, "h": pltpu.HBM, "a": pl.ANY}
    specs = [pl.BlockSpec(memory_space=kinds[c]) for c in spaces]
    shapes = [pltpu.VMEM(*spec) for spec in scratch]
    if sems:
        shapes.append(pltpu.SemaphoreType.DMA((sems,)))
    return pl.pallas_call(
        body,
        out_shape=[
            pltpu.HBM(*out) if c == "h" else jax.ShapeDtypeStruct(*out)
            for c, out in zip(spaces[len(args) :], outs)
        ],
        in_specs=specs[: len(args)],
        out_specs=specs[len(args) :],
        scratch_shapes=shapes,
        compiler_params=pltpu.CompilerParams(vmem_limit_bytes=24 << 20),
        cost_estimate=cost,
    )(*(
        pltpu.with_memory_space_constraint(arg, pltpu.HBM) if c == "h" else arg
        for c, arg in zip(spaces, args)
    ))


def local_labels(labels, n_text):
    half = labels.shape[0] // 2
    me = lax.axis_index("txt")
    core = lax.rem(me, 2)
    label = labels[pl.ds(pl.multiple_of(core * half, half), half), :] - (me - core) * n_text
    inside = (label >= 0) & (label < 2 * n_text)
    turned = jnp.where(label < n_text, label + n_text, label - n_text)
    return jnp.where(inside, jnp.where(core == 0, label, turned), -1)


def text_kernel(near, far, labels, unit, label_text, held, sem):
    n_text = near.shape[0]
    half = label_text.shape[0]
    step = 256
    count = n_text // step
    loads = []
    for k in range(2 * count):
        side = near if k < count else far
        loads.append(
            pltpu.make_async_copy(
                side.at[pl.ds((k % count) * step, step)], held.at[pl.ds(k * step, step)], sem.at[k]
            )
        )
        loads[k].start()
    label = local_labels(labels, n_text)
    total = jnp.zeros(label_text.shape, F32)
    stores = []
    for k in range(2 * count):
        loads[k].wait()
        block = held[k * step : (k + 1) * step, :].astype(F32)
        squares = jnp.sum(block * block, axis=1, keepdims=True)
        low = (block / jnp.sqrt(squares + 1e-06)).astype(BF)
        held[k * step : (k + 1) * step, :] = low
        place = pl.ds(k * step, step)
        stores.append(
            pltpu.make_async_copy(held.at[place], unit.at[place], sem.at[2 * count + k])
        )
        stores[k].start()
        columns = lax.broadcasted_iota(jnp.int32, (half, step), 1) + k * step
        pick = jnp.where(columns == label, 1.0, 0.0).astype(BF)
        total += jnp.dot(pick, low, preferred_element_type=F32)
    label_text[...] = total.astype(BF)
    for store in stores:
        store.wait()


def message_kernel(projection, resid, gain, bias, up_bias, out):
    emb, images = projection.shape[1], resid.shape[1]

    def parts(value):
        found = []
        for _ in range(3):
            part = value.astype(BF).astype(F32)
            found.append(part)
            value = value - part
        return found

    out[:, :emb] = projection[...]
    out[:, emb : emb + images] = resid[...]
    blank = jnp.zeros((1, 128 - gain.shape[1]), F32)
    lines = [
        jnp.concatenate([part, blank], axis=1)
        for part in parts(gain[...]) + parts(bias[...])
    ]
    lines += [jnp.zeros((1, 128), F32)] * 2
    lines += [part[:, 128 * k : 128 * k + 128] for part in parts(up_bias[...]) for k in range(2)]
    lines += [jnp.zeros((1, 128), F32)] * 2
    lines = jnp.concatenate(lines, axis=0)
    out[:, emb + images :] = jnp.zeros((out.shape[0], 128), BF)
    out[: lines.shape[0], emb + images :] = lines.astype(BF)


def split_kernel(near, other, proj, rest):
    emb = proj.shape[3]
    for k, part in enumerate((near, other)):
        block = part[:, :emb]
        for y in range(proj.shape[0]):
            proj[y, k] = block
        rest[k] = part[:, emb:]


def stack_kernel(*refs):
    out = refs[-1]
    for k, part in enumerate(refs[:-1]):
        out[k] = part[...]


def rows_kernel(near, far, gain, bias, own, lines, normed, far_bias, state, vectors):
    n_txt = vectors.shape[0]
    share = near.shape[2]
    rows, half = own.shape[0], state.shape[1]
    at = lax.axis_index("txt")
    first = lax.rem(at, 2) == 0
    for core, side in enumerate((near, far)):
        for y in range(side.shape[0]):
            for x in range(side.shape[1]):
                owner = at ^ (4 * y + 2 * x + core)
                there = pl.multiple_of(owner * share, share)
                left = side[y, x, :, :half]
                right = side[y, x, :, half : 2 * half]
                state[pl.ds(there, share), :] = jnp.where(first, left, right)
                vectors[owner] = side[y, x, :8, 2 * half :].astype(F32)
    parts = far[0, 0, 8:16, 2 * half :].astype(F32)
    for k in range(2):
        far_bias[:, 128 * k : 128 * k + 128] = (
            parts[k : k + 1] + parts[k + 2 : k + 3] + parts[k + 4 : k + 5]
        )
    start = (at // 2) * rows
    column = lax.broadcasted_iota(jnp.int32, (rows, half), 1)
    line = lax.broadcasted_iota(jnp.int32, (rows, half), 0)
    pick = jnp.where(column == line + start, 1.0, 0.0).astype(BF)
    own[...] = lax.dot_general(pick, state[...], NT, preferred_element_type=F32)
    for k in range(2):
        line = [
            vectors[t, 3 * k : 3 * k + 1, :share]
            + vectors[t, 3 * k + 1 : 3 * k + 2, :share]
            + vectors[t, 3 * k + 2 : 3 * k + 3, :share]
            for t in range(n_txt)
        ]
        lines[k : k + 1, :] = jnp.concatenate(line, axis=1)
    xhat, _ = row_norm(state[...].astype(F32).T)
    normed[...] = (xhat * gain[...] + bias[...]).astype(BF)


def in_arrival_order(rows, share):
    low = lax.rem(lax.axis_index("txt"), 4)
    sides = ([], [])
    for y in range(rows.shape[1] // (4 * share)):
        pair = [rows[:, (4 * y + 2 * x) * share : (4 * y + 2 * x + 2) * share] for x in range(2)]
        for x in range(2):
            block = jnp.where(low < 2, pair[x], pair[1 - x])
            first, second = block[:, :share], block[:, share:]
            even = lax.rem(low, 2) == 0
            sides[0].append(jnp.where(even, first, second))
            sides[1].append(jnp.where(even, second, first))
    return [jnp.concatenate(side, axis=1) for side in sides]


def in_natural_order(near, far, share):
    low = lax.rem(lax.axis_index("txt"), 4)
    even = lax.rem(low, 2) == 0
    blocks = []
    for y in range(near.shape[1] // (2 * share)):
        pair = []
        for x in range(2):
            place = slice((2 * y + x) * share, (2 * y + x + 1) * share)
            first = jnp.where(even, near[:, place], far[:, place])
            second = jnp.where(even, far[:, place], near[:, place])
            pair.append(jnp.concatenate([first, second], axis=1))
        blocks += [jnp.where(low < 2, pair[x], pair[1 - x]) for x in range(2)]
    return jnp.concatenate(blocks, axis=1)


def ordered_weights(own, other, far_own, far_other, weights, sem):
    side = lax.rem(lax.axis_index("dp"), 2)
    loads = {}
    for matrix in weights:
        for k, pair in enumerate(((own, other), (far_own, far_other))):
            for x, part in enumerate(pair):
                place = weights[matrix].at[k, :, side if x == 0 else 1 - side]
                number = 4 * matrix + 2 * k + x
                load = pltpu.make_async_copy(part.at[:, matrix], place, sem.at[number])
                load.start()
                loads[matrix, k, x] = load
    return loads


def mlp_kernel(own, other, far_own, far_other, normed, bias, far_bias, *refs):
    pre_act, mixed, up, down, sem = refs
    width, hid = normed.shape[1], bias.shape[1]
    loads = ordered_weights(own, other, far_own, far_other, {0: up, 1: down}, sem)
    total = jnp.zeros(normed.shape, F32)
    for k, add in enumerate((bias, far_bias)):
        for matrix in range(2):
            for x in range(2):
                loads[matrix, k, x].wait()
        w_up = up[k].reshape(width, hid)
        pre = jnp.dot(normed[...], w_up, preferred_element_type=F32) + add[...]
        pre_act[k] = pre
        hidden = (pre * jax.nn.sigmoid(1.702 * pre)).astype(BF)
        w_down = down[k].reshape(width, hid)
        total += lax.dot_general(hidden, w_down, NT, preferred_element_type=F32)
    mixed[...] = total.astype(BF)


def mlp_back_kernel(own, other, far_own, far_other, arrived, pre_act, *refs):
    normed_grad, up, down, sem = refs
    width, hid = arrived.shape[1], pre_act.shape[2]
    loads = ordered_weights(own, other, far_own, far_other, {1: down, 0: up}, sem)
    total = jnp.zeros(normed_grad.shape, F32)
    for k in range(2):
        for x in range(2):
            loads[1, k, x].wait()
        w_down = down[k].reshape(width, hid)
        hid_grad = jnp.dot(arrived[...], w_down, preferred_element_type=F32)
        pre = pre_act[k]
        gate = jax.nn.sigmoid(1.702 * pre)
        act_grad = (hid_grad * (gate + 1.702 * pre * gate * (1.0 - gate))).astype(BF)
        for x in range(2):
            loads[0, k, x].wait()
        w_up = up[k].reshape(width, hid)
        total += lax.dot_general(act_grad, w_up, NT, preferred_element_type=F32)
    normed_grad[...] = total.astype(BF)


def softmax_kernel(arrived, text_unit, labels, back, label_rows, logits, unit_low, held, sem):
    half, emb = unit_low.shape
    n = arrived.shape[0]
    n_block = 5
    step = text_unit.shape[0] // n_block
    loads = []
    for k in range(n_block):
        place = pl.ds(k * step, step)
        loads.append(pltpu.make_async_copy(text_unit.at[place], held.at[place], sem.at[k]))
        loads[k].start()
    texts = jnp.zeros(label_rows.shape, F32)
    for j in range(n):
        unit_low[j * half // n : (j + 1) * half // n, :] = arrived[j, :, :emb]
        texts += arrived[j, :, emb:].astype(F32)
    label_rows[...] = texts
    label = local_labels(labels, text_unit.shape[0] // 2)
    top = None
    for k in range(n_block):
        loads[k].wait()
        texts = held[k * step : (k + 1) * step, :]
        block = 100.0 * lax.dot_general(unit_low[...], texts, NT, preferred_element_type=F32)
        logits[:, k * step : (k + 1) * step] = block
        block = jnp.max(block, axis=1, keepdims=True)
        top = block if top is None else jnp.maximum(top, block)
    top = top.astype(BF).astype(F32)
    rest = jnp.zeros_like(top)
    hit = jnp.zeros_like(top)
    total = jnp.zeros((half, emb), F32)
    for k in range(n_block):
        block = jnp.exp(logits[:, k * step : (k + 1) * step] - top)
        columns = lax.broadcasted_iota(jnp.int32, (half, step), 1) + k * step
        target = columns == label
        others = jnp.where(target, 0.0, block)
        rest += jnp.sum(others, axis=1, keepdims=True)
        hit += jnp.sum(jnp.where(target, block, 0.0), axis=1, keepdims=True)
        total += jnp.dot(
            others.astype(BF), held[k * step : (k + 1) * step, :], preferred_element_type=F32
        )
    back[:, :emb] = total.astype(BF)
    lane = lax.broadcasted_iota(jnp.int32, (half, 128), 1)
    rest_high = rest.astype(BF).astype(F32)
    hit_high = hit.astype(BF).astype(F32)
    stats = jnp.zeros((half, 128), F32)
    for k, value in enumerate((top, rest_high, rest - rest_high, hit_high, hit - hit_high)):
        stats = jnp.where(lane == k, value, stats)
    back[:, emb:] = stats.astype(BF)


def embed_kernel(mixed, own, bias, lines, near, far, label_text, *refs):
    sent, unit, norm, yhat, rstd = refs
    n = mixed.shape[0]
    emb = unit.shape[1]
    rows = own.shape[0]
    total = own[...] + bias[...]
    for j in range(n):
        total += mixed[j].astype(F32)
    normed, scale = row_norm(total)
    yhat[...] = normed
    rstd[...] = jnp.broadcast_to(scale, rstd.shape)
    post_normed = normed * lines[0:1, :] + lines[1:2, :]
    embedding = jnp.zeros(unit.shape, F32)
    for side, part in zip((near, far), in_arrival_order(post_normed, near.shape[2])):
        w_proj = side[...].reshape(-1, emb)
        embedding += jnp.dot(part.astype(BF), w_proj, preferred_element_type=F32)
    length = jnp.sqrt(jnp.sum(embedding * embedding, axis=1, keepdims=True) + 1e-06)
    norm[...] = jnp.broadcast_to(length, norm.shape)
    vec = embedding / length
    unit[...] = vec
    low = vec.astype(BF)
    for j in range(n):
        sent[j, :, :emb] = low
        sent[j, :, emb:] = label_text[j * rows : (j + 1) * rows, :]


def embed_back_kernel(back, label_rows, unit, norm, yhat, rstd, lines, near, far, *refs):
    sent, grad = refs
    n = back.shape[0]
    emb = unit.shape[1]
    stats = [back[j, :, emb:].astype(F32) for j in range(n)]
    top = stats[0][:, 0:1]
    for j in range(1, n):
        top = jnp.maximum(top, stats[j][:, 0:1])
    rest = jnp.zeros_like(top)
    hit = jnp.zeros_like(top)
    unit_grad = jnp.zeros(unit.shape, F32)
    for j in range(n):
        weight = jnp.exp(stats[j][:, 0:1] - top)
        rest += weight * (stats[j][:, 1:2] + stats[j][:, 2:3])
        hit += weight * (stats[j][:, 3:4] + stats[j][:, 4:5])
        unit_grad += weight * back[j, :, :emb].astype(F32)
    unit_grad = (unit_grad - rest * label_rows[...]) * (100.0 / (rest + hit))
    vec = unit[...]
    along = jnp.sum(vec * unit_grad, axis=1, keepdims=True)
    emb_grad = ((unit_grad - vec * along) / norm[:, 0:1]).astype(BF)
    post_grad = in_natural_order(
        *(
            lax.dot_general(
                emb_grad, side[...].reshape(-1, emb), NT, preferred_element_type=F32
            )
            for side in (near, far)
        ),
        near.shape[2],
    )
    out_grad = norm_back(post_grad * lines[0:1, :], yhat[...], rstd[:, 0:1])
    grad[...] = out_grad
    low = out_grad.astype(BF)
    for j in range(n):
        sent[j] = low


def change_kernel(parts, gain, own, out_grad, step, sent):
    n, half, _ = sent.shape
    share = own.shape[1] // n
    total = parts[0].astype(F32)
    for j in range(1, parts.shape[0]):
        total += parts[j].astype(F32)
    xhat, scale = row_norm(own[...])
    grad = out_grad[...] + norm_back(total * gain[...], xhat, scale)
    rms = jnp.sqrt(jnp.mean(grad * grad, axis=1, keepdims=True) + 1e-06)
    change = step[0:1, 0:1] * grad / rms
    for j in range(n):
        block = change[:, j * share : (j + 1) * share]
        sent[j, :, :share] = block[:half]
        sent[j, :, share:] = block[half:]


def result_kernel(parts, resid, out):
    n, _, width = parts.shape
    share = width // 2
    blocks = []
    for c in range(2):
        for g in range(n // 2):
            block = parts[2 * g + c]
            blocks += [block[:, :share], block[:, share:]]
    change = jnp.concatenate(blocks, axis=0)
    out[...] = resid[...].astype(F32) + change.T


def local(
    resid,
    prenorm_gain,
    prenorm_bias,
    up_weight,
    up_bias,
    down_weight,
    down_bias,
    post_gain,
    post_bias,
    projection,
    texts,
    labels,
    step_size,
):
    n_txt, n_dp = lax.axis_size("txt"), lax.axis_size("dp")
    n_z, n_pair = n_dp // 2, n_txt // 2
    images, share = resid.shape
    half = images // 2
    rows = images // n_txt
    hid = up_weight.shape[1]
    n_text, emb = texts.shape
    cores = [[2 * i + c for i in range(n_pair)] for c in range(2)]
    along_y = [[b + 4 * y for y in range(4)] for b in range(4)]
    along_z = [[2 * z + x for z in range(n_z)] for x in range(2)]

    mine = jnp.stack([up_weight, down_weight.T], axis=0)
    mine = swapped(copies(mine, n_z), "dp", along_z)

    (chain,) = call(
        message_kernel,
        (((share, emb + images + 128), BF),),
        "vvvvvv",
        projection,
        resid.T,
        post_gain[None],
        post_bias[None],
        up_bias[None],
        cost=SMALL,
    )
    chain, labels = lax.optimization_barrier((chain, labels[:, None]))
    proj, rest = call(
        split_kernel,
        (((4, 2, share, emb), BF), ((2, share, images + 128), BF)),
        "vvvv",
        chain,
        from_partner(chain, "txt", 2),
        cost=SMALL,
    )
    rest = [rest] + [from_partner(rest, "txt", 4 * k) for k in (1, 2, 3)]
    (rest,) = call(stack_kernel, (((4, *rest[0].shape), BF),), "vvvvv", *rest, cost=SMALL)
    far_rest = from_partner(rest, "txt", 1)
    own, lines, normed, far_bias = call(
        rows_kernel,
        (((rows, WIDTH), F32), ((8, WIDTH), F32), ((half, WIDTH), BF), ((1, hid), F32)),
        "vvvvvvvv",
        rest,
        far_rest,
        prenorm_gain[None],
        prenorm_bias[None],
        cost=SMALL,
        scratch=(((WIDTH, half), BF), ((n_txt, 8, 128), F32)),
    )

    mine, proj, normed, far_texts = lax.optimization_barrier((mine, proj, normed, texts))
    other = from_partner(mine, "dp", 1)
    far_mine = from_partner(mine, "txt", 1)
    far_texts = from_partner(far_texts, "txt", 1)
    proj = swapped(proj, "txt", along_y)
    far_other = from_partner(other, "txt", 1)
    weights = (mine, other, far_mine, far_other)
    held = ((2, n_z, 2, WIDTH // n_dp, hid), BF)
    pre_act, mixed = call(
        mlp_kernel,
        (((2, half, hid), F32), ((half, WIDTH), BF)),
        "hhaavvvvv",
        *weights,
        normed,
        up_bias[None],
        far_bias,
        scratch=(held, held),
        sems=8,
    )
    mixed, far_texts, proj = lax.optimization_barrier((mixed, far_texts, proj))
    far_proj = from_partner(proj, "txt", 1)
    text_unit, label_text = call(
        text_kernel,
        (((2 * n_text, emb), BF), ((half, emb), BF)),
        "hhvhv",
        texts,
        far_texts,
        labels,
        cost=pl.CostEstimate(flops=2**31, bytes_accessed=12 << 20, transcendentals=0),
        scratch=(((2 * n_text, emb), BF),),
        sems=4 * n_text // 256,
    )
    mixed = swapped(mixed.reshape(n_pair, rows, WIDTH), "txt", cores)

    sent, unit_vec, emb_norm, yhat, rstd_out = call(
        embed_kernel,
        (
            ((n_pair, rows, 2 * emb), BF),
            ((rows, emb), F32),
            ((rows, 128), F32),
            ((rows, WIDTH), F32),
            ((rows, 128), F32),
        ),
        "vvvvvvvvvvvv",
        mixed,
        own,
        down_bias[None],
        lines,
        proj,
        far_proj,
        label_text,
    )
    arrived = swapped(sent, "txt", cores)

    back, label_rows = call(
        softmax_kernel,
        (((half, emb + 128), BF), ((rows, emb), F32)),
        "vhvvv",
        arrived,
        text_unit,
        labels,
        scratch=(((half, 2 * n_text), F32), ((half, emb), BF), ((2 * n_text, emb), BF)),
        sems=5,
    )
    back = swapped(back.reshape(n_pair, rows, emb + 128), "txt", cores)

    sent, out_grad = call(
        embed_back_kernel,
        (((n_pair, rows, WIDTH), BF), ((rows, WIDTH), F32)),
        "vvvvvvvvvvv",
        back,
        label_rows,
        unit_vec,
        emb_norm,
        yhat,
        rstd_out,
        lines,
        proj,
        far_proj,
    )
    out_low = swapped(sent, "txt", cores).reshape(half, WIDTH)

    (normed_grad,) = call(
        mlp_back_kernel,
        (((half, WIDTH), BF),),
        "hhaavvv",
        *weights,
        out_low,
        pre_act,
        scratch=(held, held),
        sems=8,
    )
    normed_grad = swapped(normed_grad.reshape(n_pair, rows, WIDTH), "txt", cores)
    (change,) = call(
        change_kernel,
        (((n_txt, rows // 2, 2 * share), F32),),
        "vvvvvv",
        normed_grad,
        prenorm_gain[None],
        own,
        out_grad,
        step_size[None],
    )
    change = swapped(change, "txt")
    (out,) = call(result_kernel, (((share, images), F32),), "vvv", change, resid.T)
    return out.T


def solution(mesh):
    placed = (
        P("dp", "txt"),
        P(),
        P(),
        P("dp", "txt"),
        P("txt"),
        P("txt", "dp"),
        P(),
        P("txt"),
        P("txt"),
        P("txt", None),
        P("txt", None),
        P("dp"),
        P(),
    )
    return jax.shard_map(
        local, mesh=mesh, in_specs=placed, out_specs=P("dp", "txt"), check_vma=False
    )
```

```python
import jax
import jax.numpy as jnp
from jax import lax
from jax.experimental import pallas as pl
from jax.experimental.pallas import tpu as pltpu
from jax.sharding import PartitionSpec as P

WIDTH = 1024
BF = jnp.bfloat16
F32 = jnp.float32
NT = (((1,), (1,)), ((), ()))
SMALL = pl.CostEstimate(flops=1024, bytes_accessed=1024, transcendentals=0)


def swapped(x, axis, groups=None):
    return lax.all_to_all(x, axis, 0, 0, tiled=True, axis_index_groups=groups)


def from_partner(x, axis, bits):
    pairs = [(i, i ^ bits) for i in range(lax.axis_size(axis))]
    return lax.ppermute(x, axis, pairs)


def row_norm(rows):
    mean = jnp.mean(rows, axis=1, keepdims=True)
    var = jnp.mean(rows * rows, axis=1, keepdims=True) - mean * mean
    rstd = lax.rsqrt(var + 1e-05)
    return (rows - mean) * rstd, rstd


def norm_back(scaled, normed, rstd):
    first = jnp.mean(scaled, axis=1, keepdims=True)
    second = jnp.mean(scaled * normed, axis=1, keepdims=True)
    return (scaled - first - normed * second) * rstd


def call(body, outs, spaces, *args, cost=None, scratch=(), sems=0):
    kinds = {"v": pltpu.VMEM, "h": pltpu.HBM, "a": pl.ANY}
    specs = [pl.BlockSpec(memory_space=kinds[c]) for c in spaces]
    shapes = [pltpu.VMEM(*spec) for spec in scratch]
    if sems:
        shapes.append(pltpu.SemaphoreType.DMA((sems,)))
    return pl.pallas_call(
        body,
        out_shape=[
            pltpu.HBM(*out) if c == "h" else jax.ShapeDtypeStruct(*out)
            for c, out in zip(spaces[len(args) :], outs)
        ],
        in_specs=specs[: len(args)],
        out_specs=specs[len(args) :],
        scratch_shapes=shapes,
        compiler_params=pltpu.CompilerParams(vmem_limit_bytes=24 << 20),
        cost_estimate=cost,
    )(*(
        pltpu.with_memory_space_constraint(arg, pltpu.HBM) if c == "h" else arg
        for c, arg in zip(spaces, args)
    ))


def local_labels(labels, n_text):
    half = labels.shape[0] // 2
    me = lax.axis_index("txt")
    core = lax.rem(me, 2)
    label = labels[pl.ds(pl.multiple_of(core * half, half), half), :] - (me - core) * n_text
    inside = (label >= 0) & (label < 2 * n_text)
    turned = jnp.where(label < n_text, label + n_text, label - n_text)
    return jnp.where(inside, jnp.where(core == 0, label, turned), -1)


def text_kernel(near, far, labels, unit, label_text, held, sem):
    n_text = near.shape[0]
    half = label_text.shape[0]
    step = 256
    count = n_text // step
    loads = []
    for k in range(2 * count):
        side = near if k < count else far
        loads.append(
            pltpu.make_async_copy(
                side.at[pl.ds((k % count) * step, step)], held.at[pl.ds(k * step, step)], sem.at[k]
            )
        )
        loads[k].start()
    label = local_labels(labels, n_text)
    total = jnp.zeros(label_text.shape, F32)
    stores = []
    for k in range(2 * count):
        loads[k].wait()
        block = held[k * step : (k + 1) * step, :].astype(F32)
        squares = jnp.sum(block * block, axis=1, keepdims=True)
        low = (block / jnp.sqrt(squares + 1e-06)).astype(BF)
        held[k * step : (k + 1) * step, :] = low
        place = pl.ds(k * step, step)
        stores.append(
            pltpu.make_async_copy(held.at[place], unit.at[place], sem.at[2 * count + k])
        )
        stores[k].start()
        columns = lax.broadcasted_iota(jnp.int32, (half, step), 1) + k * step
        pick = jnp.where(columns == label, 1.0, 0.0).astype(BF)
        total += jnp.dot(pick, low, preferred_element_type=F32)
    label_text[...] = total.astype(BF)
    for store in stores:
        store.wait()


def copies_kernel(up, down, out, sem):
    loads = [
        pltpu.make_async_copy(part, out.at[0, k], sem.at[k]) for k, part in enumerate((up, down))
    ]
    for load in loads:
        load.start()
    for load in loads:
        load.wait()
    for z in range(1, out.shape[0]):
        out[z] = out[0]


def message_kernel(projection, resid, gain, bias, up_bias, out, gains, biases, ups, sem):
    emb, images = projection.shape[1], resid.shape[1]
    places = (out.at[:, :emb], out.at[:, emb : emb + images], gains, biases, ups)
    loads = [
        pltpu.make_async_copy(part, place, sem.at[k])
        for k, (part, place) in enumerate(zip((projection, resid, gain, bias, up_bias), places))
    ]
    for load in loads:
        load.start()

    def parts(value):
        found = []
        for _ in range(3):
            part = value.astype(BF).astype(F32)
            found.append(part)
            value = value - part
        return found

    for load in loads:
        load.wait()
    blank = jnp.zeros((1, 128 - gain.shape[1]), F32)
    lines = [
        jnp.concatenate([part, blank], axis=1) for part in parts(gains[...]) + parts(biases[...])
    ]
    lines += [jnp.zeros((1, 128), F32)] * 2
    lines += [part[:, 128 * k : 128 * k + 128] for part in parts(ups[...]) for k in range(2)]
    lines += [jnp.zeros((1, 128), F32)] * 2
    lines = jnp.concatenate(lines, axis=0)
    out[:, emb + images :] = jnp.zeros((out.shape[0], 128), BF)
    out[: lines.shape[0], emb + images :] = lines.astype(BF)


def split_kernel(near, other, proj, rest):
    emb = proj.shape[3]
    for k, part in enumerate((near, other)):
        block = part[:, :emb]
        for y in range(proj.shape[0]):
            proj[y, k] = block
        rest[k] = part[:, emb:]


def stack_kernel(*refs):
    out = refs[-1]
    for k, part in enumerate(refs[:-1]):
        out[k] = part[...]


def rows_kernel(near, far, gain, bias, own, lines, normed, far_bias, state, vectors):
    n_txt = vectors.shape[0]
    share = near.shape[2]
    rows, half = own.shape[0], state.shape[1]
    at = lax.axis_index("txt")
    first = lax.rem(at, 2) == 0
    for core, side in enumerate((near, far)):
        for y in range(side.shape[0]):
            for x in range(side.shape[1]):
                owner = at ^ (4 * y + 2 * x + core)
                there = pl.multiple_of(owner * share, share)
                left = side[y, x, :, :half]
                right = side[y, x, :, half : 2 * half]
                state[pl.ds(there, share), :] = jnp.where(first, left, right)
                vectors[owner] = side[y, x, :8, 2 * half :].astype(F32)
    parts = far[0, 0, 8:16, 2 * half :].astype(F32)
    for k in range(2):
        far_bias[:, 128 * k : 128 * k + 128] = (
            parts[k : k + 1] + parts[k + 2 : k + 3] + parts[k + 4 : k + 5]
        )
    start = (at // 2) * rows
    column = lax.broadcasted_iota(jnp.int32, (rows, half), 1)
    line = lax.broadcasted_iota(jnp.int32, (rows, half), 0)
    pick = jnp.where(column == line + start, 1.0, 0.0).astype(BF)
    own[...] = lax.dot_general(pick, state[...], NT, preferred_element_type=F32)
    for k in range(2):
        line = [
            vectors[t, 3 * k : 3 * k + 1, :share]
            + vectors[t, 3 * k + 1 : 3 * k + 2, :share]
            + vectors[t, 3 * k + 2 : 3 * k + 3, :share]
            for t in range(n_txt)
        ]
        lines[k : k + 1, :] = jnp.concatenate(line, axis=1)
    xhat, _ = row_norm(state[...].astype(F32).T)
    normed[...] = (xhat * gain[...] + bias[...]).astype(BF)


def in_arrival_order(rows, share):
    low = lax.rem(lax.axis_index("txt"), 4)
    sides = ([], [])
    for y in range(rows.shape[1] // (4 * share)):
        pair = [rows[:, (4 * y + 2 * x) * share : (4 * y + 2 * x + 2) * share] for x in range(2)]
        for x in range(2):
            block = jnp.where(low < 2, pair[x], pair[1 - x])
            first, second = block[:, :share], block[:, share:]
            even = lax.rem(low, 2) == 0
            sides[0].append(jnp.where(even, first, second))
            sides[1].append(jnp.where(even, second, first))
    return [jnp.concatenate(side, axis=1) for side in sides]


def in_natural_order(near, far, share):
    low = lax.rem(lax.axis_index("txt"), 4)
    even = lax.rem(low, 2) == 0
    blocks = []
    for y in range(near.shape[1] // (2 * share)):
        pair = []
        for x in range(2):
            place = slice((2 * y + x) * share, (2 * y + x + 1) * share)
            first = jnp.where(even, near[:, place], far[:, place])
            second = jnp.where(even, far[:, place], near[:, place])
            pair.append(jnp.concatenate([first, second], axis=1))
        blocks += [jnp.where(low < 2, pair[x], pair[1 - x]) for x in range(2)]
    return jnp.concatenate(blocks, axis=1)


def ordered_weights(own, other, far_own, far_other, weights, sem):
    side = lax.rem(lax.axis_index("dp"), 2)
    loads = {}
    for matrix in weights:
        for k, pair in enumerate(((own, other), (far_own, far_other))):
            for x, part in enumerate(pair):
                place = weights[matrix].at[k, :, side if x == 0 else 1 - side]
                number = 4 * matrix + 2 * k + x
                load = pltpu.make_async_copy(part.at[:, matrix], place, sem.at[number])
                load.start()
                loads[matrix, k, x] = load
    return loads


def mlp_kernel(own, other, far_own, far_other, normed, bias, far_bias, *refs):
    pre_act, mixed, up, down, sem = refs
    width, hid = normed.shape[1], bias.shape[1]
    loads = ordered_weights(own, other, far_own, far_other, {0: up, 1: down}, sem)
    hidden = []
    for k, add in enumerate((bias, far_bias)):
        for x in range(2):
            loads[0, k, x].wait()
        w_up = up[k].reshape(width, hid)
        pre = jnp.dot(normed[...], w_up, preferred_element_type=F32) + add[...]
        pre_act[k] = pre
        hidden.append((pre * jax.nn.sigmoid(1.702 * pre)).astype(BF))
    total = jnp.zeros(normed.shape, F32)
    for k in range(2):
        for x in range(2):
            loads[1, k, x].wait()
        w_down = down[k].reshape(width, hid)
        total += lax.dot_general(hidden[k], w_down, NT, preferred_element_type=F32)
    mixed[...] = total.astype(BF)


def mlp_back_kernel(own, other, far_own, far_other, arrived, pre_act, *refs):
    normed_grad, up, down, sem = refs
    width, hid = arrived.shape[1], pre_act.shape[2]
    loads = ordered_weights(own, other, far_own, far_other, {1: down, 0: up}, sem)
    act_grad = []
    for k in range(2):
        for x in range(2):
            loads[1, k, x].wait()
        w_down = down[k].reshape(width, hid)
        hid_grad = jnp.dot(arrived[...], w_down, preferred_element_type=F32)
        pre = pre_act[k]
        gate = jax.nn.sigmoid(1.702 * pre)
        act_grad.append((hid_grad * (gate + 1.702 * pre * gate * (1.0 - gate))).astype(BF))
    total = jnp.zeros(normed_grad.shape, F32)
    for k in range(2):
        for x in range(2):
            loads[0, k, x].wait()
        w_up = up[k].reshape(width, hid)
        total += lax.dot_general(act_grad[k], w_up, NT, preferred_element_type=F32)
    normed_grad[...] = total.astype(BF)


def softmax_kernel(arrived, text_unit, labels, back, label_rows, logits, unit_low, held, sem):
    half, emb = unit_low.shape
    n = arrived.shape[0]
    n_block = 5
    step = text_unit.shape[0] // n_block
    loads = []
    for k in range(n_block):
        place = pl.ds(k * step, step)
        loads.append(pltpu.make_async_copy(text_unit.at[place], held.at[place], sem.at[k]))
        loads[k].start()
    texts = jnp.zeros(label_rows.shape, F32)
    for j in range(n):
        unit_low[j * half // n : (j + 1) * half // n, :] = arrived[j, :, :emb]
        texts += arrived[j, :, emb:].astype(F32)
    label_rows[...] = texts
    label = local_labels(labels, text_unit.shape[0] // 2)
    top = None
    for k in range(n_block):
        loads[k].wait()
        texts = held[k * step : (k + 1) * step, :]
        block = 100.0 * lax.dot_general(unit_low[...], texts, NT, preferred_element_type=F32)
        logits[:, k * step : (k + 1) * step] = block
        block = jnp.max(block, axis=1, keepdims=True)
        top = block if top is None else jnp.maximum(top, block)
    top = top.astype(BF).astype(F32)
    rest = jnp.zeros_like(top)
    hit = jnp.zeros_like(top)
    total = jnp.zeros((half, emb), F32)
    for k in range(n_block):
        block = jnp.exp(logits[:, k * step : (k + 1) * step] - top)
        columns = lax.broadcasted_iota(jnp.int32, (half, step), 1) + k * step
        target = columns == label
        others = jnp.where(target, 0.0, block)
        rest += jnp.sum(others, axis=1, keepdims=True)
        hit += jnp.sum(jnp.where(target, block, 0.0), axis=1, keepdims=True)
        total += jnp.dot(
            others.astype(BF), held[k * step : (k + 1) * step, :], preferred_element_type=F32
        )
    back[:, :emb] = total.astype(BF)
    lane = lax.broadcasted_iota(jnp.int32, (half, 128), 1)
    rest_high = rest.astype(BF).astype(F32)
    hit_high = hit.astype(BF).astype(F32)
    stats = jnp.zeros((half, 128), F32)
    for k, value in enumerate((top, rest_high, rest - rest_high, hit_high, hit - hit_high)):
        stats = jnp.where(lane == k, value, stats)
    back[:, emb:] = stats.astype(BF)


def embed_kernel(mixed, own, bias, lines, near, far, label_text, *refs):
    sent, unit, norm, yhat, rstd = refs
    n = mixed.shape[0]
    emb = unit.shape[1]
    rows = own.shape[0]
    total = own[...] + bias[...]
    for j in range(n):
        total += mixed[j].astype(F32)
    normed, scale = row_norm(total)
    yhat[...] = normed
    rstd[...] = jnp.broadcast_to(scale, rstd.shape)
    post_normed = normed * lines[0:1, :] + lines[1:2, :]
    embedding = jnp.zeros(unit.shape, F32)
    for side, part in zip((near, far), in_arrival_order(post_normed, near.shape[2])):
        w_proj = side[...].reshape(-1, emb)
        embedding += jnp.dot(part.astype(BF), w_proj, preferred_element_type=F32)
    length = jnp.sqrt(jnp.sum(embedding * embedding, axis=1, keepdims=True) + 1e-06)
    norm[...] = jnp.broadcast_to(length, norm.shape)
    vec = embedding / length
    unit[...] = vec
    low = vec.astype(BF)
    for j in range(n):
        sent[j, :, :emb] = low
        sent[j, :, emb:] = label_text[j * rows : (j + 1) * rows, :]


def embed_back_kernel(back, label_rows, unit, norm, yhat, rstd, lines, near, far, *refs):
    sent, grad = refs
    n = back.shape[0]
    emb = unit.shape[1]
    stats = [back[j, :, emb:].astype(F32) for j in range(n)]
    top = stats[0][:, 0:1]
    for j in range(1, n):
        top = jnp.maximum(top, stats[j][:, 0:1])
    rest = jnp.zeros_like(top)
    hit = jnp.zeros_like(top)
    unit_grad = jnp.zeros(unit.shape, F32)
    for j in range(n):
        weight = jnp.exp(stats[j][:, 0:1] - top)
        rest += weight * (stats[j][:, 1:2] + stats[j][:, 2:3])
        hit += weight * (stats[j][:, 3:4] + stats[j][:, 4:5])
        unit_grad += weight * back[j, :, :emb].astype(F32)
    unit_grad = (unit_grad - rest * label_rows[...]) * (100.0 / (rest + hit))
    vec = unit[...]
    along = jnp.sum(vec * unit_grad, axis=1, keepdims=True)
    emb_grad = ((unit_grad - vec * along) / norm[:, 0:1]).astype(BF)
    post_grad = in_natural_order(
        *(
            lax.dot_general(
                emb_grad, side[...].reshape(-1, emb), NT, preferred_element_type=F32
            )
            for side in (near, far)
        ),
        near.shape[2],
    )
    out_grad = norm_back(post_grad * lines[0:1, :], yhat[...], rstd[:, 0:1])
    grad[...] = out_grad
    low = out_grad.astype(BF)
    for j in range(n):
        sent[j] = low


def change_kernel(parts, gain, own, out_grad, step, sent):
    n, half, _ = sent.shape
    share = own.shape[1] // n
    total = parts[0].astype(F32)
    for j in range(1, parts.shape[0]):
        total += parts[j].astype(F32)
    xhat, scale = row_norm(own[...])
    grad = out_grad[...] + norm_back(total * gain[...], xhat, scale)
    rms = jnp.sqrt(jnp.mean(grad * grad, axis=1, keepdims=True) + 1e-06)
    change = step[0:1, 0:1] * grad / rms
    for j in range(n):
        block = change[:, j * share : (j + 1) * share]
        sent[j, :, :share] = block[:half]
        sent[j, :, share:] = block[half:]


def result_kernel(parts, resid, out):
    n, _, width = parts.shape
    share = width // 2
    blocks = []
    for c in range(2):
        for g in range(n // 2):
            block = parts[2 * g + c]
            blocks += [block[:, :share], block[:, share:]]
    change = jnp.concatenate(blocks, axis=0)
    out[...] = resid[...].astype(F32) + change.T


def local(
    resid,
    prenorm_gain,
    prenorm_bias,
    up_weight,
    up_bias,
    down_weight,
    down_bias,
    post_gain,
    post_bias,
    projection,
    texts,
    labels,
    step_size,
):
    n_txt, n_dp = lax.axis_size("txt"), lax.axis_size("dp")
    n_z, n_pair = n_dp // 2, n_txt // 2
    images, share = resid.shape
    half = images // 2
    rows = images // n_txt
    hid = up_weight.shape[1]
    n_text, emb = texts.shape
    cores = [[2 * i + c for i in range(n_pair)] for c in range(2)]
    along_y = [[b + 4 * y for y in range(4)] for b in range(4)]
    along_z = [[2 * z + x for z in range(n_z)] for x in range(2)]

    (mine,) = call(
        copies_kernel,
        (((n_z, 2, WIDTH // n_dp, hid), BF),),
        "hhv",
        up_weight,
        down_weight.T,
        sems=2,
    )
    mine = swapped(mine, "dp", along_z)

    (chain,) = call(
        message_kernel,
        (((share, emb + images + 128), BF),),
        "hhhhhv",
        projection,
        resid.T,
        post_gain[None],
        post_bias[None],
        up_bias[None],
        cost=SMALL,
        scratch=(((1, share), F32), ((1, share), F32), ((1, hid), F32)),
        sems=5,
    )
    chain, labels, far_texts = lax.optimization_barrier((chain, labels[:, None], texts))
    far_texts = from_partner(far_texts, "txt", 1)
    proj, rest = call(
        split_kernel,
        (((4, 2, share, emb), BF), ((2, share, images + 128), BF)),
        "vvvv",
        chain,
        from_partner(chain, "txt", 2),
        cost=SMALL,
    )
    for bits in (4, 8):
        both = (rest, from_partner(rest, "txt", bits))
        (rest,) = call(stack_kernel, (((2, *rest.shape), BF),), "vvv", *both, cost=SMALL)
    rest = rest.reshape(4, 2, share, images + 128)
    far_rest = from_partner(rest, "txt", 1)
    own, lines, normed, far_bias = call(
        rows_kernel,
        (((rows, WIDTH), F32), ((8, WIDTH), F32), ((half, WIDTH), BF), ((1, hid), F32)),
        "vvvvvvvv",
        rest,
        far_rest,
        prenorm_gain[None],
        prenorm_bias[None],
        cost=SMALL,
        scratch=(((WIDTH, half), BF), ((n_txt, 8, 128), F32)),
    )

    mine, proj, normed = lax.optimization_barrier((mine, proj, normed))
    other = from_partner(mine, "dp", 1)
    far_mine = from_partner(mine, "txt", 1)
    proj = swapped(proj, "txt", along_y)
    far_other = from_partner(other, "txt", 1)
    weights = (mine, other, far_mine, far_other)
    held = ((2, n_z, 2, WIDTH // n_dp, hid), BF)
    pre_act, mixed = call(
        mlp_kernel,
        (((2, half, hid), F32), ((half, WIDTH), BF)),
        "hhaavvvvv",
        *weights,
        normed,
        up_bias[None],
        far_bias,
        scratch=(held, held),
        sems=8,
    )
    mixed, far_texts, proj = lax.optimization_barrier((mixed, far_texts, proj))
    far_proj = from_partner(proj, "txt", 1)
    text_unit, label_text = call(
        text_kernel,
        (((2 * n_text, emb), BF), ((half, emb), BF)),
        "hhvhv",
        texts,
        far_texts,
        labels,
        cost=pl.CostEstimate(flops=2**31, bytes_accessed=12 << 20, transcendentals=0),
        scratch=(((2 * n_text, emb), BF),),
        sems=4 * n_text // 256,
    )
    mixed = swapped(mixed.reshape(n_pair, rows, WIDTH), "txt", cores)

    sent, unit_vec, emb_norm, yhat, rstd_out = call(
        embed_kernel,
        (
            ((n_pair, rows, 2 * emb), BF),
            ((rows, emb), F32),
            ((rows, 128), F32),
            ((rows, WIDTH), F32),
            ((rows, 128), F32),
        ),
        "vvvvvvvvvvvv",
        mixed,
        own,
        down_bias[None],
        lines,
        proj,
        far_proj,
        label_text,
    )
    arrived = swapped(sent, "txt", cores)

    back, label_rows = call(
        softmax_kernel,
        (((half, emb + 128), BF), ((rows, emb), F32)),
        "vhvvv",
        arrived,
        text_unit,
        labels,
        scratch=(((half, 2 * n_text), F32), ((half, emb), BF), ((2 * n_text, emb), BF)),
        sems=5,
    )
    back = swapped(back.reshape(n_pair, rows, emb + 128), "txt", cores)

    sent, out_grad = call(
        embed_back_kernel,
        (((n_pair, rows, WIDTH), BF), ((rows, WIDTH), F32)),
        "vvvvvvvvvvv",
        back,
        label_rows,
        unit_vec,
        emb_norm,
        yhat,
        rstd_out,
        lines,
        proj,
        far_proj,
    )
    out_low = swapped(sent, "txt", cores).reshape(half, WIDTH)

    (normed_grad,) = call(
        mlp_back_kernel,
        (((half, WIDTH), BF),),
        "hhaavvv",
        *weights,
        out_low,
        pre_act,
        scratch=(held, held),
        sems=8,
    )
    normed_grad = swapped(normed_grad.reshape(n_pair, rows, WIDTH), "txt", cores)
    (change,) = call(
        change_kernel,
        (((n_txt, rows // 2, 2 * share), F32),),
        "vvvvvv",
        normed_grad,
        prenorm_gain[None],
        own,
        out_grad,
        step_size[None],
    )
    change = swapped(change, "txt")
    (out,) = call(result_kernel, (((share, images), F32),), "vvv", change, resid.T)
    return out.T


def solution(mesh):
    placed = (
        P("dp", "txt"),
        P(),
        P(),
        P("dp", "txt"),
        P("txt"),
        P("txt", "dp"),
        P(),
        P("txt"),
        P("txt"),
        P("txt", None),
        P("txt", None),
        P("dp"),
        P(),
    )
    return jax.shard_map(
        local, mesh=mesh, in_specs=placed, out_specs=P("dp", "txt"), check_vma=False
    )
```

```python
import jax
import jax.numpy as jnp
from jax import lax
from jax.experimental import pallas as pl
from jax.experimental.pallas import tpu as pltpu
from jax.sharding import PartitionSpec as P

WIDTH = 1024
BF = jnp.bfloat16
F32 = jnp.float32
NT = (((1,), (1,)), ((), ()))
SMALL = pl.CostEstimate(flops=1024, bytes_accessed=1024, transcendentals=0)


def swapped(x, axis, groups=None):
    return lax.all_to_all(x, axis, 0, 0, tiled=True, axis_index_groups=groups)


def from_partner(x, axis, bits):
    pairs = [(i, i ^ bits) for i in range(lax.axis_size(axis))]
    return lax.ppermute(x, axis, pairs)


def row_norm(rows):
    mean = jnp.mean(rows, axis=1, keepdims=True)
    var = jnp.mean(rows * rows, axis=1, keepdims=True) - mean * mean
    rstd = lax.rsqrt(var + 1e-05)
    return (rows - mean) * rstd, rstd


def norm_back(scaled, normed, rstd):
    first = jnp.mean(scaled, axis=1, keepdims=True)
    second = jnp.mean(scaled * normed, axis=1, keepdims=True)
    return (scaled - first - normed * second) * rstd


def call(body, outs, spaces, *args, cost=None, scratch=(), sems=0):
    kinds = {"v": pltpu.VMEM, "h": pltpu.HBM, "a": pl.ANY}
    specs = [pl.BlockSpec(memory_space=kinds[c]) for c in spaces]
    shapes = [pltpu.VMEM(*spec) for spec in scratch]
    if sems:
        shapes.append(pltpu.SemaphoreType.DMA((sems,)))
    return pl.pallas_call(
        body,
        out_shape=[
            pltpu.HBM(*out) if c == "h" else jax.ShapeDtypeStruct(*out)
            for c, out in zip(spaces[len(args) :], outs)
        ],
        in_specs=specs[: len(args)],
        out_specs=specs[len(args) :],
        scratch_shapes=shapes,
        compiler_params=pltpu.CompilerParams(vmem_limit_bytes=24 << 20),
        cost_estimate=cost,
    )(*(
        pltpu.with_memory_space_constraint(arg, pltpu.HBM) if c == "h" else arg
        for c, arg in zip(spaces, args)
    ))


def local_labels(labels, n_text):
    half = labels.shape[0] // 2
    me = lax.axis_index("txt")
    core = lax.rem(me, 2)
    label = labels[pl.ds(pl.multiple_of(core * half, half), half), :] - (me - core) * n_text
    inside = (label >= 0) & (label < 2 * n_text)
    turned = jnp.where(label < n_text, label + n_text, label - n_text)
    return jnp.where(inside, jnp.where(core == 0, label, turned), -1)


def text_kernel(near, far, labels, unit, label_text, held, sem):
    n_text = near.shape[0]
    half = label_text.shape[0]
    step = 256
    count = n_text // step
    loads = []
    for k in range(2 * count):
        side = near if k < count else far
        loads.append(
            pltpu.make_async_copy(
                side.at[pl.ds((k % count) * step, step)], held.at[pl.ds(k * step, step)], sem.at[k]
            )
        )
        loads[k].start()
    label = local_labels(labels, n_text)
    total = jnp.zeros(label_text.shape, F32)
    stores = []
    for k in range(2 * count):
        loads[k].wait()
        block = held[k * step : (k + 1) * step, :].astype(F32)
        squares = jnp.sum(block * block, axis=1, keepdims=True)
        low = (block / jnp.sqrt(squares + 1e-06)).astype(BF)
        held[k * step : (k + 1) * step, :] = low
        place = pl.ds(k * step, step)
        stores.append(
            pltpu.make_async_copy(held.at[place], unit.at[place], sem.at[2 * count + k])
        )
        stores[k].start()
        columns = lax.broadcasted_iota(jnp.int32, (half, step), 1) + k * step
        pick = jnp.where(columns == label, 1.0, 0.0).astype(BF)
        total += jnp.dot(pick, low, preferred_element_type=F32)
    label_text[...] = total.astype(BF)
    for store in stores:
        store.wait()


def copies_kernel(up, down, out, sem):
    loads = [
        pltpu.make_async_copy(part, out.at[0, k], sem.at[k]) for k, part in enumerate((up, down))
    ]
    for load in loads:
        load.start()
    for load in loads:
        load.wait()
    for z in range(1, out.shape[0]):
        out[z] = out[0]


def message_kernel(projection, resid, gain, bias, up_bias, step, *refs):
    out, gains, biases, ups, steps, sem = refs
    emb, images = projection.shape[1], resid.shape[1]
    places = (out.at[:, :emb], out.at[:, emb : emb + images], gains, biases, ups, steps)
    loads = [
        pltpu.make_async_copy(part, place, sem.at[k])
        for k, (part, place) in enumerate(
            zip((projection, resid, gain, bias, up_bias, step), places)
        )
    ]
    for load in loads:
        load.start()

    def parts(value):
        found = []
        for _ in range(3):
            part = value.astype(BF).astype(F32)
            found.append(part)
            value = value - part
        return found

    for load in loads:
        load.wait()
    blank = jnp.zeros((1, 128 - gain.shape[1]), F32)
    lines = [
        jnp.concatenate([part, blank], axis=1) for part in parts(gains[...]) + parts(biases[...])
    ]
    lines += [jnp.zeros((1, 128), F32)] * 2
    lines += [part[:, 128 * k : 128 * k + 128] for part in parts(ups[...]) for k in range(2)]
    lines.append(jnp.concatenate(parts(steps[:, 0:1]) + [jnp.zeros((1, 125), F32)], axis=1))
    lines.append(jnp.zeros((1, 128), F32))
    lines = jnp.concatenate(lines, axis=0)
    out[:, emb + images :] = jnp.zeros((out.shape[0], 128), BF)
    out[: lines.shape[0], emb + images :] = lines.astype(BF)


def proj_copies_kernel(near, other, proj):
    emb = proj.shape[3]
    for k, part in enumerate((near, other)):
        block = part[:, :emb]
        for y in range(proj.shape[0]):
            proj[y, k] = block


def rest_kernel(near, other, rest):
    for k, part in enumerate((near, other)):
        rest[k] = part[:, part.shape[1] - rest.shape[2] :]


def stack_kernel(*refs):
    out = refs[-1]
    for k, part in enumerate(refs[:-1]):
        out[k] = part[...]


def rows_kernel(near, far, gain, bias, kept, normed, far_bias, state, vectors):
    n_txt = vectors.shape[0]
    share = near.shape[2]
    half = state.shape[1]
    rows = 2 * half // n_txt
    at = lax.axis_index("txt")
    first = lax.rem(at, 2) == 0
    for core, side in enumerate((near, far)):
        for y in range(side.shape[0]):
            for x in range(side.shape[1]):
                owner = at ^ (4 * y + 2 * x + core)
                there = pl.multiple_of(owner * share, share)
                left = side[y, x, :, :half]
                right = side[y, x, :, half : 2 * half]
                state[pl.ds(there, share), :] = jnp.where(first, left, right)
                vectors[owner] = side[y, x, :8, 2 * half :].astype(F32)
    parts = far[0, 0, 8:16, 2 * half :].astype(F32)
    for k in range(2):
        far_bias[:, 128 * k : 128 * k + 128] = (
            parts[k : k + 1] + parts[k + 2 : k + 3] + parts[k + 4 : k + 5]
        )
    start = (at // 2) * rows
    column = lax.broadcasted_iota(jnp.int32, (rows, half), 1)
    line = lax.broadcasted_iota(jnp.int32, (rows, half), 0)
    pick = jnp.where(column == line + start, 1.0, 0.0).astype(BF)
    kept[:rows, :] = lax.dot_general(pick, state[...], NT, preferred_element_type=F32)
    for k in range(2):
        line = [
            vectors[t, 3 * k : 3 * k + 1, :share]
            + vectors[t, 3 * k + 1 : 3 * k + 2, :share]
            + vectors[t, 3 * k + 2 : 3 * k + 3, :share]
            for t in range(n_txt)
        ]
        kept[rows + k : rows + k + 1, :] = jnp.concatenate(line, axis=1)
    step = near[0, 0, 8:16, 2 * half :].astype(F32)[6:7, :]
    step = jnp.sum(step, axis=1, keepdims=True)
    kept[rows + 2 :, :] = jnp.broadcast_to(step, (kept.shape[0] - rows - 2, kept.shape[1]))
    xhat, _ = row_norm(state[...].astype(F32).T)
    normed[...] = (xhat * gain[...] + bias[...]).astype(BF)


def in_arrival_order(rows, share):
    low = lax.rem(lax.axis_index("txt"), 4)
    sides = ([], [])
    for y in range(rows.shape[1] // (4 * share)):
        pair = [rows[:, (4 * y + 2 * x) * share : (4 * y + 2 * x + 2) * share] for x in range(2)]
        for x in range(2):
            block = jnp.where(low < 2, pair[x], pair[1 - x])
            first, second = block[:, :share], block[:, share:]
            even = lax.rem(low, 2) == 0
            sides[0].append(jnp.where(even, first, second))
            sides[1].append(jnp.where(even, second, first))
    return [jnp.concatenate(side, axis=1) for side in sides]


def in_natural_order(near, far, share):
    low = lax.rem(lax.axis_index("txt"), 4)
    even = lax.rem(low, 2) == 0
    blocks = []
    for y in range(near.shape[1] // (2 * share)):
        pair = []
        for x in range(2):
            place = slice((2 * y + x) * share, (2 * y + x + 1) * share)
            first = jnp.where(even, near[:, place], far[:, place])
            second = jnp.where(even, far[:, place], near[:, place])
            pair.append(jnp.concatenate([first, second], axis=1))
        blocks += [jnp.where(low < 2, pair[x], pair[1 - x]) for x in range(2)]
    return jnp.concatenate(blocks, axis=1)


def start_loads(own, other, weights, sem):
    side = lax.rem(lax.axis_index("dp"), 2)
    loads = {}
    for matrix in weights:
        for x, part in enumerate((own, other)):
            place = weights[matrix].at[:, side if x == 0 else 1 - side]
            load = pltpu.make_async_copy(part.at[:, matrix], place, sem.at[2 * matrix + x])
            load.start()
            loads[matrix, x] = load
    return loads


def placed_weights(own, other, matrix, held):
    side = lax.rem(lax.axis_index("dp"), 2)
    for z in range(own.shape[0]):
        held[z, side] = own[z, matrix]
        held[z, 1 - side] = other[z, matrix]
    return held[...].reshape(-1, own.shape[3])


def hidden_units(normed, w_up, bias, pre_act):
    pre = jnp.dot(normed[...], w_up, preferred_element_type=F32) + bias[...]
    pre_act[...] = pre
    return (pre * jax.nn.sigmoid(1.702 * pre)).astype(BF)


def act_gradient(arrived, w_down, pre_act):
    hid_grad = jnp.dot(arrived[...], w_down, preferred_element_type=F32)
    pre = pre_act[...]
    gate = jax.nn.sigmoid(1.702 * pre)
    return (hid_grad * (gate + 1.702 * pre * gate * (1.0 - gate))).astype(BF)


def mlp_near_kernel(own, other, normed, bias, pre_act, part, up, down, held_pre_act, sem):
    loads = start_loads(own, other, {0: up, 1: down}, sem)
    for x in range(2):
        loads[0, x].wait()
    hidden = hidden_units(normed, up[...].reshape(-1, bias.shape[1]), bias, held_pre_act)
    store = pltpu.make_async_copy(held_pre_act, pre_act, sem.at[4])
    store.start()
    for x in range(2):
        loads[1, x].wait()
    w_down = down[...].reshape(-1, bias.shape[1])
    part[...] = lax.dot_general(hidden, w_down, NT, preferred_element_type=F32)
    store.wait()


def mlp_far_kernel(own, other, normed, bias, part, pre_act, mixed, up, down):
    hidden = hidden_units(normed, placed_weights(own, other, 0, up), bias, pre_act)
    w_down = placed_weights(own, other, 1, down)
    total = part[...] + lax.dot_general(hidden, w_down, NT, preferred_element_type=F32)
    mixed[...] = total.astype(BF)


def mlp_back_kernel(own, other, far_own, far_other, arrived, pre_act, far_pre_act, *refs):
    normed_grad, up, down, far_up, far_down, sem = refs
    hid = pre_act.shape[1]
    loads = start_loads(own, other, {1: down, 0: up}, sem)
    act_grad = act_gradient(
        arrived, placed_weights(far_own, far_other, 1, far_down), far_pre_act
    )
    w_up = placed_weights(far_own, far_other, 0, far_up)
    total = lax.dot_general(act_grad, w_up, NT, preferred_element_type=F32)
    for x in range(2):
        loads[1, x].wait()
    act_grad = act_gradient(arrived, down[...].reshape(-1, hid), pre_act)
    for x in range(2):
        loads[0, x].wait()
    w_up = up[...].reshape(-1, hid)
    total += lax.dot_general(act_grad, w_up, NT, preferred_element_type=F32)
    normed_grad[...] = total.astype(BF)


def softmax_kernel(arrived, text_unit, labels, back, label_rows, logits, unit_low, held, sem):
    half, emb = unit_low.shape
    n = arrived.shape[0]
    n_block = 5
    step = text_unit.shape[0] // n_block
    cut = step // 4
    loads = []
    for k in range(4 * n_block):
        place = pl.ds(k * cut, cut)
        loads.append(pltpu.make_async_copy(text_unit.at[place], held.at[place], sem.at[k]))
        loads[k].start()
    texts = jnp.zeros(label_rows.shape, F32)
    for j in range(n):
        unit_low[j * half // n : (j + 1) * half // n, :] = arrived[j, :, :emb]
        texts += arrived[j, :, emb:].astype(F32)
    label_rows[...] = texts
    label = local_labels(labels, text_unit.shape[0] // 2)
    top = None
    for k in range(n_block):
        for load in loads[4 * k : 4 * k + 4]:
            load.wait()
        texts = held[k * step : (k + 1) * step, :]
        block = 100.0 * lax.dot_general(unit_low[...], texts, NT, preferred_element_type=F32)
        logits[:, k * step : (k + 1) * step] = block
        block = jnp.max(block, axis=1, keepdims=True)
        top = block if top is None else jnp.maximum(top, block)
    top = top.astype(BF).astype(F32)
    rest = jnp.zeros_like(top)
    hit = jnp.zeros_like(top)
    total = jnp.zeros((half, emb), F32)
    for k in range(n_block):
        block = jnp.exp(logits[:, k * step : (k + 1) * step] - top)
        columns = lax.broadcasted_iota(jnp.int32, (half, step), 1) + k * step
        target = columns == label
        others = jnp.where(target, 0.0, block)
        rest += jnp.sum(others, axis=1, keepdims=True)
        hit += jnp.sum(jnp.where(target, block, 0.0), axis=1, keepdims=True)
        total += jnp.dot(
            others.astype(BF), held[k * step : (k + 1) * step, :], preferred_element_type=F32
        )
    back[:, :emb] = total.astype(BF)
    lane = lax.broadcasted_iota(jnp.int32, (half, 128), 1)
    rest_high = rest.astype(BF).astype(F32)
    hit_high = hit.astype(BF).astype(F32)
    stats = jnp.zeros((half, 128), F32)
    for k, value in enumerate((top, rest_high, rest - rest_high, hit_high, hit - hit_high)):
        stats = jnp.where(lane == k, value, stats)
    back[:, emb:] = stats.astype(BF)


def embed_kernel(mixed, kept, bias, near, far, label_text, *refs):
    sent, unit, norm, yhat, rstd = refs
    n = mixed.shape[0]
    emb = unit.shape[1]
    rows = mixed.shape[1]
    total = kept[:rows, :] + bias[...]
    for j in range(n):
        total += mixed[j].astype(F32)
    normed, scale = row_norm(total)
    yhat[...] = normed
    rstd[...] = jnp.broadcast_to(scale, rstd.shape)
    post_normed = normed * kept[rows : rows + 1, :] + kept[rows + 1 : rows + 2, :]
    embedding = jnp.zeros(unit.shape, F32)
    for side, part in zip((near, far), in_arrival_order(post_normed, near.shape[2])):
        w_proj = side[...].reshape(-1, emb)
        embedding += jnp.dot(part.astype(BF), w_proj, preferred_element_type=F32)
    length = jnp.sqrt(jnp.sum(embedding * embedding, axis=1, keepdims=True) + 1e-06)
    norm[...] = jnp.broadcast_to(length, norm.shape)
    vec = embedding / length
    unit[...] = vec
    low = vec.astype(BF)
    for j in range(n):
        sent[j, :, :emb] = low
        sent[j, :, emb:] = label_text[j * rows : (j + 1) * rows, :]


def embed_back_kernel(back, label_rows, unit, norm, yhat, rstd, kept, near, far, *refs):
    sent, grad = refs
    n, rows = back.shape[:2]
    emb = unit.shape[1]
    stats = [back[j, :, emb:].astype(F32) for j in range(n)]
    top = stats[0][:, 0:1]
    for j in range(1, n):
        top = jnp.maximum(top, stats[j][:, 0:1])
    rest = jnp.zeros_like(top)
    hit = jnp.zeros_like(top)
    unit_grad = jnp.zeros(unit.shape, F32)
    for j in range(n):
        weight = jnp.exp(stats[j][:, 0:1] - top)
        rest += weight * (stats[j][:, 1:2] + stats[j][:, 2:3])
        hit += weight * (stats[j][:, 3:4] + stats[j][:, 4:5])
        unit_grad += weight * back[j, :, :emb].astype(F32)
    unit_grad = (unit_grad - rest * label_rows[...]) * (100.0 / (rest + hit))
    vec = unit[...]
    along = jnp.sum(vec * unit_grad, axis=1, keepdims=True)
    emb_grad = ((unit_grad - vec * along) / norm[:, 0:1]).astype(BF)
    post_grad = in_natural_order(
        *(
            lax.dot_general(
                emb_grad, side[...].reshape(-1, emb), NT, preferred_element_type=F32
            )
            for side in (near, far)
        ),
        near.shape[2],
    )
    out_grad = norm_back(post_grad * kept[rows : rows + 1, :], yhat[...], rstd[:, 0:1])
    grad[...] = out_grad
    low = out_grad.astype(BF)
    for j in range(n):
        sent[j] = low


def change_kernel(parts, gain, kept, out_grad, sent):
    n, half, _ = sent.shape
    rows = out_grad.shape[0]
    share = out_grad.shape[1] // n
    total = parts[0].astype(F32)
    for j in range(1, parts.shape[0]):
        total += parts[j].astype(F32)
    xhat, scale = row_norm(kept[:rows, :])
    grad = out_grad[...] + norm_back(total * gain[...], xhat, scale)
    rms = jnp.sqrt(jnp.mean(grad * grad, axis=1, keepdims=True) + 1e-06)
    change = kept[rows + 2 : rows + 3, 0:1] * grad / rms
    for j in range(n):
        block = change[:, j * share : (j + 1) * share]
        sent[j, :, :share] = block[:half]
        sent[j, :, share:] = block[half:]


def result_kernel(parts, resid, out):
    n, _, width = parts.shape
    share = width // 2
    blocks = []
    for c in range(2):
        for g in range(n // 2):
            block = parts[2 * g + c]
            blocks += [block[:, :share], block[:, share:]]
    change = jnp.concatenate(blocks, axis=0)
    out[...] = resid[...].astype(F32) + change.T


def local(
    resid,
    prenorm_gain,
    prenorm_bias,
    up_weight,
    up_bias,
    down_weight,
    down_bias,
    post_gain,
    post_bias,
    projection,
    texts,
    labels,
    step_size,
):
    n_txt, n_dp = lax.axis_size("txt"), lax.axis_size("dp")
    n_z, n_pair = n_dp // 2, n_txt // 2
    images, share = resid.shape
    half = images // 2
    rows = images // n_txt
    hid = up_weight.shape[1]
    n_text, emb = texts.shape
    cores = [[2 * i + c for i in range(n_pair)] for c in range(2)]
    along_y = [[b + 4 * y for y in range(4)] for b in range(4)]
    along_z = [[2 * z + x for z in range(n_z)] for x in range(2)]

    (mine,) = call(
        copies_kernel,
        (((n_z, 2, WIDTH // n_dp, hid), BF),),
        "hhv",
        up_weight,
        down_weight.T,
        sems=2,
    )
    mine = swapped(mine, "dp", along_z)

    (chain,) = call(
        message_kernel,
        (((share, emb + images + 128), BF),),
        "hhhhhhv",
        projection,
        resid.T,
        post_gain[None],
        post_bias[None],
        up_bias[None],
        jnp.broadcast_to(step_size, (1, 128)),
        cost=SMALL,
        scratch=(((1, share), F32), ((1, share), F32), ((1, hid), F32), ((1, 128), F32)),
        sems=6,
    )
    chain, labels, far_texts = lax.optimization_barrier((chain, labels[:, None], texts))
    far_texts = from_partner(far_texts, "txt", 1)
    both = (chain, from_partner(chain, "txt", 2))
    (rest,) = call(rest_kernel, (((2, share, images + 128), BF),), "vvv", *both, cost=SMALL)
    (proj,) = call(proj_copies_kernel, (((4, 2, share, emb), BF),), "vvv", *both, cost=SMALL)
    for bits in (4, 8):
        both = (rest, from_partner(rest, "txt", bits))
        (rest,) = call(stack_kernel, (((2, *rest.shape), BF),), "vvv", *both, cost=SMALL)
    rest = rest.reshape(4, 2, share, images + 128)
    far_rest = from_partner(rest, "txt", 1)
    kept, normed, far_bias = call(
        rows_kernel,
        (((rows + 8, WIDTH), F32), ((half, WIDTH), BF), ((1, hid), F32)),
        "vvvvvvv",
        rest,
        far_rest,
        prenorm_gain[None],
        prenorm_bias[None],
        cost=SMALL,
        scratch=(((WIDTH, half), BF), ((n_txt, 8, 128), F32)),
    )

    mine, proj, normed = lax.optimization_barrier((mine, proj, normed))
    other = from_partner(mine, "dp", 1)
    far_mine = from_partner(mine, "txt", 1)
    proj = swapped(proj, "txt", along_y)
    far_other = from_partner(other, "txt", 1)
    held = ((n_z, 2, WIDTH // n_dp, hid), BF)
    pre_act, part = call(
        mlp_near_kernel,
        (((half, hid), F32), ((half, WIDTH), F32)),
        "hhvvhv",
        mine,
        other,
        normed,
        up_bias[None],
        scratch=(held, held, ((half, hid), F32)),
        sems=5,
    )
    far_pre_act, mixed = call(
        mlp_far_kernel,
        (((half, hid), F32), ((half, WIDTH), BF)),
        "vvvvvvv",
        far_mine,
        far_other,
        normed,
        far_bias,
        part,
        scratch=(held, held),
    )
    mixed, far_texts, proj = lax.optimization_barrier((mixed, far_texts, proj))
    far_proj = from_partner(proj, "txt", 1)
    text_unit, label_text = call(
        text_kernel,
        (((2 * n_text, emb), BF), ((half, emb), BF)),
        "hhvhv",
        texts,
        far_texts,
        labels,
        cost=pl.CostEstimate(flops=2**31, bytes_accessed=12 << 20, transcendentals=0),
        scratch=(((2 * n_text, emb), BF),),
        sems=4 * n_text // 256,
    )
    mixed = swapped(mixed.reshape(n_pair, rows, WIDTH), "txt", cores)

    sent, unit_vec, emb_norm, yhat, rstd_out = call(
        embed_kernel,
        (
            ((n_pair, rows, 2 * emb), BF),
            ((rows, emb), F32),
            ((rows, 128), F32),
            ((rows, WIDTH), F32),
            ((rows, 128), F32),
        ),
        "vvvvvvvvvvv",
        mixed,
        kept,
        down_bias[None],
        proj,
        far_proj,
        label_text,
    )
    arrived = swapped(sent, "txt", cores)

    back, label_rows = call(
        softmax_kernel,
        (((half, emb + 128), BF), ((rows, emb), F32)),
        "vhvvv",
        arrived,
        text_unit,
        labels,
        scratch=(((half, 2 * n_text), F32), ((half, emb), BF), ((2 * n_text, emb), BF)),
        sems=20,
    )
    back = swapped(back.reshape(n_pair, rows, emb + 128), "txt", cores)

    sent, out_grad = call(
        embed_back_kernel,
        (((n_pair, rows, WIDTH), BF), ((rows, WIDTH), F32)),
        "vvvvvvvvvvv",
        back,
        label_rows,
        unit_vec,
        emb_norm,
        yhat,
        rstd_out,
        kept,
        proj,
        far_proj,
    )
    out_low = swapped(sent, "txt", cores).reshape(half, WIDTH)

    (normed_grad,) = call(
        mlp_back_kernel,
        (((half, WIDTH), BF),),
        "hhvvvvvv",
        mine,
        other,
        far_mine,
        far_other,
        out_low,
        pre_act,
        far_pre_act,
        scratch=(held, held, held, held),
        sems=4,
    )
    normed_grad = swapped(normed_grad.reshape(n_pair, rows, WIDTH), "txt", cores)
    (change,) = call(
        change_kernel,
        (((n_txt, rows // 2, 2 * share), F32),),
        "vvvvv",
        normed_grad,
        prenorm_gain[None],
        kept,
        out_grad,
    )
    change = swapped(change, "txt")
    (out,) = call(result_kernel, (((share, images), F32),), "vvv", change, resid.T)
    return out.T


def solution(mesh):
    placed = (
        P("dp", "txt"),
        P(),
        P(),
        P("dp", "txt"),
        P("txt"),
        P("txt", "dp"),
        P(),
        P("txt"),
        P("txt"),
        P("txt", None),
        P("txt", None),
        P("dp"),
        P(),
    )
    return jax.shard_map(
        local, mesh=mesh, in_specs=placed, out_specs=P("dp", "txt"), check_vma=False
    )
```

```python
import jax
import jax.numpy as jnp
from jax import lax
from jax.experimental import pallas as pl
from jax.experimental.pallas import tpu as pltpu
from jax.sharding import PartitionSpec as P

WIDTH = 1024
BF = jnp.bfloat16
F32 = jnp.float32
NT = (((1,), (1,)), ((), ()))
SMALL = pl.CostEstimate(flops=1024, bytes_accessed=1024, transcendentals=0)


def swapped(x, axis, groups=None):
    return lax.all_to_all(x, axis, 0, 0, tiled=True, axis_index_groups=groups)


def from_partner(x, axis, bits):
    pairs = [(i, i ^ bits) for i in range(lax.axis_size(axis))]
    return lax.ppermute(x, axis, pairs)


def row_norm(rows):
    mean = jnp.mean(rows, axis=1, keepdims=True)
    var = jnp.mean(rows * rows, axis=1, keepdims=True) - mean * mean
    rstd = lax.rsqrt(var + 1e-05)
    return (rows - mean) * rstd, rstd


def norm_back(scaled, normed, rstd):
    first = jnp.mean(scaled, axis=1, keepdims=True)
    second = jnp.mean(scaled * normed, axis=1, keepdims=True)
    return (scaled - first - normed * second) * rstd


def call(body, outs, spaces, *args, cost=None, scratch=(), sems=0):
    kinds = {"v": pltpu.VMEM, "h": pltpu.HBM, "a": pl.ANY}
    specs = [pl.BlockSpec(memory_space=kinds[c]) for c in spaces]
    shapes = [pltpu.VMEM(*spec) for spec in scratch]
    if sems:
        shapes.append(pltpu.SemaphoreType.DMA((sems,)))
    return pl.pallas_call(
        body,
        out_shape=[
            pltpu.HBM(*out) if c == "h" else jax.ShapeDtypeStruct(*out)
            for c, out in zip(spaces[len(args) :], outs)
        ],
        in_specs=specs[: len(args)],
        out_specs=specs[len(args) :],
        scratch_shapes=shapes,
        compiler_params=pltpu.CompilerParams(vmem_limit_bytes=24 << 20),
        cost_estimate=cost,
    )(*(
        pltpu.with_memory_space_constraint(arg, pltpu.HBM) if c == "h" else arg
        for c, arg in zip(spaces, args)
    ))


def local_labels(labels, n_text):
    half = labels.shape[0] // 2
    me = lax.axis_index("txt")
    core = lax.rem(me, 2)
    label = labels[pl.ds(pl.multiple_of(core * half, half), half), :] - (me - core) * n_text
    inside = (label >= 0) & (label < 2 * n_text)
    turned = jnp.where(label < n_text, label + n_text, label - n_text)
    return jnp.where(inside, jnp.where(core == 0, label, turned), -1)


def text_kernel(near, far, labels, unit, label_text, held, sem):
    n_text = near.shape[0]
    half = label_text.shape[0]
    step = 256
    count = n_text // step
    loads = []
    for k in range(2 * count):
        side = near if k < count else far
        loads.append(
            pltpu.make_async_copy(
                side.at[pl.ds((k % count) * step, step)], held.at[pl.ds(k * step, step)], sem.at[k]
            )
        )
        loads[k].start()
    label = local_labels(labels, n_text)
    total = jnp.zeros(label_text.shape, F32)
    stores = []
    for k in range(2 * count):
        loads[k].wait()
        block = held[k * step : (k + 1) * step, :].astype(F32)
        squares = jnp.sum(block * block, axis=1, keepdims=True)
        low = (block / jnp.sqrt(squares + 1e-06)).astype(BF)
        held[k * step : (k + 1) * step, :] = low
        place = pl.ds(k * step, step)
        stores.append(
            pltpu.make_async_copy(held.at[place], unit.at[place], sem.at[2 * count + k])
        )
        stores[k].start()
        columns = lax.broadcasted_iota(jnp.int32, (half, step), 1) + k * step
        pick = jnp.where(columns == label, 1.0, 0.0).astype(BF)
        total += jnp.dot(pick, low, preferred_element_type=F32)
    label_text[...] = total.astype(BF)
    for store in stores:
        store.wait()


def copies_kernel(up, down, out, sem):
    loads = [
        pltpu.make_async_copy(part, out.at[z, k], sem.at[2 * z + k])
        for z in range(out.shape[0])
        for k, part in enumerate((up, down))
    ]
    for load in loads:
        load.start()
    for load in loads:
        load.wait()


def message_kernel(projection, resid, gain, bias, up_bias, *refs):
    out, gains, biases, ups, sem = refs
    emb, images = projection.shape[1], resid.shape[1]
    places = (out.at[:, :emb], out.at[:, emb : emb + images], gains, biases, ups)
    loads = [
        pltpu.make_async_copy(part, place, sem.at[k])
        for k, (part, place) in enumerate(
            zip((projection, resid, gain, bias, up_bias), places)
        )
    ]
    for load in loads:
        load.start()

    def parts(value):
        found = []
        for _ in range(3):
            part = value.astype(BF).astype(F32)
            found.append(part)
            value = value - part
        return found

    for load in loads:
        load.wait()
    blank = jnp.zeros((1, 128 - gain.shape[1]), F32)
    lines = [
        jnp.concatenate([part, blank], axis=1) for part in parts(gains[...]) + parts(biases[...])
    ]
    lines += [jnp.zeros((1, 128), F32)] * 2
    lines += [part[:, 128 * k : 128 * k + 128] for part in parts(ups[...]) for k in range(2)]
    lines += [jnp.zeros((1, 128), F32)] * 2
    lines = jnp.concatenate(lines, axis=0)
    out[:, emb + images :] = jnp.zeros((out.shape[0], 128), BF)
    out[: lines.shape[0], emb + images :] = lines.astype(BF)


def proj_copies_kernel(near, other, proj):
    emb = proj.shape[3]
    for k, part in enumerate((near, other)):
        block = part[:, :emb]
        for y in range(proj.shape[0]):
            proj[y, k] = block


def rest_kernel(near, other, rest):
    for k, part in enumerate((near, other)):
        rest[k] = part[:, part.shape[1] - rest.shape[2] :]


def stack_kernel(*refs):
    out = refs[-1]
    for k, part in enumerate(refs[:-1]):
        out[k] = part[...]


def rows_kernel(near, far, gain, bias, step, kept, normed, far_bias, state, vectors):
    n_txt = vectors.shape[0]
    share = near.shape[2]
    half = state.shape[1]
    rows = 2 * half // n_txt
    at = lax.axis_index("txt")
    first = lax.rem(at, 2) == 0
    for core, side in enumerate((near, far)):
        for y in range(side.shape[0]):
            for x in range(side.shape[1]):
                owner = at ^ (4 * y + 2 * x + core)
                there = pl.multiple_of(owner * share, share)
                left = side[y, x, :, :half]
                right = side[y, x, :, half : 2 * half]
                state[pl.ds(there, share), :] = jnp.where(first, left, right)
                vectors[owner] = side[y, x, :8, 2 * half :].astype(F32)
    parts = far[0, 0, 8:16, 2 * half :].astype(F32)
    for k in range(2):
        far_bias[:, 128 * k : 128 * k + 128] = (
            parts[k : k + 1] + parts[k + 2 : k + 3] + parts[k + 4 : k + 5]
        )
    start = (at // 2) * rows
    column = lax.broadcasted_iota(jnp.int32, (rows, half), 1)
    line = lax.broadcasted_iota(jnp.int32, (rows, half), 0)
    pick = jnp.where(column == line + start, 1.0, 0.0).astype(BF)
    kept[:rows, :] = lax.dot_general(pick, state[...], NT, preferred_element_type=F32)
    for k in range(2):
        line = [
            vectors[t, 3 * k : 3 * k + 1, :share]
            + vectors[t, 3 * k + 1 : 3 * k + 2, :share]
            + vectors[t, 3 * k + 2 : 3 * k + 3, :share]
            for t in range(n_txt)
        ]
        kept[rows + k : rows + k + 1, :] = jnp.concatenate(line, axis=1)
    kept[rows + 2 :, :] = jnp.broadcast_to(
        step[0:1, 0:1], (kept.shape[0] - rows - 2, kept.shape[1])
    )
    xhat, _ = row_norm(state[...].astype(F32).T)
    normed[...] = (xhat * gain[...] + bias[...]).astype(BF)


def in_arrival_order(rows, share):
    low = lax.rem(lax.axis_index("txt"), 4)
    sides = ([], [])
    for y in range(rows.shape[1] // (4 * share)):
        pair = [rows[:, (4 * y + 2 * x) * share : (4 * y + 2 * x + 2) * share] for x in range(2)]
        for x in range(2):
            block = jnp.where(low < 2, pair[x], pair[1 - x])
            first, second = block[:, :share], block[:, share:]
            even = lax.rem(low, 2) == 0
            sides[0].append(jnp.where(even, first, second))
            sides[1].append(jnp.where(even, second, first))
    return [jnp.concatenate(side, axis=1) for side in sides]


def in_natural_order(near, far, share):
    low = lax.rem(lax.axis_index("txt"), 4)
    even = lax.rem(low, 2) == 0
    blocks = []
    for y in range(near.shape[1] // (2 * share)):
        pair = []
        for x in range(2):
            place = slice((2 * y + x) * share, (2 * y + x + 1) * share)
            first = jnp.where(even, near[:, place], far[:, place])
            second = jnp.where(even, far[:, place], near[:, place])
            pair.append(jnp.concatenate([first, second], axis=1))
        blocks += [jnp.where(low < 2, pair[x], pair[1 - x]) for x in range(2)]
    return jnp.concatenate(blocks, axis=1)


def start_loads(own, other, weights, sem):
    side = lax.rem(lax.axis_index("dp"), 2)
    loads = {}
    for matrix in weights:
        for x, part in enumerate((own, other)):
            place = weights[matrix].at[:, side if x == 0 else 1 - side]
            load = pltpu.make_async_copy(part.at[:, matrix], place, sem.at[2 * matrix + x])
            load.start()
            loads[matrix, x] = load
    return loads


def placed_weights(own, other, matrix, held):
    side = lax.rem(lax.axis_index("dp"), 2)
    for z in range(own.shape[0]):
        held[z, side] = own[z, matrix]
        held[z, 1 - side] = other[z, matrix]
    return held[...].reshape(-1, own.shape[3])


def hidden_units(normed, w_up, bias, pre_act):
    pre = jnp.dot(normed[...], w_up, preferred_element_type=F32) + bias[...]
    pre_act[...] = pre
    return (pre * jax.nn.sigmoid(1.702 * pre)).astype(BF)


def act_gradient(arrived, w_down, pre_act):
    hid_grad = jnp.dot(arrived[...], w_down, preferred_element_type=F32)
    pre = pre_act[...]
    gate = jax.nn.sigmoid(1.702 * pre)
    return (hid_grad * (gate + 1.702 * pre * gate * (1.0 - gate))).astype(BF)


def mlp_near_kernel(own, other, normed, bias, pre_act, part, up, down, held_pre_act, sem):
    loads = start_loads(own, other, {0: up, 1: down}, sem)
    for x in range(2):
        loads[0, x].wait()
    hidden = hidden_units(normed, up[...].reshape(-1, bias.shape[1]), bias, held_pre_act)
    store = pltpu.make_async_copy(held_pre_act, pre_act, sem.at[4])
    store.start()
    for x in range(2):
        loads[1, x].wait()
    w_down = down[...].reshape(-1, bias.shape[1])
    part[...] = lax.dot_general(hidden, w_down, NT, preferred_element_type=F32)
    store.wait()


def mlp_far_kernel(own, other, normed, bias, part, pre_act, mixed, up, down):
    hidden = hidden_units(normed, placed_weights(own, other, 0, up), bias, pre_act)
    w_down = placed_weights(own, other, 1, down)
    total = part[...] + lax.dot_general(hidden, w_down, NT, preferred_element_type=F32)
    mixed[...] = total.astype(BF)


def mlp_back_kernel(own, other, far_own, far_other, arrived, pre_act, far_pre_act, *refs):
    normed_grad, up, down, far_up, far_down, sem = refs
    hid = pre_act.shape[1]
    loads = start_loads(own, other, {1: down, 0: up}, sem)
    act_grad = act_gradient(
        arrived, placed_weights(far_own, far_other, 1, far_down), far_pre_act
    )
    w_up = placed_weights(far_own, far_other, 0, far_up)
    total = lax.dot_general(act_grad, w_up, NT, preferred_element_type=F32)
    for x in range(2):
        loads[1, x].wait()
    act_grad = act_gradient(arrived, down[...].reshape(-1, hid), pre_act)
    for x in range(2):
        loads[0, x].wait()
    w_up = up[...].reshape(-1, hid)
    total += lax.dot_general(act_grad, w_up, NT, preferred_element_type=F32)
    normed_grad[...] = total.astype(BF)


def softmax_kernel(arrived, text_unit, labels, back, label_rows, unit_low, held, sem):
    half, emb = unit_low.shape
    n = arrived.shape[0]
    n_block = 5
    step = text_unit.shape[0] // n_block
    cut = step // 4
    loads = []
    for k in range(4 * n_block):
        place = pl.ds(k * cut, cut)
        loads.append(pltpu.make_async_copy(text_unit.at[place], held.at[place], sem.at[k]))
        loads[k].start()
    texts = jnp.zeros(label_rows.shape, F32)
    for j in range(n):
        unit_low[j * half // n : (j + 1) * half // n, :] = arrived[j, :, :emb]
        texts += arrived[j, :, emb:].astype(F32)
    label_rows[...] = texts
    label = local_labels(labels, text_unit.shape[0] // 2)
    top = None
    for k in range(n_block):
        for load in loads[4 * k : 4 * k + 4]:
            load.wait()
        texts = held[k * step : (k + 1) * step, :]
        block = 100.0 * lax.dot_general(unit_low[...], texts, NT, preferred_element_type=F32)
        highest = jnp.max(block, axis=1, keepdims=True).astype(BF).astype(F32)
        if k:
            highest = jnp.maximum(top, highest)
            scale = jnp.exp(top - highest)
        top = highest
        block = jnp.exp(block - top)
        columns = lax.broadcasted_iota(jnp.int32, (half, step), 1) + k * step
        target = columns == label
        others = jnp.where(target, 0.0, block)
        new_rest = jnp.sum(others, axis=1, keepdims=True)
        new_hit = jnp.sum(jnp.where(target, block, 0.0), axis=1, keepdims=True)
        new_total = jnp.dot(others.astype(BF), texts, preferred_element_type=F32)
        if k:
            rest = rest * scale + new_rest
            hit = hit * scale + new_hit
            total = total * scale + new_total
        else:
            rest, hit, total = new_rest, new_hit, new_total
    back[:, :emb] = total.astype(BF)
    lane = lax.broadcasted_iota(jnp.int32, (half, 128), 1)
    rest_high = rest.astype(BF).astype(F32)
    hit_high = hit.astype(BF).astype(F32)
    stats = jnp.zeros((half, 128), F32)
    for k, value in enumerate((top, rest_high, rest - rest_high, hit_high, hit - hit_high)):
        stats = jnp.where(lane == k, value, stats)
    back[:, emb:] = stats.astype(BF)


def embed_kernel(mixed, kept, bias, near, far, label_text, *refs):
    sent, unit, norm, yhat, rstd = refs
    n = mixed.shape[0]
    emb = unit.shape[1]
    rows = mixed.shape[1]
    total = kept[:rows, :] + bias[...]
    for j in range(n):
        total += mixed[j].astype(F32)
    normed, scale = row_norm(total)
    yhat[...] = normed
    rstd[...] = jnp.broadcast_to(scale, rstd.shape)
    post_normed = normed * kept[rows : rows + 1, :] + kept[rows + 1 : rows + 2, :]
    embedding = jnp.zeros(unit.shape, F32)
    for side, part in zip((near, far), in_arrival_order(post_normed, near.shape[2])):
        w_proj = side[...].reshape(-1, emb)
        embedding += jnp.dot(part.astype(BF), w_proj, preferred_element_type=F32)
    length = jnp.sqrt(jnp.sum(embedding * embedding, axis=1, keepdims=True) + 1e-06)
    norm[...] = jnp.broadcast_to(length, norm.shape)
    vec = embedding / length
    unit[...] = vec
    low = vec.astype(BF)
    for j in range(n):
        sent[j, :, :emb] = low
        sent[j, :, emb:] = label_text[j * rows : (j + 1) * rows, :]


def embed_back_kernel(back, label_rows, unit, norm, yhat, rstd, kept, near, far, *refs):
    sent, grad = refs
    n, rows = back.shape[:2]
    emb = unit.shape[1]
    stats = [back[j, :, emb:].astype(F32) for j in range(n)]
    top = stats[0][:, 0:1]
    for j in range(1, n):
        top = jnp.maximum(top, stats[j][:, 0:1])
    rest = jnp.zeros_like(top)
    hit = jnp.zeros_like(top)
    unit_grad = jnp.zeros(unit.shape, F32)
    for j in range(n):
        weight = jnp.exp(stats[j][:, 0:1] - top)
        rest += weight * (stats[j][:, 1:2] + stats[j][:, 2:3])
        hit += weight * (stats[j][:, 3:4] + stats[j][:, 4:5])
        unit_grad += weight * back[j, :, :emb].astype(F32)
    unit_grad = (unit_grad - rest * label_rows[...]) * (100.0 / (rest + hit))
    vec = unit[...]
    along = jnp.sum(vec * unit_grad, axis=1, keepdims=True)
    emb_grad = ((unit_grad - vec * along) / norm[:, 0:1]).astype(BF)
    post_grad = in_natural_order(
        *(
            lax.dot_general(
                emb_grad, side[...].reshape(-1, emb), NT, preferred_element_type=F32
            )
            for side in (near, far)
        ),
        near.shape[2],
    )
    out_grad = norm_back(post_grad * kept[rows : rows + 1, :], yhat[...], rstd[:, 0:1])
    grad[...] = out_grad
    low = out_grad.astype(BF)
    for j in range(n):
        sent[j] = low


def change_kernel(parts, gain, kept, out_grad, sent):
    n, half, _ = sent.shape
    rows = out_grad.shape[0]
    share = out_grad.shape[1] // n
    total = parts[0].astype(F32)
    for j in range(1, parts.shape[0]):
        total += parts[j].astype(F32)
    xhat, scale = row_norm(kept[:rows, :])
    grad = out_grad[...] + norm_back(total * gain[...], xhat, scale)
    rms = jnp.sqrt(jnp.mean(grad * grad, axis=1, keepdims=True) + 1e-06)
    change = kept[rows + 2 : rows + 3, 0:1] * grad / rms
    for j in range(n):
        block = change[:, j * share : (j + 1) * share]
        sent[j, :, :share] = block[:half]
        sent[j, :, share:] = block[half:]


def result_kernel(parts, resid, out):
    n, _, width = parts.shape
    share = width // 2
    blocks = []
    for c in range(2):
        for g in range(n // 2):
            block = parts[2 * g + c]
            blocks += [block[:, :share], block[:, share:]]
    change = jnp.concatenate(blocks, axis=0)
    out[...] = resid[...].astype(F32) + change.T


def local(
    resid,
    prenorm_gain,
    prenorm_bias,
    up_weight,
    up_bias,
    down_weight,
    down_bias,
    post_gain,
    post_bias,
    projection,
    texts,
    labels,
    step_size,
):
    n_txt, n_dp = lax.axis_size("txt"), lax.axis_size("dp")
    n_z, n_pair = n_dp // 2, n_txt // 2
    images, share = resid.shape
    half = images // 2
    rows = images // n_txt
    hid = up_weight.shape[1]
    n_text, emb = texts.shape
    cores = [[2 * i + c for i in range(n_pair)] for c in range(2)]
    along_y = [[b + 4 * y for y in range(4)] for b in range(4)]
    along_z = [[2 * z + x for z in range(n_z)] for x in range(2)]

    (mine,) = call(
        copies_kernel,
        (((n_z, 2, WIDTH // n_dp, hid), BF),),
        "hhh",
        up_weight,
        down_weight.T,
        sems=2 * n_z,
    )
    mine = swapped(mine, "dp", along_z)

    (chain,) = call(
        message_kernel,
        (((share, emb + images + 128), BF),),
        "hhhhhv",
        projection,
        resid.T,
        post_gain[None],
        post_bias[None],
        up_bias[None],
        cost=SMALL,
        scratch=(((1, share), F32), ((1, share), F32), ((1, hid), F32)),
        sems=5,
    )
    chain, labels, far_texts = lax.optimization_barrier((chain, labels[:, None], texts))
    far_texts = from_partner(far_texts, "txt", 1)
    both = (chain, from_partner(chain, "txt", 2))
    (rest,) = call(rest_kernel, (((2, share, images + 128), BF),), "vvv", *both, cost=SMALL)
    (proj,) = call(proj_copies_kernel, (((4, 2, share, emb), BF),), "vvv", *both, cost=SMALL)
    for bits in (4, 8):
        both = (rest, from_partner(rest, "txt", bits))
        (rest,) = call(stack_kernel, (((2, *rest.shape), BF),), "vvv", *both, cost=SMALL)
    rest = rest.reshape(4, 2, share, images + 128)
    far_rest = from_partner(rest, "txt", 1)
    kept, normed, far_bias = call(
        rows_kernel,
        (((rows + 8, WIDTH), F32), ((half, WIDTH), BF), ((1, hid), F32)),
        "vvvvvvvv",
        rest,
        far_rest,
        prenorm_gain[None],
        prenorm_bias[None],
        jnp.broadcast_to(step_size, (1, 128)),
        cost=SMALL,
        scratch=(((WIDTH, half), BF), ((n_txt, 8, 128), F32)),
    )

    mine, proj, normed = lax.optimization_barrier((mine, proj, normed))
    other = from_partner(mine, "dp", 1)
    far_mine = from_partner(mine, "txt", 1)
    proj = swapped(proj, "txt", along_y)
    far_other = from_partner(other, "txt", 1)
    held = ((n_z, 2, WIDTH // n_dp, hid), BF)
    pre_act, part = call(
        mlp_near_kernel,
        (((half, hid), F32), ((half, WIDTH), F32)),
        "hhvvhv",
        mine,
        other,
        normed,
        up_bias[None],
        scratch=(held, held, ((half, hid), F32)),
        sems=5,
    )
    far_pre_act, mixed = call(
        mlp_far_kernel,
        (((half, hid), F32), ((half, WIDTH), BF)),
        "vvvvvvv",
        far_mine,
        far_other,
        normed,
        far_bias,
        part,
        scratch=(held, held),
    )
    mixed, far_texts, proj = lax.optimization_barrier((mixed, far_texts, proj))
    far_proj = from_partner(proj, "txt", 1)
    text_unit, label_text = call(
        text_kernel,
        (((2 * n_text, emb), BF), ((half, emb), BF)),
        "hhvhv",
        texts,
        far_texts,
        labels,
        cost=pl.CostEstimate(flops=2**31, bytes_accessed=12 << 20, transcendentals=0),
        scratch=(((2 * n_text, emb), BF),),
        sems=4 * n_text // 256,
    )
    mixed = swapped(mixed.reshape(n_pair, rows, WIDTH), "txt", cores)

    sent, unit_vec, emb_norm, yhat, rstd_out = call(
        embed_kernel,
        (
            ((n_pair, rows, 2 * emb), BF),
            ((rows, emb), F32),
            ((rows, 128), F32),
            ((rows, WIDTH), F32),
            ((rows, 128), F32),
        ),
        "vvvvvvvvvvv",
        mixed,
        kept,
        down_bias[None],
        proj,
        far_proj,
        label_text,
    )
    arrived = swapped(sent, "txt", cores)

    back, label_rows = call(
        softmax_kernel,
        (((half, emb + 128), BF), ((rows, emb), F32)),
        "vhvvv",
        arrived,
        text_unit,
        labels,
        scratch=(((half, emb), BF), ((2 * n_text, emb), BF)),
        sems=20,
    )
    back = swapped(back.reshape(n_pair, rows, emb + 128), "txt", cores)

    sent, out_grad = call(
        embed_back_kernel,
        (((n_pair, rows, WIDTH), BF), ((rows, WIDTH), F32)),
        "vvvvvvvvvvv",
        back,
        label_rows,
        unit_vec,
        emb_norm,
        yhat,
        rstd_out,
        kept,
        proj,
        far_proj,
    )
    out_low = swapped(sent, "txt", cores).reshape(half, WIDTH)

    (normed_grad,) = call(
        mlp_back_kernel,
        (((half, WIDTH), BF),),
        "hhvvvvvv",
        mine,
        other,
        far_mine,
        far_other,
        out_low,
        pre_act,
        far_pre_act,
        scratch=(held, held, held, held),
        sems=4,
    )
    normed_grad = swapped(normed_grad.reshape(n_pair, rows, WIDTH), "txt", cores)
    (change,) = call(
        change_kernel,
        (((n_txt, rows // 2, 2 * share), F32),),
        "vvvvv",
        normed_grad,
        prenorm_gain[None],
        kept,
        out_grad,
    )
    change = swapped(change, "txt")
    (out,) = call(result_kernel, (((share, images), F32),), "vvv", change, resid.T)
    return out.T


def solution(mesh):
    placed = (
        P("dp", "txt"),
        P(),
        P(),
        P("dp", "txt"),
        P("txt"),
        P("txt", "dp"),
        P(),
        P("txt"),
        P("txt"),
        P("txt", None),
        P("txt", None),
        P("dp"),
        P(),
    )
    return jax.shard_map(
        local, mesh=mesh, in_specs=placed, out_specs=P("dp", "txt"), check_vma=False
    )
```

```python
import jax
import jax.numpy as jnp
from jax import lax
from jax.experimental import pallas as pl
from jax.experimental.pallas import tpu as pltpu
from jax.sharding import PartitionSpec as P

WIDTH = 1024
BF = jnp.bfloat16
F32 = jnp.float32
NT = (((1,), (1,)), ((), ()))
SMALL = pl.CostEstimate(flops=1024, bytes_accessed=1024, transcendentals=0)


def swapped(x, axis, groups=None):
    return lax.all_to_all(x, axis, 0, 0, tiled=True, axis_index_groups=groups)


def from_partner(x, axis, bits):
    pairs = [(i, i ^ bits) for i in range(lax.axis_size(axis))]
    return lax.ppermute(x, axis, pairs)


def row_norm(rows):
    mean = jnp.mean(rows, axis=1, keepdims=True)
    var = jnp.mean(rows * rows, axis=1, keepdims=True) - mean * mean
    rstd = lax.rsqrt(var + 1e-05)
    return (rows - mean) * rstd, rstd


def norm_back(scaled, normed, rstd):
    first = jnp.mean(scaled, axis=1, keepdims=True)
    second = jnp.mean(scaled * normed, axis=1, keepdims=True)
    return (scaled - first - normed * second) * rstd


def call(body, outs, spaces, *args, cost=None, scratch=(), sems=0):
    kinds = {"v": pltpu.VMEM, "h": pltpu.HBM, "a": pl.ANY}
    specs = [pl.BlockSpec(memory_space=kinds[c]) for c in spaces]
    shapes = [pltpu.VMEM(*spec) for spec in scratch]
    if sems:
        shapes.append(pltpu.SemaphoreType.DMA((sems,)))
    return pl.pallas_call(
        body,
        out_shape=[
            pltpu.HBM(*out) if c == "h" else jax.ShapeDtypeStruct(*out)
            for c, out in zip(spaces[len(args) :], outs)
        ],
        in_specs=specs[: len(args)],
        out_specs=specs[len(args) :],
        scratch_shapes=shapes,
        compiler_params=pltpu.CompilerParams(vmem_limit_bytes=24 << 20),
        cost_estimate=cost,
    )(*(
        pltpu.with_memory_space_constraint(arg, pltpu.HBM) if c == "h" else arg
        for c, arg in zip(spaces, args)
    ))


def local_labels(labels, n_text):
    half = labels.shape[0] // 2
    me = lax.axis_index("txt")
    core = lax.rem(me, 2)
    label = labels[pl.ds(pl.multiple_of(core * half, half), half), :] - (me - core) * n_text
    inside = (label >= 0) & (label < 2 * n_text)
    turned = jnp.where(label < n_text, label + n_text, label - n_text)
    return jnp.where(inside, jnp.where(core == 0, label, turned), -1)


def text_kernel(near, far, labels, unit, label_text, held, sem):
    n_text = near.shape[0]
    half = label_text.shape[0]
    step = 256
    count = n_text // step
    loads = []
    for k in range(2 * count):
        side = near if k < count else far
        loads.append(
            pltpu.make_async_copy(
                side.at[pl.ds((k % count) * step, step)], held.at[pl.ds(k * step, step)], sem.at[k]
            )
        )
        loads[k].start()
    label = local_labels(labels, n_text)
    total = jnp.zeros(label_text.shape, F32)
    stores = []
    for k in range(2 * count):
        loads[k].wait()
        block = held[k * step : (k + 1) * step, :].astype(F32)
        squares = jnp.sum(block * block, axis=1, keepdims=True)
        low = (block / jnp.sqrt(squares + 1e-06)).astype(BF)
        held[k * step : (k + 1) * step, :] = low
        place = pl.ds(k * step, step)
        stores.append(
            pltpu.make_async_copy(held.at[place], unit.at[place], sem.at[2 * count + k])
        )
        stores[k].start()
        columns = lax.broadcasted_iota(jnp.int32, (half, step), 1) + k * step
        pick = jnp.where(columns == label, 1.0, 0.0).astype(BF)
        total += jnp.dot(pick, low, preferred_element_type=F32)
    label_text[...] = total.astype(BF)
    for store in stores:
        store.wait()


def copies_kernel(up, down, out, sem):
    loads = [
        pltpu.make_async_copy(part, out.at[0, k], sem.at[k]) for k, part in enumerate((up, down))
    ]
    for load in loads:
        load.start()
    for load in loads:
        load.wait()
    for z in range(1, out.shape[0]):
        out[z] = out[0]


def message_kernel(projection, resid, gain, bias, up_bias, *refs):
    out, gains, biases, ups, sem = refs
    emb, images = projection.shape[1], resid.shape[1]
    places = (out.at[:, :emb], out.at[:, emb : emb + images], gains, biases, ups)
    loads = [
        pltpu.make_async_copy(part, place, sem.at[k])
        for k, (part, place) in enumerate(
            zip((projection, resid, gain, bias, up_bias), places)
        )
    ]
    for load in loads:
        load.start()

    def parts(value):
        found = []
        for _ in range(3):
            part = value.astype(BF).astype(F32)
            found.append(part)
            value = value - part
        return found

    for load in loads:
        load.wait()
    blank = jnp.zeros((1, 128 - gain.shape[1]), F32)
    lines = [
        jnp.concatenate([part, blank], axis=1) for part in parts(gains[...]) + parts(biases[...])
    ]
    lines += [jnp.zeros((1, 128), F32)] * 2
    lines += [part[:, 128 * k : 128 * k + 128] for part in parts(ups[...]) for k in range(2)]
    lines += [jnp.zeros((1, 128), F32)] * 2
    lines = jnp.concatenate(lines, axis=0)
    out[:, emb + images :] = jnp.zeros((out.shape[0], 128), BF)
    out[: lines.shape[0], emb + images :] = lines.astype(BF)


def proj_copies_kernel(near, other, proj):
    emb = proj.shape[3]
    for k, part in enumerate((near, other)):
        block = part[:, :emb]
        for y in range(proj.shape[0]):
            proj[y, k] = block


def rest_kernel(near, other, rest):
    for k, part in enumerate((near, other)):
        rest[k] = part[:, part.shape[1] - rest.shape[2] :]


def stack_kernel(*refs):
    out = refs[-1]
    for k, part in enumerate(refs[:-1]):
        out[k] = part[...]


def rows_kernel(near, far, gain, bias, step, kept, normed, far_bias, state, vectors):
    n_txt = vectors.shape[0]
    share = near.shape[2]
    half = state.shape[1]
    rows = 2 * half // n_txt
    at = lax.axis_index("txt")
    first = lax.rem(at, 2) == 0
    for core, side in enumerate((near, far)):
        for y in range(side.shape[0]):
            for x in range(side.shape[1]):
                owner = at ^ (4 * y + 2 * x + core)
                there = pl.multiple_of(owner * share, share)
                left = side[y, x, :, :half]
                right = side[y, x, :, half : 2 * half]
                state[pl.ds(there, share), :] = jnp.where(first, left, right)
                vectors[owner] = side[y, x, :8, 2 * half :].astype(F32)
    parts = far[0, 0, 8:16, 2 * half :].astype(F32)
    for k in range(2):
        far_bias[:, 128 * k : 128 * k + 128] = (
            parts[k : k + 1] + parts[k + 2 : k + 3] + parts[k + 4 : k + 5]
        )
    start = (at // 2) * rows
    column = lax.broadcasted_iota(jnp.int32, (rows, half), 1)
    line = lax.broadcasted_iota(jnp.int32, (rows, half), 0)
    pick = jnp.where(column == line + start, 1.0, 0.0).astype(BF)
    kept[:rows, :] = lax.dot_general(pick, state[...], NT, preferred_element_type=F32)
    for k in range(2):
        line = [
            vectors[t, 3 * k : 3 * k + 1, :share]
            + vectors[t, 3 * k + 1 : 3 * k + 2, :share]
            + vectors[t, 3 * k + 2 : 3 * k + 3, :share]
            for t in range(n_txt)
        ]
        kept[rows + k : rows + k + 1, :] = jnp.concatenate(line, axis=1)
    kept[rows + 2 :, :] = jnp.broadcast_to(
        step[0:1, 0:1], (kept.shape[0] - rows - 2, kept.shape[1])
    )
    xhat, _ = row_norm(state[...].astype(F32).T)
    normed[...] = (xhat * gain[...] + bias[...]).astype(BF)


def in_arrival_order(rows, share):
    low = lax.rem(lax.axis_index("txt"), 4)
    sides = ([], [])
    for y in range(rows.shape[1] // (4 * share)):
        pair = [rows[:, (4 * y + 2 * x) * share : (4 * y + 2 * x + 2) * share] for x in range(2)]
        for x in range(2):
            block = jnp.where(low < 2, pair[x], pair[1 - x])
            first, second = block[:, :share], block[:, share:]
            even = lax.rem(low, 2) == 0
            sides[0].append(jnp.where(even, first, second))
            sides[1].append(jnp.where(even, second, first))
    return [jnp.concatenate(side, axis=1) for side in sides]


def in_natural_order(near, far, share):
    low = lax.rem(lax.axis_index("txt"), 4)
    even = lax.rem(low, 2) == 0
    blocks = []
    for y in range(near.shape[1] // (2 * share)):
        pair = []
        for x in range(2):
            place = slice((2 * y + x) * share, (2 * y + x + 1) * share)
            first = jnp.where(even, near[:, place], far[:, place])
            second = jnp.where(even, far[:, place], near[:, place])
            pair.append(jnp.concatenate([first, second], axis=1))
        blocks += [jnp.where(low < 2, pair[x], pair[1 - x]) for x in range(2)]
    return jnp.concatenate(blocks, axis=1)


def start_loads(own, other, weights, sem):
    side = lax.rem(lax.axis_index("dp"), 2)
    loads = {}
    for matrix in weights:
        for x, part in enumerate((own, other)):
            place = weights[matrix].at[:, side if x == 0 else 1 - side]
            load = pltpu.make_async_copy(part.at[:, matrix], place, sem.at[2 * matrix + x])
            load.start()
            loads[matrix, x] = load
    return loads


def placed_weights(own, other, matrix, held):
    side = lax.rem(lax.axis_index("dp"), 2)
    for z in range(own.shape[0]):
        held[z, side] = own[z, matrix]
        held[z, 1 - side] = other[z, matrix]
    return held[...].reshape(-1, own.shape[3])


def hidden_units(normed, w_up, bias, pre_act):
    pre = jnp.dot(normed[...], w_up, preferred_element_type=F32) + bias[...]
    pre_act[...] = pre
    return (pre * jax.nn.sigmoid(1.702 * pre)).astype(BF)


def act_gradient(arrived, w_down, pre_act):
    hid_grad = jnp.dot(arrived[...], w_down, preferred_element_type=F32)
    pre = pre_act[...]
    gate = jax.nn.sigmoid(1.702 * pre)
    return (hid_grad * (gate + 1.702 * pre * gate * (1.0 - gate))).astype(BF)


def mlp_near_kernel(own, other, normed, bias, pre_act, part, up, down, held_pre_act, sem):
    loads = start_loads(own, other, {0: up, 1: down}, sem)
    for x in range(2):
        loads[0, x].wait()
    hidden = hidden_units(normed, up[...].reshape(-1, bias.shape[1]), bias, held_pre_act)
    store = pltpu.make_async_copy(held_pre_act, pre_act, sem.at[4])
    store.start()
    for x in range(2):
        loads[1, x].wait()
    w_down = down[...].reshape(-1, bias.shape[1])
    part[...] = lax.dot_general(hidden, w_down, NT, preferred_element_type=F32)
    store.wait()


def mlp_far_kernel(own, other, normed, bias, part, pre_act, mixed, up, down):
    hidden = hidden_units(normed, placed_weights(own, other, 0, up), bias, pre_act)
    w_down = placed_weights(own, other, 1, down)
    total = part[...] + lax.dot_general(hidden, w_down, NT, preferred_element_type=F32)
    mixed[...] = total.astype(BF)


def mlp_back_kernel(own, other, far_own, far_other, arrived, pre_act, far_pre_act, *refs):
    normed_grad, up, down, far_up, far_down, sem = refs
    hid = pre_act.shape[1]
    loads = start_loads(own, other, {1: down, 0: up}, sem)
    act_grad = act_gradient(
        arrived, placed_weights(far_own, far_other, 1, far_down), far_pre_act
    )
    w_up = placed_weights(far_own, far_other, 0, far_up)
    total = lax.dot_general(act_grad, w_up, NT, preferred_element_type=F32)
    for x in range(2):
        loads[1, x].wait()
    act_grad = act_gradient(arrived, down[...].reshape(-1, hid), pre_act)
    for x in range(2):
        loads[0, x].wait()
    w_up = up[...].reshape(-1, hid)
    total += lax.dot_general(act_grad, w_up, NT, preferred_element_type=F32)
    normed_grad[...] = total.astype(BF)


def softmax_kernel(arrived, text_unit, labels, back, label_rows, logits, unit_low, held, sem):
    half, emb = unit_low.shape
    n = arrived.shape[0]
    n_block = 5
    step = text_unit.shape[0] // n_block
    loads = []
    for k in range(n_block):
        place = pl.ds(k * step, step)
        loads.append(pltpu.make_async_copy(text_unit.at[place], held.at[place], sem.at[k]))
        loads[k].start()
    texts = jnp.zeros(label_rows.shape, F32)
    for j in range(n):
        unit_low[j * half // n : (j + 1) * half // n, :] = arrived[j, :, :emb]
        texts += arrived[j, :, emb:].astype(F32)
    label_rows[...] = texts
    label = local_labels(labels, text_unit.shape[0] // 2)
    top = None
    for k in range(n_block):
        loads[k].wait()
        texts = held[k * step : (k + 1) * step, :]
        block = 100.0 * lax.dot_general(unit_low[...], texts, NT, preferred_element_type=F32)
        logits[:, k * step : (k + 1) * step] = block
        block = jnp.max(block, axis=1, keepdims=True)
        top = block if top is None else jnp.maximum(top, block)
    top = top.astype(BF).astype(F32)
    rest = jnp.zeros_like(top)
    hit = jnp.zeros_like(top)
    total = jnp.zeros((half, emb), F32)
    for k in range(n_block):
        block = jnp.exp(logits[:, k * step : (k + 1) * step] - top)
        columns = lax.broadcasted_iota(jnp.int32, (half, step), 1) + k * step
        target = columns == label
        others = jnp.where(target, 0.0, block)
        rest += jnp.sum(others, axis=1, keepdims=True)
        hit += jnp.sum(jnp.where(target, block, 0.0), axis=1, keepdims=True)
        total += jnp.dot(
            others.astype(BF), held[k * step : (k + 1) * step, :], preferred_element_type=F32
        )
    back[:, :emb] = total.astype(BF)
    lane = lax.broadcasted_iota(jnp.int32, (half, 128), 1)
    rest_high = rest.astype(BF).astype(F32)
    hit_high = hit.astype(BF).astype(F32)
    stats = jnp.zeros((half, 128), F32)
    for k, value in enumerate((top, rest_high, rest - rest_high, hit_high, hit - hit_high)):
        stats = jnp.where(lane == k, value, stats)
    back[:, emb:] = stats.astype(BF)


def embed_kernel(mixed, kept, bias, near, far, label_text, *refs):
    sent, unit, norm, yhat, rstd = refs
    n = mixed.shape[0]
    emb = unit.shape[1]
    rows = mixed.shape[1]
    total = kept[:rows, :] + bias[...]
    for j in range(n):
        total += mixed[j].astype(F32)
    normed, scale = row_norm(total)
    yhat[...] = normed
    rstd[...] = jnp.broadcast_to(scale, rstd.shape)
    post_normed = normed * kept[rows : rows + 1, :] + kept[rows + 1 : rows + 2, :]
    embedding = jnp.zeros(unit.shape, F32)
    for side, part in zip((near, far), in_arrival_order(post_normed, near.shape[2])):
        w_proj = side[...].reshape(-1, emb)
        embedding += jnp.dot(part.astype(BF), w_proj, preferred_element_type=F32)
    length = jnp.sqrt(jnp.sum(embedding * embedding, axis=1, keepdims=True) + 1e-06)
    norm[...] = jnp.broadcast_to(length, norm.shape)
    vec = embedding / length
    unit[...] = vec
    low = vec.astype(BF)
    for j in range(n):
        sent[j, :, :emb] = low
        sent[j, :, emb:] = label_text[j * rows : (j + 1) * rows, :]


def embed_back_kernel(back, label_rows, unit, norm, yhat, rstd, kept, near, far, *refs):
    sent, grad = refs
    n, rows = back.shape[:2]
    emb = unit.shape[1]
    stats = [back[j, :, emb:].astype(F32) for j in range(n)]
    top = stats[0][:, 0:1]
    for j in range(1, n):
        top = jnp.maximum(top, stats[j][:, 0:1])
    rest = jnp.zeros_like(top)
    hit = jnp.zeros_like(top)
    unit_grad = jnp.zeros(unit.shape, F32)
    for j in range(n):
        weight = jnp.exp(stats[j][:, 0:1] - top)
        rest += weight * (stats[j][:, 1:2] + stats[j][:, 2:3])
        hit += weight * (stats[j][:, 3:4] + stats[j][:, 4:5])
        unit_grad += weight * back[j, :, :emb].astype(F32)
    unit_grad = (unit_grad - rest * label_rows[...]) * (100.0 / (rest + hit))
    vec = unit[...]
    along = jnp.sum(vec * unit_grad, axis=1, keepdims=True)
    emb_grad = ((unit_grad - vec * along) / norm[:, 0:1]).astype(BF)
    post_grad = in_natural_order(
        *(
            lax.dot_general(
                emb_grad, side[...].reshape(-1, emb), NT, preferred_element_type=F32
            )
            for side in (near, far)
        ),
        near.shape[2],
    )
    out_grad = norm_back(post_grad * kept[rows : rows + 1, :], yhat[...], rstd[:, 0:1])
    grad[...] = out_grad
    low = out_grad.astype(BF)
    for j in range(n):
        sent[j] = low


def change_kernel(parts, gain, kept, out_grad, sent):
    n, half, _ = sent.shape
    rows = out_grad.shape[0]
    share = out_grad.shape[1] // n
    total = parts[0].astype(F32)
    for j in range(1, parts.shape[0]):
        total += parts[j].astype(F32)
    xhat, scale = row_norm(kept[:rows, :])
    grad = out_grad[...] + norm_back(total * gain[...], xhat, scale)
    rms = jnp.sqrt(jnp.mean(grad * grad, axis=1, keepdims=True) + 1e-06)
    change = kept[rows + 2 : rows + 3, 0:1] * grad / rms
    for j in range(n):
        block = change[:, j * share : (j + 1) * share]
        sent[j, :, :share] = block[:half]
        sent[j, :, share:] = block[half:]


def result_kernel(parts, resid, out):
    n, _, width = parts.shape
    share = width // 2
    blocks = []
    for c in range(2):
        for g in range(n // 2):
            block = parts[2 * g + c]
            blocks += [block[:, :share], block[:, share:]]
    change = jnp.concatenate(blocks, axis=0)
    out[...] = resid[...].astype(F32) + change.T


def local(
    resid,
    prenorm_gain,
    prenorm_bias,
    up_weight,
    up_bias,
    down_weight,
    down_bias,
    post_gain,
    post_bias,
    projection,
    texts,
    labels,
    step_size,
):
    n_txt, n_dp = lax.axis_size("txt"), lax.axis_size("dp")
    n_z, n_pair = n_dp // 2, n_txt // 2
    images, share = resid.shape
    half = images // 2
    rows = images // n_txt
    hid = up_weight.shape[1]
    n_text, emb = texts.shape
    cores = [[2 * i + c for i in range(n_pair)] for c in range(2)]
    along_y = [[b + 4 * y for y in range(4)] for b in range(4)]
    along_z = [[2 * z + x for z in range(n_z)] for x in range(2)]

    (mine,) = call(
        copies_kernel,
        (((n_z, 2, WIDTH // n_dp, hid), BF),),
        "hhv",
        up_weight,
        down_weight.T,
        sems=2,
    )
    mine = swapped(mine, "dp", along_z)

    (chain,) = call(
        message_kernel,
        (((share, emb + images + 128), BF),),
        "hhhhhv",
        projection,
        resid.T,
        post_gain[None],
        post_bias[None],
        up_bias[None],
        cost=SMALL,
        scratch=(((1, share), F32), ((1, share), F32), ((1, hid), F32)),
        sems=5,
    )
    chain, labels, far_texts = lax.optimization_barrier((chain, labels[:, None], texts))
    far_texts = from_partner(far_texts, "txt", 1)
    both = (chain, from_partner(chain, "txt", 2))
    (rest,) = call(rest_kernel, (((2, share, images + 128), BF),), "vvv", *both, cost=SMALL)
    (proj,) = call(proj_copies_kernel, (((4, 2, share, emb), BF),), "vvv", *both, cost=SMALL)
    for bits in (4, 8):
        both = (rest, from_partner(rest, "txt", bits))
        (rest,) = call(stack_kernel, (((2, *rest.shape), BF),), "vvv", *both, cost=SMALL)
    rest = rest.reshape(4, 2, share, images + 128)
    far_rest = from_partner(rest, "txt", 1)
    kept, normed, far_bias = call(
        rows_kernel,
        (((rows + 8, WIDTH), F32), ((half, WIDTH), BF), ((1, hid), F32)),
        "vvvvvvvv",
        rest,
        far_rest,
        prenorm_gain[None],
        prenorm_bias[None],
        jnp.broadcast_to(step_size, (1, 128)),
        cost=SMALL,
        scratch=(((WIDTH, half), BF), ((n_txt, 8, 128), F32)),
    )

    mine, proj, normed = lax.optimization_barrier((mine, proj, normed))
    other = from_partner(mine, "dp", 1)
    far_mine = from_partner(mine, "txt", 1)
    proj = swapped(proj, "txt", along_y)
    far_other = from_partner(other, "txt", 1)
    held = ((n_z, 2, WIDTH // n_dp, hid), BF)
    pre_act, part = call(
        mlp_near_kernel,
        (((half, hid), F32), ((half, WIDTH), F32)),
        "hhvvhv",
        mine,
        other,
        normed,
        up_bias[None],
        scratch=(held, held, ((half, hid), F32)),
        sems=5,
    )
    far_pre_act, mixed = call(
        mlp_far_kernel,
        (((half, hid), F32), ((half, WIDTH), BF)),
        "vvvvvvv",
        far_mine,
        far_other,
        normed,
        far_bias,
        part,
        scratch=(held, held),
    )
    mixed, far_texts, proj = lax.optimization_barrier((mixed, far_texts, proj))
    far_proj = from_partner(proj, "txt", 1)
    text_unit, label_text = call(
        text_kernel,
        (((2 * n_text, emb), BF), ((half, emb), BF)),
        "hhvhv",
        texts,
        far_texts,
        labels,
        cost=pl.CostEstimate(flops=2**31, bytes_accessed=12 << 20, transcendentals=0),
        scratch=(((2 * n_text, emb), BF),),
        sems=4 * n_text // 256,
    )
    mixed = swapped(mixed.reshape(n_pair, rows, WIDTH), "txt", cores)

    sent, unit_vec, emb_norm, yhat, rstd_out = call(
        embed_kernel,
        (
            ((n_pair, rows, 2 * emb), BF),
            ((rows, emb), F32),
            ((rows, 128), F32),
            ((rows, WIDTH), F32),
            ((rows, 128), F32),
        ),
        "vvvvvvvvvvv",
        mixed,
        kept,
        down_bias[None],
        proj,
        far_proj,
        label_text,
    )
    arrived = swapped(sent, "txt", cores)

    back, label_rows = call(
        softmax_kernel,
        (((half, emb + 128), BF), ((rows, emb), F32)),
        "vhvvv",
        arrived,
        text_unit,
        labels,
        scratch=(((half, 2 * n_text), F32), ((half, emb), BF), ((2 * n_text, emb), BF)),
        sems=5,
    )
    back = swapped(back.reshape(n_pair, rows, emb + 128), "txt", cores)

    sent, out_grad = call(
        embed_back_kernel,
        (((n_pair, rows, WIDTH), BF), ((rows, WIDTH), F32)),
        "vvvvvvvvvvv",
        back,
        label_rows,
        unit_vec,
        emb_norm,
        yhat,
        rstd_out,
        kept,
        proj,
        far_proj,
    )
    out_low = swapped(sent, "txt", cores).reshape(half, WIDTH)

    (normed_grad,) = call(
        mlp_back_kernel,
        (((half, WIDTH), BF),),
        "hhvvvvvv",
        mine,
        other,
        far_mine,
        far_other,
        out_low,
        pre_act,
        far_pre_act,
        scratch=(held, held, held, held),
        sems=4,
    )
    normed_grad = swapped(normed_grad.reshape(n_pair, rows, WIDTH), "txt", cores)
    (change,) = call(
        change_kernel,
        (((n_txt, rows // 2, 2 * share), F32),),
        "vvvvv",
        normed_grad,
        prenorm_gain[None],
        kept,
        out_grad,
    )
    change = swapped(change, "txt")
    (out,) = call(result_kernel, (((share, images), F32),), "vvv", change, resid.T)
    return out.T


def solution(mesh):
    placed = (
        P("dp", "txt"),
        P(),
        P(),
        P("dp", "txt"),
        P("txt"),
        P("txt", "dp"),
        P(),
        P("txt"),
        P("txt"),
        P("txt", None),
        P("txt", None),
        P("dp"),
        P(),
    )
    return jax.shard_map(
        local, mesh=mesh, in_specs=placed, out_specs=P("dp", "txt"), check_vma=False
    )
```
